32 devices in a mesh: outer: 8 (over z, x), inner: 4 (over y, core).
Axes of the slice: x: 2, y: 2, z: 4, core: 2. Of those that a mesh axis runs over, the one named last changes fastest.
Arguments:
- resid: bfloat16 [4096, 2048], P(('outer', 'inner')), may hold values from -40 to 40
- queries: bfloat16 [4096, 256], P(('outer', 'inner')), may hold values from -80 to 80
- keyvals: bfloat16 [4096, 256], P(('outer', 'inner')), may hold values from -10 to 10
- piece_order: int32 [8], replicated, may hold values from 0 to 7, each once
- out_proj: bfloat16 [256, 2048], replicated, may hold values from -0.75 to 0.75
- mlp_gain: float32 [2048], replicated, may hold values from 0.25 to 1.75
- w_gate: bfloat16 [2048, 7168], P('inner', 'outer'), may hold values from -0.125 to 0.125
- w_up: bfloat16 [2048, 7168], P('inner', 'outer'), may hold values from -0.125 to 0.125
- w_down: bfloat16 [7168, 2048], P('outer', 'inner'), may hold values from -0.0625 to 0.0625
Outputs:
- layer_out: bfloat16 [4096, 2048], P(('outer', 'inner'))
The draws below stay inside these ranges and needn't reach their ends.
Inputs may be any that keep to these rules, and one draw needn't show every extreme that they name: `piece_order`: each of the 8 piece numbers appears once.
All inputs are finite; a program needn't handle non-finite values.
Results may differ from the reference program's by a relative error of at most 0.014.
Values may be sent and summed in bfloat16 or wider, within the bound.
A program may use at most 64 MiB of HBM per device.

```python
import jax
import jax.numpy as jnp
from jax import lax

D = 2048
FF = 7168
HD = 128
QHEADS = 2
SPAN = 64
PIECES = 8
BLOCK = 512
SEQ = 4096


def attention_inputs(key):
    base_key = jax.random.fold_in(key, 7)
    query_key, key_key, value_key = jax.random.split(base_key, 3)
    queries = jnp.clip(jax.random.normal(query_key, (SEQ, QHEADS * HD), jnp.float32), -4.0, 4.0)
    key_rows = 2.5 * jnp.clip(jax.random.normal(key_key, (SEQ, HD), jnp.float32), -4.0, 4.0)
    values = jnp.clip(jax.random.normal(value_key, (SEQ, HD), jnp.float32), -4.0, 4.0)
    return (queries, jnp.concatenate([key_rows, values], 1))


def draw_queries(key, part):
    return attention_inputs(key)[0].astype(jnp.bfloat16)


def draw_keyvals(key, part):
    return attention_inputs(key)[1].astype(jnp.bfloat16)


def draw_resid(key, part):
    base_key = jax.random.fold_in(key, 11)
    normal_key = jax.random.fold_in(base_key, 0)
    values = jnp.clip(jax.random.normal(normal_key, (SEQ, D), jnp.float32), -4.0, 4.0)
    return values.astype(jnp.bfloat16)


def block_scale(rng, extent, shards, low, top_value):
    gain, own = 1.0, jax.random.fold_in(rng, 6)
    for dim, parts in shards:
        draws = jnp.exp(jax.random.uniform(jax.random.fold_in(own, dim), (parts,), jnp.float32, low / len(shards), top_value / len(shards)))
        gain = gain * jnp.repeat(draws, extent[dim] // parts).reshape([-1 if axis == dim else 1 for axis in range(len(extent))])
    return gain


def scatter_about(rng, extent, scale, reach, cuts=(), held_as=jnp.bfloat16):
    gain = block_scale(rng, extent, cuts, -0.22, 0.18) if cuts else 1.0
    entries = jax.random.normal(rng, extent, jnp.float32) * scale * gain
    return jnp.minimum(jnp.maximum(entries, -reach), reach).astype(held_as)


def setup_inputs(seed: int = 0) -> dict:
    streams_of = jax.random.split(jax.random.key(seed), 10)
    return {
        "resid": draw_resid(jax.random.fold_in(streams_of[9], 71), 0),
        "queries": draw_queries(jax.random.fold_in(streams_of[9], 71), 0),
        "keyvals": draw_keyvals(jax.random.fold_in(streams_of[9], 71), 0),
        "piece_order": jax.random.permutation(streams_of[3], PIECES).astype(jnp.int32),
        "out_proj": scatter_about(streams_of[4], (QHEADS * HD, D), 64 ** -0.5, 0.75),
        "mlp_gain": jnp.clip(1.0 + 0.15 * jax.random.normal(streams_of[5], (D,), jnp.float32), 0.25, 1.75),
        "w_gate": scatter_about(streams_of[6], (D, FF), D ** -0.5, 0.125, ((0, 4), (1, 8))),
        "w_up": scatter_about(streams_of[7], (D, FF), D ** -0.5, 0.125, ((0, 4), (1, 8))),
        "w_down": scatter_about(streams_of[8], (FF, D), FF ** -0.5, 0.0625, ((0, 8), (1, 4))),
    }


def reference(resid, queries, keyvals, piece_order, out_proj, mlp_gain, w_gate, w_up, w_down):
    block_pos = (piece_order[:, None] * SPAN + jnp.arange(SPAN, dtype=jnp.int32)[None, :]).reshape(BLOCK)
    block_count = SEQ // BLOCK
    query_blocks = queries.reshape(block_count, BLOCK, QHEADS, HD)
    kv_blocks = keyvals.reshape(block_count, BLOCK, 2 * HD)
    before_blocks = jnp.concatenate([jnp.zeros_like(kv_blocks[:1]), kv_blocks[:-1]], 0)
    score_scale = HD ** (-0.5)

    def one_block(inputs):
        query_part, own_part, before_part, block_id = inputs
        key_rows = jnp.concatenate([own_part[:, :HD], before_part[:, :HD]], 0)
        value_rows = jnp.concatenate([own_part[:, HD:], before_part[:, HD:]], 0)
        scores = jnp.einsum('thd,kd->htk', query_part.astype(jnp.float32), key_rows.astype(jnp.float32)) * score_scale
        own_visible = block_pos[None, :] <= block_pos[:, None]
        before_visible = jnp.broadcast_to(block_id > 0, (BLOCK, BLOCK))
        visible = jnp.concatenate([own_visible, before_visible], 1)
        scores = jnp.where(visible[None], scores, -jnp.inf)
        top_score = lax.optimization_barrier(jnp.max(scores, axis=-1, keepdims=True))
        weights = jnp.where(visible[None], jnp.exp(scores - top_score), 0.0)
        totals = lax.optimization_barrier(jnp.sum(weights, axis=-1, keepdims=True))
        probs = weights.astype(jnp.bfloat16)
        mixed = jnp.einsum('htk,kd->htd', probs.astype(jnp.float32), value_rows.astype(jnp.float32)) / totals
        return mixed.transpose(1, 0, 2).reshape(BLOCK, QHEADS * HD).astype(jnp.bfloat16)
    attended = lax.map(one_block, (query_blocks, kv_blocks, before_blocks, jnp.arange(block_count, dtype=jnp.int32)))
    attended = attended.reshape(SEQ, QHEADS * HD)
    after_attn = (resid.astype(jnp.float32) + jnp.dot(attended, out_proj, preferred_element_type=jnp.float32)).astype(jnp.bfloat16)

    def mlp_block(rows_in):
        after_wide = rows_in.astype(jnp.float32)
        normed = (after_wide * lax.rsqrt(lax.optimization_barrier(jnp.mean(after_wide * after_wide, axis=-1, keepdims=True)) + 1e-05) * mlp_gain).astype(jnp.bfloat16)
        gate = jnp.dot(normed, w_gate, preferred_element_type=jnp.float32)
        upward = jnp.dot(normed, w_up, preferred_element_type=jnp.float32)
        hidden = (jax.nn.silu(gate) * upward).astype(jnp.bfloat16)
        mlp_sum = jnp.dot(hidden, w_down, preferred_element_type=jnp.float32)
        return (after_wide + mlp_sum).astype(jnp.bfloat16)
    layer_out = lax.map(mlp_block, after_attn.reshape(block_count, BLOCK, D))
    return layer_out.reshape(SEQ, D)
```

```python
import functools

import jax
import jax.numpy as jnp
from jax import lax
from jax.experimental import pallas as pl
from jax.experimental.pallas import tpu as pltpu
from jax.sharding import PartitionSpec as P

MESH = pl.DeviceIdType.MESH
F32 = jnp.float32
BF16 = jnp.bfloat16
EPS = 1e-05


def layer_kernel(
    n_out, n_in, cuts, pieces_w, early,
    order_ref, resid_ref, query_ref, kv_ref, proj_ref, gain_ref, wg_ref, wu_ref, wd_ref,
    out_ref,
    kv_all, wg, wu, wd, tok, after, att_own, res_in, att_in, gates, hidden,
    x_out, x_in, own_part, z_out, z_in, h_own, h_out, h_in,
    kv_loc, kv_snd, kv_relay_snd, kv_rcv, w_loc, w_pair_snd, w_snd, w_relay_snd, w_rcv,
    r_snd, r_rcv, a_snd, a_rcv, n_snd, n_rcv, z_snd, z_rcv, g_snd, g_rcv, x_snd, x_rcv,
    rx_snd, rx_rcv, rz_snd, rz_rcv, rh_snd, rh_rcv,
):
    o = lax.axis_index("outer")
    i = lax.axis_index("inner")
    nz = n_out // 2
    z, x = o // 2, o % 2
    core = i % 2
    partner = i + 1 - 2 * core
    x_peer = (z * 2 + 1 - x, i)
    core_peer = (o, partner)
    rows = resid_ref.shape[0]
    head = kv_ref.shape[1] // 2
    heads = query_ref.shape[1] // head
    pieces = order_ref.shape[0]
    block = n_in * rows
    span = block // pieces
    depth = wg_ref.shape[0]
    units, width = wd_ref.shape
    chips = n_in // 2
    parts_n = chips * cuts
    cw = width // cuts
    keep = rows // 2
    last_z = nz - 1

    def remote(src, dst, ssem, rsem, device):
        return pltpu.make_async_remote_copy(
            src_ref=src, dst_ref=dst, send_sem=ssem, recv_sem=rsem,
            device_id=device, device_id_type=MESH,
        )

    def inside(zz):
        return jnp.logical_and(zz >= 0, zz < nz)

    def middle(zz):
        return jnp.logical_and(zz > 0, zz < last_z)

    def z_device(zz):
        return (zz * 2 + x, i)

    barrier = pltpu.get_barrier_semaphore()
    after_o, before_o = lax.rem(o + 1, n_out), lax.rem(o + n_out - 1, n_out)
    count = 0
    for d in range(1, n_in):
        pl.semaphore_signal(barrier, inc=1, device_id=(o, lax.rem(i + d, n_in)), device_id_type=MESH)
        count += 1
    for d in range(n_in // 2):
        for there in (after_o, before_o):
            pl.semaphore_signal(
                barrier, inc=1, device_id=(there, lax.rem(i + 2 * d, n_in)), device_id_type=MESH)
            count += 1
    for d in range(1, nz):
        pl.semaphore_signal(
            barrier, inc=1, device_id=(lax.rem(z + d, nz) * 2 + x, i), device_id_type=MESH)
        count += 1
    pl.semaphore_signal(barrier, inc=1, device_id=x_peer, device_id_type=MESH)
    count += 1
    pl.semaphore_wait(barrier, count)

    own_rows = pl.ds(pl.multiple_of(i * rows, rows), rows)
    kv_copy = pltpu.make_async_copy(kv_ref, kv_all.at[own_rows], kv_loc)
    kv_copy.start()

    steps = range(1, chips)

    def kv_slot(part, q):
        return kv_all.at[pl.ds(pl.multiple_of(part * block + q * rows, rows), rows)]

    def kv_send(part, d):
        return remote(kv_ref, kv_slot(part, i), kv_snd.at[part, d], kv_rcv.at[part, i],
                      (after_o if part else o, lax.rem(i + 2 * d, n_in)))

    def kv_relay(part, d):
        q = lax.rem(i + n_in - 2 * d, n_in)
        src = kv_ref if part == 0 and d == 0 else kv_slot(part, q)
        return remote(src, kv_slot(part, q), kv_relay_snd.at[part, d], kv_rcv.at[part, q], core_peer)

    def kv_arrived(part, q):
        here = kv_slot(part, q)
        remote(here, here, kv_relay_snd.at[part, 0], kv_rcv.at[part, q], core_peer).wait_recv()

    for d in steps:
        kv_send(0, d).start()

    @pl.when(o < n_out - 1)
    def _():
        for d in range(chips):
            kv_send(1, d).start()

    kv_relay(0, 0).start()

    def tok_rows(zz, xx, start=0, size=rows):
        return tok.at[pl.ds(pl.multiple_of((zz * 2 + xx) * rows + start, 16), size)]

    targets = (z_device(z + 1), z_device(z - 1), x_peer)
    sources = ((z - 1, x), (z + 1, x), (z, 1 - x))

    def first_resid(link):
        return remote(resid_ref.at[pl.ds(0, early)], res_in.at[link], r_snd.at[link], r_rcv.at[link],
                      targets[link])

    def first_attended(link):
        return remote(att_own.at[pl.ds(0, early)], att_in.at[link], a_snd.at[link], a_rcv.at[link],
                      targets[link])

    def first_normed(link, source=None):
        here = tok_rows(*(source or (z, x)), early, rows - early)
        return remote(here, here, n_snd.at[link], n_rcv.at[link], targets[link])

    def send_link(link, act):
        if link == 2:
            act()
        else:
            pl.when(inside(z + 1 - 2 * link))(act)

    for link in range(3):
        send_link(link, lambda link=link: first_resid(link).start())

    def slot(k, q, s):
        if k == 2:
            return wd.at[q, s]
        full = wg if k == 0 else wu
        size = depth // pieces_w
        return full.at[pl.ds(pl.multiple_of(q * depth + s * size, size), size)]

    srcs = (wg_ref, wu_ref, wd_ref)

    def w_src(k, s):
        if k == 2:
            return wd_ref.at[:, pl.ds(s * cw, cw)]
        size = depth // pieces_w
        return srcs[k].at[pl.ds(s * size, size)]

    def w_parts(k):
        return cuts if k == 2 else pieces_w

    def w_far(k, d, s):
        return remote(w_src(k, s), slot(k, i, s), w_snd.at[k, d, s], w_rcv.at[k, i, s],
                      (o, lax.rem(i + 2 * d, n_in)))

    def w_pair(k, s):
        return remote(w_src(k, s), slot(k, i, s), w_pair_snd.at[k, s], w_rcv.at[k, i, s], core_peer)

    def w_arrived(k, q, s):
        here = slot(k, q, s)
        remote(here, here, w_pair_snd.at[k, s], w_rcv.at[k, q, s], core_peer).wait_recv()

    def w_relay(k, d, s):
        q = lax.rem(i + n_in - 2 * d, n_in)
        here = slot(k, q, s)
        return remote(here, here, w_relay_snd.at[k, d, s], w_rcv.at[k, q, s], core_peer)

    def w_local(k, s):
        return pltpu.make_async_copy(w_src(k, s), slot(k, i, s), w_loc.at[k, s])

    for k in range(3):
        for s in range(w_parts(k)):
            for d in steps:
                w_far(k, d, s).start()
    for k in range(3):
        for s in range(w_parts(k)):
            w_pair(k, s).start()
            w_local(k, s).start()

    def relay_weight(k, s):
        for d in steps:
            w_arrived(k, lax.rem(i + n_in - 2 * d, n_in), s)
            w_relay(k, d, s).start()

    def weight_ready(k):
        for s in range(w_parts(k)):
            w_local(k, s).wait()
            for d in range(chips):
                w_arrived(k, lax.rem(partner + 2 * d, n_in), s)

    lane = lax.broadcasted_iota(jnp.int32, (rows, block), 1)
    key_pos = jnp.zeros((rows, block), jnp.int32)
    for p in range(pieces):
        key_pos = jnp.where(lane // span == p, order_ref[p] * span + lane % span, key_pos)
    row = lax.broadcasted_iota(jnp.int32, (rows, block), 0)
    query_pos = jnp.zeros((rows, block), jnp.int32)
    for p in range(rows // span):
        query_pos = jnp.where(
            row // span == p, order_ref[i * (rows // span) + p] * span + row % span, query_pos)
    own_visible = key_pos <= query_pos
    before_visible = (jnp.zeros((rows, block), jnp.int32) + o) > 0

    @pl.when(o == 0)
    def _():
        kv_all[block:, :] = jnp.zeros((block, 2 * head), BF16)

    for zz in (0, last_z):
        @pl.when(z != zz)
        def _():
            x_in[:, zz, keep:, :] = jnp.zeros((parts_n, rows - keep, 2 * cw), BF16)

    for d in steps:
        kv_arrived(0, lax.rem(i + n_in - 2 * d, n_in))
        kv_relay(0, d).start()

    @pl.when(o > 0)
    def _():
        for d in range(chips):
            kv_arrived(1, lax.rem(i + n_in - 2 * d, n_in))
            kv_relay(1, d).start()

    kv_copy.wait()
    for d in range(chips):
        kv_arrived(0, lax.rem(partner + 2 * d, n_in))

    @pl.when(o > 0)
    def _():
        for d in range(chips):
            kv_arrived(1, lax.rem(partner + 2 * d, n_in))

    if True:
        parts = []
        nt = (((1,), (1,)), ((), ()))
        for h in range(heads):
            query = query_ref[:, h * head:(h + 1) * head]
            own_score = lax.dot_general(
                query, kv_all[:block, :head], nt, preferred_element_type=F32) * head ** (-0.5)
            before_score = lax.dot_general(
                query, kv_all[block:, :head], nt, preferred_element_type=F32) * head ** (-0.5)
            own_score = jnp.where(own_visible, own_score, -1e30)
            before_score = jnp.where(before_visible, before_score, -1e30)
            top = jnp.maximum(
                jnp.max(own_score, axis=1, keepdims=True), jnp.max(before_score, axis=1, keepdims=True))
            own_w = jnp.where(own_visible, jnp.exp(own_score - top), 0.0)
            before_w = jnp.where(before_visible, jnp.exp(before_score - top), 0.0)
            total = jnp.sum(own_w, axis=1, keepdims=True) + jnp.sum(before_w, axis=1, keepdims=True)
            mixed = jnp.dot(own_w.astype(BF16), kv_all[:block, head:], preferred_element_type=F32)
            mixed += jnp.dot(before_w.astype(BF16), kv_all[block:, head:], preferred_element_type=F32)
            parts.append((mixed / total).astype(BF16))
        att_own[...] = jnp.concatenate(parts, axis=1)
        for link in range(3):
            send_link(link, lambda link=link: first_attended(link).start())

        def normed_of(resid, attended):
            after_attn = (
                resid.astype(F32) + jnp.dot(attended, proj_ref[...], preferred_element_type=F32)
            ).astype(BF16)
            wide = after_attn.astype(F32)
            normed = wide * lax.rsqrt(jnp.mean(wide * wide, axis=1, keepdims=True) + EPS) * gain_ref[...]
            return after_attn, normed.astype(BF16)

        after_attn, normed = normed_of(resid_ref[...], att_own[...])
        after[...] = after_attn
        tok_rows(z, x)[...] = normed
        for link in range(3):
            send_link(link, lambda link=link: first_normed(link).start())

    def tok_z(way, h):
        step = 1 - 2 * way
        here = tok_rows(z - step * h, x)
        return remote(here, here, z_snd.at[way, h], z_rcv.at[way, h], z_device(z + step))

    def tok_z_arrived(way, h):
        here = tok_rows(z - (1 - 2 * way) * (h + 1), x)
        remote(here, here, z_snd.at[way, h], z_rcv.at[way, h], x_peer).wait_recv()

    def tok_x(zz, xx, part):
        here = tok_rows(zz, xx, part * keep, rows - keep if part else keep)
        return remote(here, here, x_snd.at[part, zz], x_rcv.at[part, zz], x_peer)

    def send_x(zz):
        tok_x(zz, x, 0).start()

        @pl.when(middle(zz))
        def _():
            tok_x(zz, x, 1).start()

    def tok_half(way, to):
        here = tok_rows(last_z if way else 0, 1 - x, keep, rows - keep)
        return remote(here, here, g_snd.at[way], g_rcv.at[way], to)

    def from_origin(way):
        return last_z - z if way else z

    def absorb(link):
        zz, xx = sources[link]

        def act():
            if True:
                first_resid(link).wait_recv()
            if True:
                first_attended(link).wait_recv()
            tok_rows(zz, xx, 0, early)[...] = normed_of(res_in[link], att_in[link])[1]
            if True:
                first_normed(link, (zz, xx)).wait_recv()
            if link == 2:
                for way in range(2):
                    @pl.when(from_origin(way) == 0)
                    def _():
                        tok_half(way, z_device(z + 1 - 2 * way)).start()
            else:
                @pl.when(inside(z + 1 - 2 * link))
                def _():
                    tok_z(link, 1).start()

                send_x(zz)

        if link == 2:
            act()
        else:
            pl.when(inside(zz))(act)

    def pair_of(j):
        return z + ((j + 1) // 2) * (1 - 2 * (j % 2))

    def both_rows(zz):
        return pl.ds(pl.multiple_of(zz * 2 * rows, 2 * rows), 2 * rows)

    def make_gate(zz):
        here = both_rows(zz)
        gates[here, :] = jnp.dot(tok[here, :], wg[...], preferred_element_type=F32)

    def other_x_arrived(zz):
        if True:
            tok_x(zz, 1 - x, 0).wait_recv()

            @pl.when(middle(zz))
            def _():
                tok_x(zz, 1 - x, 1).wait_recv()

    def gate_step(j, carry):
        zz = pair_of(j)

        @pl.when(inside(zz))
        def _():
            @pl.when(j > 0)
            def _():
                other_x_arrived(zz)

            make_gate(zz)

        return carry

    relays = [(k, s) for k in range(2) for s in range(pieces_w)]

    def relay_to(n):
        while relays and n > 0:
            k, s = relays.pop(0)
            relay_weight(k, s)
            n -= 1

    def halves(h):
        for way in range(2):
            @pl.when(from_origin(way) == h + 1)
            def _():
                if True:
                    tok_half(way, x_peer).wait_recv()

                @pl.when(inside(z + 1 - 2 * way))
                def _():
                    tok_half(way, z_device(z + 1 - 2 * way)).start()

    if True:
        for link in range(3):
            absorb(link)
        halves(0)
        relay_to((pieces_w + 1) // 2)
    for h in range(1, nz - 1):
        if True:
            for way in range(2):
                step = 1 - 2 * way
                source = z - step * (h + 1)

                @pl.when(inside(source))
                def _():
                    if True:
                        tok_z_arrived(way, h)
                    if h < nz - 2:
                        @pl.when(inside(z + step))
                        def _():
                            tok_z(way, h + 1).start()

                    send_x(source)
        if h == 1:
            if True:
                relay_to(pieces_w - (pieces_w + 1) // 2)
                weight_ready(0)
            if True:
                lax.fori_loop(0, 3, gate_step, 0)
                relay_to(1)
        else:
            if True:
                relay_to(1)
                lax.fori_loop(2 * h - 1, 2 * h + 1, gate_step, 0)
        if True:
            halves(h)
    if True:
        relay_to(len(relays))
        weight_ready(1)

    def columns_of(chip):
        return lax.rem(i // 2 + chips - chip, chips)

    def end_way(zz):
        return jnp.where(zz == last_z, 0, 1)

    def sum_x(p, zz, part):
        there = pl.ds(part * keep, rows - keep if part else keep)
        return remote(x_out.at[p, zz, there], x_in.at[p, zz, there], rx_snd.at[part, p, zz],
                      rx_rcv.at[part, p, zz], x_peer)

    def sum_z(p, way, zz):
        step = jnp.where(inside(z + 1 - 2 * way), 1 - 2 * way, 0)
        return remote(z_out.at[p, zz], z_in.at[p, way, zz], rz_snd.at[p, zz], rz_rcv.at[p, way, zz],
                      z_device(z + step))

    def sum_half(p, way, to):
        return remote(h_out.at[p, way], h_in.at[p, way], rh_snd.at[p, way], rh_rcv.at[p, way], to)

    def next_z(way):
        return z_device(jnp.clip(z + 1 - 2 * way, 0, last_z))

    def down(chip, cs, zz):
        def half(xx):
            return hidden[pl.ds(pl.multiple_of((zz * 2 + xx) * rows, rows), rows), :]

        both = jnp.concatenate([half(1 - x), half(x)], axis=0)
        for c in cs:
            p = chip * cuts + c
            for q in range(2):
                part = jnp.dot(both, wd[2 * columns_of(chip) + q, c], preferred_element_type=F32)
                here = slice(q * cw, (q + 1) * cw)
                x_out[p, zz, :, here] = part[:rows].astype(BF16)
                own_part[p, zz, :, here] = part[rows:]
                h_own[p, jnp.where(middle(zz), 2, end_way(zz)), :, here] = part[keep:rows]

    def send_sums(p, zz):
        sum_x(p, zz, 0).start()

        @pl.when(middle(zz))
        def _():
            sum_x(p, zz, 1).start()

        for way in range(2):
            @pl.when(jnp.logical_and(from_origin(way) == 0, zz == (0 if way else last_z)))
            def _():
                h_out[p, way] = h_own[p, way].astype(BF16)
                sum_half(p, way, next_z(way)).start()

    turns = 2 * nz - 1

    def owner(j):
        way = j % 2
        return way, z + (nz - 1 - j // 2) * (1 - 2 * way)

    def finish_half(p, way):
        sum_half(p, way, x_peer).wait_recv()
        h_out[p, way] = (h_own[p, way] + h_in[p, way].astype(F32)).astype(BF16)
        sum_half(p, way, next_z(way)).start()

    near_way = jnp.where(2 * z < nz, 0, 1)

    def relay_half(p, way):
        @pl.when(middle(z))
        def _():
            if True:
                finish_half(p, way)

    def own_half(p):
        for way in range(2):
            @pl.when(z == (0 if way else last_z))
            def _():
                sum_half(p, way, x_peer).wait_recv()
                x_out[p, z, keep:, :] = (h_own[p, way] + h_in[p, way].astype(F32)).astype(BF16)
                sum_x(p, z, 1).start()

    def finish(p, way, zz):
        more = inside(z - (1 - 2 * way))

        @pl.when(inside(zz))
        def _():
            if True:
                sum_x(p, zz, 0).wait_recv()

                @pl.when(middle(zz))
                def _():
                    sum_x(p, zz, 1).wait_recv()

            @pl.when(more)
            def _():
                if True:
                    sum_z(p, way, zz).wait_recv()
                z_out[p, zz] = (
                    own_part[p, zz] + x_in[p, zz].astype(F32) + z_in[p, way, zz].astype(F32)
                ).astype(BF16)

            @pl.when(jnp.logical_not(more))
            def _():
                z_out[p, zz] = (own_part[p, zz] + x_in[p, zz].astype(F32)).astype(BF16)

            sum_z(p, way, zz).start()

    def wd_local(s):
        w_local(2, s).wait()
        w_arrived(2, partner, s)

    for s in range(cuts):
        wd_local(s)

    lag = 4

    def hidden_step(j, carry):
        _, zz = owner(j)

        @pl.when(inside(zz))
        def _():
            @pl.when(jnp.logical_or(j < 2, nz < 3))
            def _():
                @pl.when(j < turns - 1)
                def _():
                    other_x_arrived(zz)

                make_gate(zz)

            here = both_rows(zz)
            gate = gates[here, :]
            upward = jnp.dot(tok[here, :], wu[...], preferred_element_type=F32)
            hidden[here, :] = (gate / (1.0 + jnp.exp(-gate)) * upward).astype(BF16)
            down(0, range(cuts), zz)

            @pl.when(j < turns - 1)
            def _():
                send_sums(0, zz)

        @pl.when(jnp.logical_and(j >= lag, jnp.logical_not(middle(z))))
        def _():
            finish(0, *owner(j - lag))

        return carry

    if True:
        lax.fori_loop(0, turns, hidden_step, 0)

    def send_step(t, carry):
        p = t // (turns - 1)
        _, zz = owner(t % (turns - 1))

        @pl.when(inside(zz))
        def _():
            send_sums(p, zz)

        return carry

    lax.fori_loop(turns - 1, cuts * (turns - 1), send_step, 0)

    def finish_way(p, way, start=0):
        def step(n, carry):
            finish(p, way, z + (nz - 1 - n) * (1 - 2 * way))
            return carry

        lax.fori_loop(start, nz - 1, step, 0)

    def finishes(p, start=0):
        near = near_way
        if True:
            relay_half(p, near)
            finish_way(p, near, start)
        if True:
            relay_half(p, 1 - near)
            finish_way(p, 1 - near, start)

    def far_down(s):
        if True:
            relay_weight(2, s)
            for d in range(1, chips):
                w_arrived(2, lax.rem(partner + 2 * d, n_in), s)

        def step(t, carry):
            chip = 1 + t // turns
            j = t % turns
            _, zz = owner(j)

            @pl.when(inside(zz))
            def _():
                down(chip, (s,), zz)

                @pl.when(j < turns - 1)
                def _():
                    send_sums(chip * cuts + s, zz)

            return carry

        if True:
            lax.fori_loop(0, (chips - 1) * turns, step, 0)

    @pl.when(middle(z))
    def _():
        finishes(0)

    @pl.when(jnp.logical_not(middle(z)))
    def _():
        def step(j, carry):
            finish(0, *owner(j))
            return carry

        lax.fori_loop(turns - lag, turns - 1, step, 0)

    todo = list(range(cuts)) + [c * cuts + s for s in range(cuts) for c in range(1, chips)]
    for p in range(1, cuts):
        far_down(p - 1)
        if True:
            finishes(p)
    far_down(cuts - 1)
    for p in range(parts_n):
        sum_x(p, z, 0).start()

        @pl.when(middle(z))
        def _():
            sum_x(p, z, 1).start()
    for p in todo[cuts:]:
        if True:
            finishes(p)

    if True:
        for p in range(parts_n):
            own_half(p)
    if True:
        for p in range(parts_n):
            for way in range(2):
                @pl.when(inside(z - (1 - 2 * way)))
                def _():
                    sum_z(p, way, z).wait_recv()
                    own_part[p, z] = own_part[p, z] + z_in[p, way, z].astype(F32)
            for part in range(2):
                sum_x(p, z, part).wait_recv()
            for q in range(2):
                source = 2 * columns_of(p // cuts) + q
                here = pl.ds(pl.multiple_of(source * width + (p % cuts) * cw, cw), cw)
                cols = slice(q * cw, (q + 1) * cw)
                out_ref[:, here] = (
                    after[:, here].astype(F32)
                    + (own_part[p, z, :, cols] + x_in[p, z, :, cols].astype(F32))).astype(BF16)

    for d in steps:
        kv_send(0, d).wait_send()
    for d in range(chips):
        kv_relay(0, d).wait_send()

    @pl.when(o < n_out - 1)
    def _():
        for d in range(chips):
            kv_send(1, d).wait_send()

    @pl.when(o > 0)
    def _():
        for d in range(chips):
            kv_relay(1, d).wait_send()

    for link in range(3):
        def sent(link=link):
            first_resid(link).wait_send()
            first_attended(link).wait_send()
            first_normed(link).wait_send()

        send_link(link, sent)
    for k in range(3):
        for s in range(w_parts(k)):
            w_pair(k, s).wait_send()
            for d in steps:
                w_far(k, d, s).wait_send()
                w_relay(k, d, s).wait_send()
    for way in range(2):
        step = 1 - 2 * way

        @pl.when(inside(z + step))
        def _():
            tok_half(way, x_peer).wait_send()
            for h in range(1, nz - 1):
                @pl.when(inside(z - step * h))
                def _():
                    tok_z(way, h).wait_send()
            for p in range(parts_n):
                sum_half(p, way, x_peer).wait_send()
    for zz in range(nz):
        ends = zz == 0 or zz == last_z

        @pl.when(z != zz)
        def _():
            tok_x(zz, x, 0).wait_send()
            if not ends:
                tok_x(zz, x, 1).wait_send()

        for p in range(parts_n):
            sum_x(p, zz, 0).wait_send()
            if not ends:
                sum_x(p, zz, 1).wait_send()
            else:
                @pl.when(z == zz)
                def _():
                    sum_x(p, zz, 1).wait_send()

            @pl.when(z != zz)
            def _():
                sum_z(p, 0, zz).wait_send()


def per_device(n_out, n_in, resid, queries, keyvals, piece_order, out_proj, mlp_gain, w_gate, w_up, w_down):
    rows, model = resid.shape
    units, width = w_down.shape
    nz, chips = n_out // 2, n_in // 2
    cuts = max(1, width // 256)
    pieces_w = max(1, 16 // n_in)
    cw = width // cuts
    parts_n = chips * cuts
    early = rows * 3 // 4
    dma = pltpu.SemaphoreType.DMA
    vmem = pl.BlockSpec(memory_space=pltpu.VMEM)
    hbm = pl.BlockSpec(memory_space=pl.ANY)
    spl = max(cuts, pieces_w)
    half = rows - rows // 2
    return pl.pallas_call(
        functools.partial(layer_kernel, n_out, n_in, cuts, pieces_w, early),
        out_shape=jax.ShapeDtypeStruct(resid.shape, BF16),
        in_specs=[pl.BlockSpec(memory_space=pltpu.SMEM)] + [vmem] * 5 + [hbm] * 3,
        out_specs=vmem,
        scratch_shapes=[
            pltpu.VMEM((2 * n_in * rows, keyvals.shape[1]), BF16),
            pltpu.VMEM((model, units), BF16),
            pltpu.VMEM((model, units), BF16),
            pltpu.VMEM((n_in, cuts, units, cw), BF16),
            pltpu.VMEM((n_out * rows, model), BF16),
            pltpu.VMEM((rows, model), BF16),
            pltpu.VMEM(queries.shape, BF16),
            pltpu.VMEM((3, early, model), BF16),
            pltpu.VMEM((3, early, queries.shape[1]), BF16),
            pltpu.VMEM((n_out * rows, units), F32),
            pltpu.VMEM((n_out * rows, units), BF16),
            pltpu.VMEM((parts_n, nz, rows, 2 * cw), BF16),
            pltpu.VMEM((parts_n, nz, rows, 2 * cw), BF16),
            pltpu.VMEM((parts_n, nz, rows, 2 * cw), F32),
            pltpu.VMEM((parts_n, nz, rows, 2 * cw), BF16),
            pltpu.VMEM((parts_n, 2, nz, rows, 2 * cw), BF16),
            pltpu.VMEM((parts_n, 3, half, 2 * cw), F32),
            pltpu.VMEM((parts_n, 2, half, 2 * cw), BF16),
            pltpu.VMEM((parts_n, 2, half, 2 * cw), BF16),
            dma(()), dma((2, n_in)), dma((2, n_in)), dma((2, n_in)),
            dma((3, spl)), dma((3, spl)), dma((3, n_in, spl)), dma((3, n_in, spl)), dma((3, n_in, spl)),
            dma((3,)), dma((3,)), dma((3,)), dma((3,)), dma((3,)), dma((3,)),
            dma((2, nz)), dma((2, nz)), dma((2,)), dma((2,)), dma((2, nz)), dma((2, nz)),
            dma((2, parts_n, nz)), dma((2, parts_n, nz)), dma((parts_n, nz)), dma((parts_n, 2, nz)),
            dma((parts_n, 2)), dma((parts_n, 2)),
        ],
        compiler_params=pltpu.CompilerParams(
            collective_id=0, has_side_effects=True, vmem_limit_bytes=63000 * 1024
        ),
        name="layer",
    )(piece_order, resid, queries, keyvals, out_proj, mlp_gain.reshape(1, -1), w_gate, w_up, w_down)


def solution(mesh):
    placed = (
        P(("outer", "inner"), None),
        P(("outer", "inner"), None),
        P(("outer", "inner"), None),
        P(),
        P(),
        P(),
        P("inner", "outer"),
        P("inner", "outer"),
        P("outer", "inner"),
    )
    return jax.shard_map(
        functools.partial(per_device, mesh.shape["outer"], mesh.shape["inner"]),
        mesh=mesh,
        in_specs=placed,
        out_specs=P(("outer", "inner"), None),
        check_vma=False,
    )
```

```python
import functools

import jax
import jax.numpy as jnp
from jax import lax
from jax.experimental import pallas as pl
from jax.experimental.pallas import tpu as pltpu
from jax.sharding import PartitionSpec as P

MESH = pl.DeviceIdType.MESH
F32 = jnp.float32
BF16 = jnp.bfloat16
EPS = 1e-05


def layer_kernel(
    n_out, n_in, cuts, pieces_w, early,
    order_ref, resid_hbm, query_hbm, kv_ref, proj_hbm, gain_hbm, wg_ref, wu_ref, wd_ref,
    out_ref,
    resid_ref, query_ref, proj_ref, gain_ref, in_sem,
    kv_all, wg, wu, wd, tok, after, att_own, res_in, att_in, gates, hidden,
    x_out, x_in, own_part, z_out, z_in, h_own, h_out, h_in,
    kv_loc, kv_snd, kv_relay_snd, kv_rcv, w_loc, w_pair_snd, w_snd, w_relay_snd, w_rcv,
    r_snd, r_rcv, a_snd, a_rcv, n_snd, n_rcv, z_snd, z_rcv, g_snd, g_rcv, x_snd, x_rcv,
    rx_snd, rx_rcv, rz_snd, rz_rcv, rh_snd, rh_rcv,
):
    o = lax.axis_index("outer")
    i = lax.axis_index("inner")
    nz = n_out // 2
    z, x = o // 2, o % 2
    core = i % 2
    partner = i + 1 - 2 * core
    x_peer = (z * 2 + 1 - x, i)
    core_peer = (o, partner)
    rows = resid_hbm.shape[0]
    head = kv_ref.shape[1] // 2
    heads = query_ref.shape[1] // head
    pieces = order_ref.shape[0]
    block = n_in * rows
    span = block // pieces
    depth = wg_ref.shape[0]
    units, width = wd_ref.shape
    chips = n_in // 2
    parts_n = chips * cuts
    cw = width // cuts
    keep = rows // 2
    last_z = nz - 1

    def remote(src, dst, ssem, rsem, device):
        return pltpu.make_async_remote_copy(
            src_ref=src, dst_ref=dst, send_sem=ssem, recv_sem=rsem,
            device_id=device, device_id_type=MESH,
        )

    def inside(zz):
        return jnp.logical_and(zz >= 0, zz < nz)

    def middle(zz):
        return jnp.logical_and(zz > 0, zz < last_z)

    def z_device(zz):
        return (zz * 2 + x, i)

    barrier = pltpu.get_barrier_semaphore()
    after_o, before_o = lax.rem(o + 1, n_out), lax.rem(o + n_out - 1, n_out)

    def greet(device):
        pl.semaphore_signal(barrier, inc=1, device_id=device, device_id_type=MESH)

    for d in range(1, n_in):
        greet((o, lax.rem(i + d, n_in)))
    greet(x_peer)
    pl.when(z > 0)(lambda: greet(z_device(z - 1)))
    pl.when(z < last_z)(lambda: greet(z_device(z + 1)))

    @pl.when(o > 0)
    def _():
        for d in range(chips):
            greet((before_o, lax.rem(i + 2 * d, n_in)))

    loads = [
        pltpu.make_async_copy(src, dst, in_sem.at[n])
        for n, (src, dst) in enumerate((
            (query_hbm, query_ref), (resid_hbm, resid_ref), (proj_hbm, proj_ref), (gain_hbm, gain_ref)))
    ]
    for load in loads:
        load.start()

    if True:
        pl.semaphore_wait(
            barrier, n_in + jnp.where(z > 0, 1, 0) + jnp.where(z < last_z, 1, 0)
            + jnp.where(o < n_out - 1, chips, 0))

    own_rows = pl.ds(pl.multiple_of(i * rows, rows), rows)
    kv_copy = pltpu.make_async_copy(kv_ref, kv_all.at[own_rows], kv_loc)
    kv_copy.start()

    steps = range(1, chips)

    def kv_slot(part, q):
        return kv_all.at[pl.ds(pl.multiple_of(part * block + q * rows, rows), rows)]

    def kv_send(part, d):
        return remote(kv_ref, kv_slot(part, i), kv_snd.at[part, d], kv_rcv.at[part, i],
                      (after_o if part else o, lax.rem(i + 2 * d, n_in)))

    def kv_relay(part, d):
        q = lax.rem(i + n_in - 2 * d, n_in)
        src = kv_ref if part == 0 and d == 0 else kv_slot(part, q)
        return remote(src, kv_slot(part, q), kv_relay_snd.at[part, d], kv_rcv.at[part, q], core_peer)

    def kv_arrived(part, q):
        here = kv_slot(part, q)
        remote(here, here, kv_relay_snd.at[part, 0], kv_rcv.at[part, q], core_peer).wait_recv()

    for d in steps:
        kv_send(0, d).start()

    @pl.when(o < n_out - 1)
    def _():
        for d in range(chips):
            kv_send(1, d).start()

    kv_relay(0, 0).start()

    def tok_rows(zz, xx, start=0, size=rows):
        return tok.at[pl.ds(pl.multiple_of((zz * 2 + xx) * rows + start, 16), size)]

    def target(link):
        if isinstance(link, int):
            return x_peer if link == 2 else z_device(z + 1 - 2 * link)
        return z_device(z + 1 - 2 * link)

    def first_resid(link):
        return remote(resid_hbm.at[pl.ds(0, early)], res_in.at[link], r_snd.at[link], r_rcv.at[link],
                      target(link))

    def first_attended(link):
        return remote(att_own.at[pl.ds(0, early)], att_in.at[link], a_snd.at[link], a_rcv.at[link],
                      target(link))

    def first_normed(link, source=None):
        here = tok_rows(*(source or (z, x)), early, rows - early)
        return remote(here, here, n_snd.at[link], n_rcv.at[link], target(link))

    def send_link(link, act):
        if link == 2:
            act()
        else:
            pl.when(inside(z + 1 - 2 * link))(act)

    for link in range(3):
        send_link(link, lambda link=link: first_resid(link).start())

    def slot(k, q, s):
        if k == 2:
            return wd.at[q, s]
        full = wg if k == 0 else wu
        size = depth // pieces_w
        return full.at[pl.ds(pl.multiple_of(q * depth + s * size, size), size)]

    srcs = (wg_ref, wu_ref, wd_ref)

    def w_src(k, s):
        if k == 2:
            return wd_ref.at[:, pl.ds(s * cw, cw)]
        size = depth // pieces_w
        return srcs[k].at[pl.ds(s * size, size)]

    def w_parts(k):
        return cuts if k == 2 else pieces_w

    def w_far(k, d, s):
        return remote(w_src(k, s), slot(k, i, s), w_snd.at[k, d, s], w_rcv.at[k, i, s],
                      (o, lax.rem(i + 2 * d, n_in)))

    def w_pair(k, s):
        return remote(w_src(k, s), slot(k, i, s), w_pair_snd.at[k, s], w_rcv.at[k, i, s], core_peer)

    def w_arrived(k, q, s):
        here = slot(k, q, s)
        remote(here, here, w_pair_snd.at[k, s], w_rcv.at[k, q, s], core_peer).wait_recv()

    def w_relay(k, d, s):
        q = lax.rem(i + n_in - 2 * d, n_in)
        here = slot(k, q, s)
        return remote(here, here, w_relay_snd.at[k, d, s], w_rcv.at[k, q, s], core_peer)

    def w_local(k, s):
        return pltpu.make_async_copy(w_src(k, s), slot(k, i, s), w_loc.at[k, s])

    for k in range(3):
        for s in range(w_parts(k)):
            for d in steps:
                w_far(k, d, s).start()
    for k in range(3):
        for s in range(w_parts(k)):
            w_pair(k, s).start()
            w_local(k, s).start()

    def relay_weight(k, s):
        for d in steps:
            w_arrived(k, lax.rem(i + n_in - 2 * d, n_in), s)
            w_relay(k, d, s).start()

    def weight_ready(k):
        for s in range(w_parts(k)):
            w_local(k, s).wait()
            for d in range(chips):
                w_arrived(k, lax.rem(partner + 2 * d, n_in), s)

    lane = lax.broadcasted_iota(jnp.int32, (rows, block), 1)
    key_pos = jnp.zeros((rows, block), jnp.int32)
    for p in range(pieces):
        key_pos = jnp.where(lane // span == p, order_ref[p] * span + lane % span, key_pos)
    row = lax.broadcasted_iota(jnp.int32, (rows, block), 0)
    query_pos = jnp.zeros((rows, block), jnp.int32)
    for p in range(rows // span):
        query_pos = jnp.where(
            row // span == p, order_ref[i * (rows // span) + p] * span + row % span, query_pos)
    own_visible = key_pos <= query_pos
    before_visible = (jnp.zeros((rows, block), jnp.int32) + o) > 0

    @pl.when(o == 0)
    def _():
        kv_all[block:, :] = jnp.zeros((block, 2 * head), BF16)

    for zz in (0, last_z):
        @pl.when(z != zz)
        def _():
            x_in[:, zz, keep:, :] = jnp.zeros((parts_n, rows - keep, 2 * cw), BF16)

    for d in steps:
        kv_arrived(0, lax.rem(i + n_in - 2 * d, n_in))
        kv_relay(0, d).start()

    @pl.when(o > 0)
    def _():
        for d in range(chips):
            kv_arrived(1, lax.rem(i + n_in - 2 * d, n_in))
            kv_relay(1, d).start()

    kv_copy.wait()
    for d in range(chips):
        kv_arrived(0, lax.rem(partner + 2 * d, n_in))

    @pl.when(o > 0)
    def _():
        for d in range(chips):
            kv_arrived(1, lax.rem(partner + 2 * d, n_in))

    if True:
        loads[0].wait()
        parts = []
        nt = (((1,), (1,)), ((), ()))
        for h in range(heads):
            query = query_ref[:, h * head:(h + 1) * head]
            own_score = lax.dot_general(
                query, kv_all[:block, :head], nt, preferred_element_type=F32) * head ** (-0.5)
            before_score = lax.dot_general(
                query, kv_all[block:, :head], nt, preferred_element_type=F32) * head ** (-0.5)
            own_score = jnp.where(own_visible, own_score, -1e30)
            before_score = jnp.where(before_visible, before_score, -1e30)
            top = jnp.maximum(
                jnp.max(own_score, axis=1, keepdims=True), jnp.max(before_score, axis=1, keepdims=True))
            own_w = jnp.where(own_visible, jnp.exp(own_score - top), 0.0)
            before_w = jnp.where(before_visible, jnp.exp(before_score - top), 0.0)
            total = jnp.sum(own_w, axis=1, keepdims=True) + jnp.sum(before_w, axis=1, keepdims=True)
            mixed = jnp.dot(own_w.astype(BF16), kv_all[:block, head:], preferred_element_type=F32)
            mixed += jnp.dot(before_w.astype(BF16), kv_all[block:, head:], preferred_element_type=F32)
            parts.append((mixed / total).astype(BF16))
        att_own[...] = jnp.concatenate(parts, axis=1)
        for link in range(3):
            send_link(link, lambda link=link: first_attended(link).start())

        for load in loads[1:]:
            load.wait()

        def normed_of(resid, attended):
            after_attn = (
                resid.astype(F32) + jnp.dot(attended, proj_ref[...], preferred_element_type=F32)
            ).astype(BF16)
            wide = after_attn.astype(F32)
            normed = wide * lax.rsqrt(jnp.mean(wide * wide, axis=1, keepdims=True) + EPS) * gain_ref[...]
            return after_attn, normed.astype(BF16)

        after_attn, normed = normed_of(resid_ref[...], att_own[...])
        after[...] = after_attn
        tok_rows(z, x)[...] = normed
        for link in range(3):
            send_link(link, lambda link=link: first_normed(link).start())

    def part_rows(zz, xx, part):
        return tok_rows(zz, xx, part * early, rows - early if part else early)

    def tok_z(way, h, part):
        step = 1 - 2 * way
        here = part_rows(z - step * h, x, part)
        return remote(here, here, z_snd.at[part, way, h], z_rcv.at[part, way, h], z_device(z + step))

    def tok_z_arrived(way, h, part):
        here = part_rows(z - (1 - 2 * way) * (h + 1), x, part)
        remote(here, here, z_snd.at[part, way, h], z_rcv.at[part, way, h], x_peer).wait_recv()

    def tok_x(zz, xx, part):
        here = part_rows(zz, xx, part)
        return remote(here, here, x_snd.at[part, zz], x_rcv.at[part, zz], x_peer)

    def tok_x_end(zz, xx):
        here = tok_rows(zz, xx, 0, keep)
        return remote(here, here, x_snd.at[0, zz], x_rcv.at[0, zz], x_peer)

    def send_x(zz, part):
        @pl.when(middle(zz))
        def _():
            tok_x(zz, x, part).start()

        if part == 0:
            @pl.when(jnp.logical_not(middle(zz)))
            def _():
                tok_x_end(zz, x).start()

    def tok_half(way, to):
        here = tok_rows(last_z if way else 0, 1 - x, keep, rows - keep)
        return remote(here, here, g_snd.at[way], g_rcv.at[way], to)

    def from_origin(way):
        return last_z - z if way else z

    near_way = jnp.where(2 * z < nz, 0, 1)

    def absorb(link, zz, xx):
        first_resid(link).wait_recv()
        first_attended(link).wait_recv()
        tok_rows(zz, xx, 0, early)[...] = normed_of(res_in[link], att_in[link])[1]

    def hop(h, part, way):
        step = 1 - 2 * way
        source = z - step * (h + 1)

        @pl.when(inside(source))
        def _():
            if True:
                if h > 0:
                    tok_z_arrived(way, h, part)
                elif part == 0:
                    absorb(way, source, x)
                else:
                    first_normed(way, (source, x)).wait_recv()
                if h < nz - 2:
                    @pl.when(inside(z + step))
                    def _():
                        tok_z(way, h + 1, part).start()

                send_x(source, part)

    def pair_of(j):
        return z + ((j + 1) // 2) * (1 - 2 * (j % 2))

    def both_rows(zz):
        return pl.ds(pl.multiple_of(zz * 2 * rows, 2 * rows), 2 * rows)

    def make_gate(zz):
        here = both_rows(zz)
        gates[here, :] = jnp.dot(tok[here, :], wg[...], preferred_element_type=F32)

    def other_x_arrived(zz):
        if True:
            @pl.when(middle(zz))
            def _():
                tok_x(zz, 1 - x, 0).wait_recv()
                tok_x(zz, 1 - x, 1).wait_recv()

            @pl.when(jnp.logical_not(middle(zz)))
            def _():
                tok_x_end(zz, 1 - x).wait_recv()

    def gate_step(j, carry):
        zz = pair_of(j)

        @pl.when(inside(zz))
        def _():
            @pl.when(j > 0)
            def _():
                other_x_arrived(zz)

            make_gate(zz)

        return carry

    relays = [(k, s) for k in range(2) for s in range(pieces_w)]

    def relay_to(n):
        while relays and n > 0:
            k, s = relays.pop(0)
            relay_weight(k, s)
            n -= 1

    def halves(h):
        for way in range(2):
            @pl.when(from_origin(way) == h + 1)
            def _():
                if True:
                    tok_half(way, x_peer).wait_recv()

                @pl.when(inside(z + 1 - 2 * way))
                def _():
                    tok_half(way, z_device(z + 1 - 2 * way)).start()

    for h in range(nz - 1):
        for part in range(2):
            hop(h, part, 1 - near_way)
            hop(h, part, near_way)
        if h == 0:
            if True:
                absorb(2, z, 1 - x)
                first_normed(2, (z, 1 - x)).wait_recv()
                for way in range(2):
                    @pl.when(from_origin(way) == 0)
                    def _():
                        tok_half(way, z_device(z + 1 - 2 * way)).start()
            relay_to((pieces_w + 1) // 2)
        elif h == 1:
            if True:
                relay_to(pieces_w - (pieces_w + 1) // 2)
                weight_ready(0)
            if True:
                lax.fori_loop(0, 3, gate_step, 0)
            relay_to(1)
        else:
            relay_to(1)
            if True:
                lax.fori_loop(2 * h - 1, 2 * h + 1, gate_step, 0)
        halves(h)
    if True:
        relay_to(len(relays))
        weight_ready(1)

    def columns_of(chip):
        return lax.rem(i // 2 + chips - chip, chips)

    def end_way(zz):
        return jnp.where(zz == last_z, 0, 1)

    def sum_x(p, zz, part):
        there = pl.ds(part * keep, rows - keep if part else keep)
        return remote(x_out.at[p, zz, there], x_in.at[p, zz, there], rx_snd.at[part, p, zz],
                      rx_rcv.at[part, p, zz], x_peer)

    def sum_z(p, way, zz):
        step = jnp.where(inside(z + 1 - 2 * way), 1 - 2 * way, 0)
        return remote(z_out.at[p, zz], z_in.at[p, way, zz], rz_snd.at[p, zz], rz_rcv.at[p, way, zz],
                      z_device(z + step))

    def sum_half(p, way, to):
        return remote(h_out.at[p, way], h_in.at[p, way], rh_snd.at[p, way], rh_rcv.at[p, way], to)

    def next_z(way):
        return z_device(jnp.clip(z + 1 - 2 * way, 0, last_z))

    def down(chip, cs, zz):
        def half(xx):
            return hidden[pl.ds(pl.multiple_of((zz * 2 + xx) * rows, rows), rows), :]

        both = jnp.concatenate([half(1 - x), half(x)], axis=0)
        for c in cs:
            p = chip * cuts + c
            for q in range(2):
                part = jnp.dot(both, wd[2 * columns_of(chip) + q, c], preferred_element_type=F32)
                here = slice(q * cw, (q + 1) * cw)
                x_out[p, zz, :, here] = part[:rows].astype(BF16)
                own_part[p, zz, :, here] = part[rows:]
                h_own[p, jnp.where(middle(zz), 2, end_way(zz)), :, here] = part[keep:rows]

    def send_sums(p, zz):
        sum_x(p, zz, 0).start()

        @pl.when(middle(zz))
        def _():
            sum_x(p, zz, 1).start()

    def send_halves(ps, zz):
        for way in range(2):
            @pl.when(jnp.logical_and(from_origin(way) == 0, zz == (0 if way else last_z)))
            def _():
                for p in ps:
                    h_out[p, way] = h_own[p, way].astype(BF16)
                    sum_half(p, way, next_z(way)).start()

    turns = 2 * nz - 1

    def owner(j):
        way = j % 2
        return way, z + (nz - 1 - j // 2) * (1 - 2 * way)

    def finish_half(p, way):
        sum_half(p, way, x_peer).wait_recv()
        h_out[p, way] = (h_own[p, way] + h_in[p, way].astype(F32)).astype(BF16)
        sum_half(p, way, next_z(way)).start()

    def relay_half(p, way):
        @pl.when(middle(z))
        def _():
            if True:
                finish_half(p, way)

    def own_half(p):
        for way in range(2):
            @pl.when(z == (0 if way else last_z))
            def _():
                sum_half(p, way, x_peer).wait_recv()
                x_out[p, z, keep:, :] = (h_own[p, way] + h_in[p, way].astype(F32)).astype(BF16)
                sum_x(p, z, 1).start()

    def finish(p, way, zz):
        more = inside(z - (1 - 2 * way))

        @pl.when(inside(zz))
        def _():
            if True:
                sum_x(p, zz, 0).wait_recv()

                @pl.when(middle(zz))
                def _():
                    sum_x(p, zz, 1).wait_recv()

            @pl.when(more)
            def _():
                if True:
                    sum_z(p, way, zz).wait_recv()
                z_out[p, zz] = (
                    own_part[p, zz] + x_in[p, zz].astype(F32) + z_in[p, way, zz].astype(F32)
                ).astype(BF16)

            @pl.when(jnp.logical_not(more))
            def _():
                z_out[p, zz] = (own_part[p, zz] + x_in[p, zz].astype(F32)).astype(BF16)

            sum_z(p, way, zz).start()

    def wd_local(s):
        w_local(2, s).wait()
        w_arrived(2, partner, s)

    for s in range(cuts):
        wd_local(s)

    lag = 4

    def hidden_step(j, carry):
        _, zz = owner(j)

        @pl.when(jnp.logical_and(j >= lag, jnp.logical_not(middle(z))))
        def _():
            for p in range(cuts):
                finish(p, *owner(j - lag))

        @pl.when(inside(zz))
        def _():
            @pl.when(jnp.logical_or(j < 2, nz < 3))
            def _():
                @pl.when(j < turns - 1)
                def _():
                    other_x_arrived(zz)

                make_gate(zz)

            here = both_rows(zz)
            gate = gates[here, :]
            upward = jnp.dot(tok[here, :], wu[...], preferred_element_type=F32)
            hidden[here, :] = (gate / (1.0 + jnp.exp(-gate)) * upward).astype(BF16)
            down(0, range(cuts), zz)

            @pl.when(j < turns - 1)
            def _():
                for p in range(cuts):
                    send_sums(p, zz)
                send_halves(range(cuts), zz)

        return carry

    if True:
        lax.fori_loop(0, turns, hidden_step, 0)

    near_end = jnp.where(near_way == 0, last_z, 0)

    def finish_end(p):
        if True:
            relay_half(p, near_way)
            finish(p, near_way, near_end)

    def finish_way(p, way, skip):
        def step(n, carry):
            zz = z + (nz - 1 - n) * (1 - 2 * way)

            @pl.when(zz != skip)
            def _():
                finish(p, way, zz)

            return carry

        lax.fori_loop(0, nz - 1, step, 0)

    def finish_middle(ps):
        for p in ps:
            if True:
                relay_half(p, 1 - near_way)
                finish_way(p, 1 - near_way, -1)
            if True:
                finish_way(p, near_way, near_end)

    def finish_outer(ps, start, done=0):
        def step(n, carry):
            @pl.when(n >= done)
            def _():
                for p in ps:
                    finish(p, near_way, z + (nz - 1 - n) * (1 - 2 * near_way))
            return carry

        lax.fori_loop(start, nz - 1, step, 0)

    def far_down(s):
        if True:
            relay_weight(2, s)
            for d in range(1, chips):
                w_arrived(2, lax.rem(partner + 2 * d, n_in), s)

        def step(t, carry):
            chip = 1 + t // turns
            j = t % turns
            _, zz = owner(j)

            @pl.when(inside(zz))
            def _():
                down(chip, (s,), zz)

                @pl.when(j < turns - 1)
                def _():
                    send_sums(chip * cuts + s, zz)
                    send_halves((chip * cuts + s,), zz)

            return carry

        if True:
            lax.fori_loop(0, (chips - 1) * turns, step, 0)

    @pl.when(middle(z))
    def _():
        for p in range(cuts):
            finish_end(p)
        finish_middle(range(cuts))

    @pl.when(jnp.logical_not(middle(z)))
    def _():
        finish_outer(range(cuts), (turns - lag) // 2, jnp.where(near_way == 0, (turns - lag + 1) // 2, 0))

    rest = [c * cuts + s for s in range(cuts) for c in range(1, chips)]

    def drain_first():
        for d in steps:
            kv_send(0, d).wait_send()
        for d in range(chips):
            kv_relay(0, d).wait_send()

        @pl.when(o < n_out - 1)
        def _():
            for d in range(chips):
                kv_send(1, d).wait_send()

        @pl.when(o > 0)
        def _():
            for d in range(chips):
                kv_relay(1, d).wait_send()

        for link in range(3):
            def sent(link=link):
                first_resid(link).wait_send()
                first_attended(link).wait_send()
                first_normed(link).wait_send()

            send_link(link, sent)
        for way in range(2):
            step = 1 - 2 * way

            @pl.when(inside(z + step))
            def _():
                tok_half(way, x_peer).wait_send()
                for h in range(1, nz - 1):
                    @pl.when(inside(z - step * h))
                    def _():
                        tok_z(way, h, 0).wait_send()
                        tok_z(way, h, 1).wait_send()
        for zz in range(nz):
            @pl.when(z != zz)
            def _():
                if zz == 0 or zz == last_z:
                    tok_x_end(zz, x).wait_send()
                else:
                    tok_x(zz, x, 0).wait_send()
                    tok_x(zz, x, 1).wait_send()

    def drain_weights(k):
        for s in range(w_parts(k)):
            w_pair(k, s).wait_send()
            for d in steps:
                w_far(k, d, s).wait_send()
                w_relay(k, d, s).wait_send()

    def drain_sums(p):
        for way in range(2):
            @pl.when(inside(z + 1 - 2 * way))
            def _():
                sum_half(p, way, x_peer).wait_send()
        for zz in range(nz):
            sum_x(p, zz, 0).wait_send()
            if 0 < zz < last_z:
                sum_x(p, zz, 1).wait_send()
            else:
                @pl.when(z == zz)
                def _():
                    sum_x(p, zz, 1).wait_send()

            @pl.when(z != zz)
            def _():
                sum_z(p, 0, zz).wait_send()

    if True:
        drain_first()
    for s in range(cuts):
        far_down(s)
        if s == cuts - 1:
            for p in range(parts_n):
                sum_x(p, z, 0).start()

                @pl.when(middle(z))
                def _():
                    sum_x(p, z, 1).start()
        for c in range(1, chips):
            finish_end(c * cuts + s)
    if True:
        for k in range(3):
            drain_weights(k)

    @pl.when(middle(z))
    def _():
        finish_middle(rest)

    @pl.when(jnp.logical_not(middle(z)))
    def _():
        finish_outer(rest, 1)

    if True:
        for p in range(parts_n):
            own_half(p)
    for p in range(parts_n):
        if True:
            for way in range(2):
                @pl.when(inside(z - (1 - 2 * way)))
                def _():
                    sum_z(p, way, z).wait_recv()
                    own_part[p, z] = own_part[p, z] + z_in[p, way, z].astype(F32)
            for part in range(2):
                sum_x(p, z, part).wait_recv()
            for q in range(2):
                source = 2 * columns_of(p // cuts) + q
                here = pl.ds(pl.multiple_of(source * width + (p % cuts) * cw, cw), cw)
                cols = slice(q * cw, (q + 1) * cw)
                out_ref[:, here] = (
                    after[:, here].astype(F32)
                    + (own_part[p, z, :, cols] + x_in[p, z, :, cols].astype(F32))).astype(BF16)
        if p < parts_n - 1:
            drain_sums(p)

    drain_sums(parts_n - 1)


def per_device(n_out, n_in, resid, queries, keyvals, piece_order, out_proj, mlp_gain, w_gate, w_up, w_down):
    rows, model = resid.shape
    units, width = w_down.shape
    nz, chips = n_out // 2, n_in // 2
    cuts = max(1, width // 256)
    pieces_w = max(1, 16 // n_in)
    cw = width // cuts
    parts_n = chips * cuts
    early = rows * 3 // 4
    dma = pltpu.SemaphoreType.DMA
    vmem = pl.BlockSpec(memory_space=pltpu.VMEM)
    hbm = pl.BlockSpec(memory_space=pl.ANY)
    spl = max(cuts, pieces_w)
    half = rows - rows // 2
    return pl.pallas_call(
        functools.partial(layer_kernel, n_out, n_in, cuts, pieces_w, early),
        out_shape=pltpu.VMEM(resid.shape, BF16),
        in_specs=[pl.BlockSpec(memory_space=pltpu.SMEM)] + [hbm] * 8,
        out_specs=vmem,
        scratch_shapes=[
            pltpu.VMEM(resid.shape, BF16),
            pltpu.VMEM(queries.shape, BF16),
            pltpu.VMEM(out_proj.shape, BF16),
            pltpu.VMEM((1, model), F32),
            dma((4,)),
            pltpu.VMEM((2 * n_in * rows, keyvals.shape[1]), BF16),
            pltpu.VMEM((model, units), BF16),
            pltpu.VMEM((model, units), BF16),
            pltpu.VMEM((n_in, cuts, units, cw), BF16),
            pltpu.VMEM((n_out * rows, model), BF16),
            pltpu.VMEM((rows, model), BF16),
            pltpu.VMEM(queries.shape, BF16),
            pltpu.VMEM((3, early, model), BF16),
            pltpu.VMEM((3, early, queries.shape[1]), BF16),
            pltpu.VMEM((n_out * rows, units), F32),
            pltpu.VMEM((n_out * rows, units), BF16),
            pltpu.VMEM((parts_n, nz, rows, 2 * cw), BF16),
            pltpu.VMEM((parts_n, nz, rows, 2 * cw), BF16),
            pltpu.VMEM((parts_n, nz, rows, 2 * cw), F32),
            pltpu.VMEM((parts_n, nz, rows, 2 * cw), BF16),
            pltpu.VMEM((parts_n, 2, nz, rows, 2 * cw), BF16),
            pltpu.VMEM((parts_n, 3, half, 2 * cw), F32),
            pltpu.VMEM((parts_n, 2, half, 2 * cw), BF16),
            pltpu.VMEM((parts_n, 2, half, 2 * cw), BF16),
            dma(()), dma((2, chips)), dma((2, chips)), dma((2, n_in)),
            dma((3, spl)), dma((3, spl)), dma((3, chips, spl)), dma((3, chips, spl)), dma((3, n_in, spl)),
            dma((3,)), dma((3,)), dma((3,)), dma((3,)), dma((3,)), dma((3,)),
            dma((2, 2, nz)), dma((2, 2, nz)), dma((2,)), dma((2,)), dma((2, nz)), dma((2, nz)),
            dma((2, parts_n, nz)), dma((2, parts_n, nz)), dma((parts_n, nz)), dma((parts_n, 2, nz)),
            dma((parts_n, 2)), dma((parts_n, 2)),
        ],
        compiler_params=pltpu.CompilerParams(
            collective_id=0, has_side_effects=True, vmem_limit_bytes=63000 * 1024
        ),
        name="layer",
    )(piece_order, resid, queries, keyvals, out_proj, mlp_gain.reshape(1, -1), w_gate, w_up, w_down)


def solution(mesh):
    placed = (
        P(("outer", "inner"), None),
        P(("outer", "inner"), None),
        P(("outer", "inner"), None),
        P(),
        P(),
        P(),
        P("inner", "outer"),
        P("inner", "outer"),
        P("outer", "inner"),
    )
    return jax.shard_map(
        functools.partial(per_device, mesh.shape["outer"], mesh.shape["inner"]),
        mesh=mesh,
        in_specs=placed,
        out_specs=P(("outer", "inner"), None),
        check_vma=False,
    )
```

```python
import functools

import jax
import jax.numpy as jnp
from jax import lax
from jax.experimental import pallas as pl
from jax.experimental.pallas import tpu as pltpu
from jax.sharding import PartitionSpec as P

MESH = pl.DeviceIdType.MESH
F32 = jnp.float32
BF16 = jnp.bfloat16
EPS = 1e-05


def layer_kernel(
    n_out, n_in, cuts, pieces_w, early,
    order_ref, resid_hbm, query_hbm, kv_ref, proj_hbm, gain_hbm, wg_ref, wu_ref, wd_ref,
    out_ref,
    resid_ref, query_ref, proj_ref, gain_ref, in_sem,
    kv_all, wg, wu, wd, tok, after, att_own, res_in, att_in, gates, hidden,
    x_out, x_in, own_part, z_out, z_in, h_own, h_out, h_in,
    kv_loc, kv_snd, kv_relay_snd, kv_rcv, w_loc, w_pair_snd, w_pair_rcv, w_snd, w_relay_snd, w_rcv,
    r_snd, r_rcv, a_snd, a_rcv, n_rcv, z_snd, z_rcv, g_snd, g_rcv, x_snd, x_rcv,
    rx_snd, rx_rcv, rz_snd, rz_rcv, rh_snd, rh_rcv,
):
    o = lax.axis_index("outer")
    i = lax.axis_index("inner")
    nz = n_out // 2
    z, x = o // 2, o % 2
    core = i % 2
    partner = i + 1 - 2 * core
    x_peer = (z * 2 + 1 - x, i)
    core_peer = (o, partner)
    rows = resid_hbm.shape[0]
    head = kv_ref.shape[1] // 2
    heads = query_ref.shape[1] // head
    pieces = order_ref.shape[0]
    block = n_in * rows
    span = block // pieces
    depth = wg_ref.shape[0]
    units, width = wd_ref.shape
    chips = n_in // 2
    parts_n = chips * cuts
    cw = width // cuts
    keep = rows // 2
    last_z = nz - 1

    def remote(src, dst, ssem, rsem, device):
        return pltpu.make_async_remote_copy(
            src_ref=src, dst_ref=dst, send_sem=ssem, recv_sem=rsem,
            device_id=device, device_id_type=MESH,
        )

    def inside(zz):
        return jnp.logical_and(zz >= 0, zz < nz)

    def middle(zz):
        return jnp.logical_and(zz > 0, zz < last_z)

    def z_device(zz):
        return (zz * 2 + x, i)

    barrier = pltpu.get_barrier_semaphore()
    after_o, before_o = lax.rem(o + 1, n_out), lax.rem(o + n_out - 1, n_out)

    def greet(device):
        pl.semaphore_signal(barrier, inc=1, device_id=device, device_id_type=MESH)

    for d in range(1, n_in):
        greet((o, lax.rem(i + d, n_in)))
    greet(x_peer)
    pl.when(z > 0)(lambda: greet(z_device(z - 1)))
    pl.when(z < last_z)(lambda: greet(z_device(z + 1)))

    @pl.when(o > 0)
    def _():
        for d in range(chips):
            greet((before_o, lax.rem(i + 2 * d, n_in)))

    loads = [
        pltpu.make_async_copy(src, dst, in_sem.at[n])
        for n, (src, dst) in enumerate((
            (query_hbm, query_ref), (resid_hbm, resid_ref), (proj_hbm, proj_ref), (gain_hbm, gain_ref)))
    ]
    for load in loads:
        load.start()

    if True:
        pl.semaphore_wait(
            barrier, n_in + jnp.where(z > 0, 1, 0) + jnp.where(z < last_z, 1, 0)
            + jnp.where(o < n_out - 1, chips, 0))

    own_rows = pl.ds(pl.multiple_of(i * rows, rows), rows)
    kv_copy = pltpu.make_async_copy(kv_ref, kv_all.at[own_rows], kv_loc)
    kv_copy.start()

    steps = range(1, chips)

    def kv_slot(part, q):
        return kv_all.at[pl.ds(pl.multiple_of(part * block + q * rows, rows), rows)]

    def kv_send(part, d):
        return remote(kv_ref, kv_slot(part, i), kv_snd.at[part, d], kv_rcv.at[part, i],
                      (after_o if part else o, lax.rem(i + 2 * d, n_in)))

    def kv_relay(part, d):
        q = lax.rem(i + n_in - 2 * d, n_in)
        src = kv_ref if part == 0 and d == 0 else kv_slot(part, q)
        return remote(src, kv_slot(part, q), kv_relay_snd.at[part, d], kv_rcv.at[part, q], core_peer)

    def kv_arrived(part, q):
        here = kv_slot(part, q)
        remote(here, here, kv_relay_snd.at[part, 0], kv_rcv.at[part, q], core_peer).wait_recv()

    for d in steps:
        kv_send(0, d).start()

    @pl.when(o < n_out - 1)
    def _():
        for d in range(chips):
            kv_send(1, d).start()

    kv_relay(0, 0).start()

    def tok_rows(zz, xx, start=0, size=rows):
        return tok.at[pl.ds(pl.multiple_of((zz * 2 + xx) * rows + start, 16), size)]

    def target(link):
        if isinstance(link, int):
            return x_peer if link == 2 else z_device(z + 1 - 2 * link)
        return z_device(z + 1 - 2 * link)

    def first_resid(link):
        return remote(resid_hbm.at[pl.ds(0, early)], res_in.at[link], r_snd.at[link], r_rcv.at[link],
                      target(link))

    def first_attended(link):
        return remote(att_own.at[pl.ds(0, early)], att_in.at[link], a_snd.at[link], a_rcv.at[link],
                      target(link))

    def first_normed(link, source=None):
        here = tok_rows(*(source or (z, x)), early, rows - early)
        return remote(here, here, r_snd.at[link], n_rcv.at[link], target(link))

    def send_link(link, act):
        if link == 2:
            act()
        else:
            pl.when(inside(z + 1 - 2 * link))(act)

    for link in range(3):
        send_link(link, lambda link=link: first_resid(link).start())

    def slot(k, q, s):
        if k == 2:
            return wd.at[q, s]
        full = wg if k == 0 else wu
        size = depth // pieces_w
        return full.at[pl.ds(pl.multiple_of(q * depth + s * size, size), size)]

    srcs = (wg_ref, wu_ref, wd_ref)

    def w_src(k, s):
        if k == 2:
            return wd_ref.at[:, pl.ds(s * cw, cw)]
        size = depth // pieces_w
        return srcs[k].at[pl.ds(s * size, size)]

    def w_parts(k):
        return cuts if k == 2 else pieces_w

    def shard(k, q):
        if k == 2:
            return wd.at[q]
        full = wg if k == 0 else wu
        return full.at[pl.ds(pl.multiple_of(q * depth, depth), depth)]

    def far(d):
        return lax.rem(i + n_in - 2 * d, n_in)

    def w_far(k, d, s):
        return remote(w_src(k, s), slot(k, i, s), w_snd.at[k, d], w_rcv.at[k, d - 1, 0, s],
                      (o, lax.rem(i + 2 * d, n_in)))

    def w_relay(k, d, s):
        here = slot(k, far(d), s)
        return remote(here, here, w_relay_snd.at[k, d], w_rcv.at[k, d - 1, 1, s], core_peer)

    def w_pair(k, s):
        return remote(w_src(k, s), slot(k, i, s), w_pair_snd.at[k], w_pair_rcv.at[k], core_peer)

    def w_local(k, s):
        return pltpu.make_async_copy(w_src(k, s), slot(k, i, s), w_loc.at[k])

    def near_ready(k):
        mine, other = shard(k, i), shard(k, partner)
        pltpu.make_async_copy(mine, mine, w_loc.at[k]).wait()
        remote(other, other, w_pair_snd.at[k], w_pair_rcv.at[k], core_peer).wait_recv()

    def far_ready(k, s):
        for d in steps:
            here = slot(k, lax.rem(partner + n_in - 2 * d, n_in), s)
            remote(here, here, w_relay_snd.at[k, d], w_rcv.at[k, d - 1, 1, s], core_peer).wait_recv()

    def relay_weight(k, s):
        for d in steps:
            here = slot(k, far(d), s)
            remote(here, here, w_relay_snd.at[k, d], w_rcv.at[k, d - 1, 0, s], core_peer).wait_recv()
            w_relay(k, d, s).start()

    def weight_ready(k):
        near_ready(k)
        for s in range(w_parts(k)):
            far_ready(k, s)

    def drain_weights(k):
        mine = shard(k, i)
        remote(mine, mine, w_pair_snd.at[k], w_pair_rcv.at[k], core_peer).wait_send()
        for d in steps:
            remote(mine, mine, w_snd.at[k, d], w_pair_rcv.at[k], core_peer).wait_send()
            remote(mine, mine, w_relay_snd.at[k, d], w_pair_rcv.at[k], core_peer).wait_send()

    for k in range(3):
        for s in range(w_parts(k)):
            for d in steps:
                w_far(k, d, s).start()
    for k in range(3):
        for s in range(w_parts(k)):
            w_pair(k, s).start()
            w_local(k, s).start()

    lane = lax.broadcasted_iota(jnp.int32, (rows, block), 1)
    key_pos = jnp.zeros((rows, block), jnp.int32)
    for p in range(pieces):
        key_pos = jnp.where(lane // span == p, order_ref[p] * span + lane % span, key_pos)
    row = lax.broadcasted_iota(jnp.int32, (rows, block), 0)
    query_pos = jnp.zeros((rows, block), jnp.int32)
    for p in range(rows // span):
        query_pos = jnp.where(
            row // span == p, order_ref[i * (rows // span) + p] * span + row % span, query_pos)
    own_visible = key_pos <= query_pos
    before_visible = (jnp.zeros((rows, block), jnp.int32) + o) > 0

    @pl.when(o == 0)
    def _():
        kv_all[block:, :] = jnp.zeros((block, 2 * head), BF16)

    for zz in (0, last_z):
        @pl.when(z != zz)
        def _():
            x_in[:, zz, keep:, :] = jnp.zeros((parts_n, rows - keep, 2 * cw), BF16)

    for d in steps:
        kv_arrived(0, lax.rem(i + n_in - 2 * d, n_in))
        kv_relay(0, d).start()

    @pl.when(o > 0)
    def _():
        for d in range(chips):
            kv_arrived(1, lax.rem(i + n_in - 2 * d, n_in))
            kv_relay(1, d).start()

    kv_copy.wait()
    for d in range(chips):
        kv_arrived(0, lax.rem(partner + 2 * d, n_in))

    @pl.when(o > 0)
    def _():
        for d in range(chips):
            kv_arrived(1, lax.rem(partner + 2 * d, n_in))

    if True:
        loads[0].wait()
        parts = []
        nt = (((1,), (1,)), ((), ()))
        for h in range(heads):
            query = query_ref[:, h * head:(h + 1) * head]
            own_score = lax.dot_general(
                query, kv_all[:block, :head], nt, preferred_element_type=F32) * head ** (-0.5)
            before_score = lax.dot_general(
                query, kv_all[block:, :head], nt, preferred_element_type=F32) * head ** (-0.5)
            own_score = jnp.where(own_visible, own_score, -1e30)
            before_score = jnp.where(before_visible, before_score, -1e30)
            top = jnp.maximum(
                jnp.max(own_score, axis=1, keepdims=True), jnp.max(before_score, axis=1, keepdims=True))
            own_w = jnp.where(own_visible, jnp.exp(own_score - top), 0.0)
            before_w = jnp.where(before_visible, jnp.exp(before_score - top), 0.0)
            total = jnp.sum(own_w, axis=1, keepdims=True) + jnp.sum(before_w, axis=1, keepdims=True)
            mixed = jnp.dot(own_w.astype(BF16), kv_all[:block, head:], preferred_element_type=F32)
            mixed += jnp.dot(before_w.astype(BF16), kv_all[block:, head:], preferred_element_type=F32)
            parts.append((mixed / total).astype(BF16))
        att_own[...] = jnp.concatenate(parts, axis=1)
        for link in range(3):
            send_link(link, lambda link=link: first_attended(link).start())

        for load in loads[1:]:
            load.wait()

        def normed_of(resid, attended):
            after_attn = (
                resid.astype(F32) + jnp.dot(attended, proj_ref[...], preferred_element_type=F32)
            ).astype(BF16)
            wide = after_attn.astype(F32)
            normed = wide * lax.rsqrt(jnp.mean(wide * wide, axis=1, keepdims=True) + EPS) * gain_ref[...]
            return after_attn, normed.astype(BF16)

        after_attn, normed = normed_of(resid_ref[...], att_own[...])
        after[...] = after_attn
        tok_rows(z, x)[...] = normed
        for link in range(3):
            send_link(link, lambda link=link: first_normed(link).start())

    def part_rows(zz, xx, part):
        return tok_rows(zz, xx, part * early, rows - early if part else early)

    def tok_z(way, h, part):
        step = 1 - 2 * way
        here = part_rows(z - step * h, x, part)
        return remote(here, here, z_snd.at[way, h - 1], z_rcv.at[part, way, h - 1], z_device(z + step))

    def tok_z_arrived(way, h, part):
        here = part_rows(z - (1 - 2 * way) * (h + 1), x, part)
        remote(here, here, z_snd.at[way, h - 1], z_rcv.at[part, way, h - 1], x_peer).wait_recv()

    def tok_x(zz, xx, part):
        here = part_rows(zz, xx, part)
        return remote(here, here, x_snd.at[zz], x_rcv.at[zz], x_peer)

    def tok_x_end(zz, xx):
        here = tok_rows(zz, xx, 0, keep)
        return remote(here, here, x_snd.at[zz], x_rcv.at[zz], x_peer)

    def send_x(zz, part):
        @pl.when(middle(zz))
        def _():
            tok_x(zz, x, part).start()

        if part == 0:
            @pl.when(jnp.logical_not(middle(zz)))
            def _():
                tok_x_end(zz, x).start()

    def tok_half(way, to):
        here = tok_rows(last_z if way else 0, 1 - x, keep, rows - keep)
        return remote(here, here, g_snd.at[way], g_rcv.at[way], to)

    def from_origin(way):
        return last_z - z if way else z

    near_way = jnp.where(2 * z < nz, 0, 1)

    def absorb(link, zz, xx):
        first_resid(link).wait_recv()
        first_attended(link).wait_recv()
        tok_rows(zz, xx, 0, early)[...] = normed_of(res_in[link], att_in[link])[1]

    def hop(h, part, way):
        step = 1 - 2 * way
        source = z - step * (h + 1)

        @pl.when(inside(source))
        def _():
            if True:
                if h > 0:
                    tok_z_arrived(way, h, part)
                elif part == 0:
                    absorb(way, source, x)
                else:
                    first_normed(way, (source, x)).wait_recv()
                if h < nz - 2:
                    @pl.when(inside(z + step))
                    def _():
                        tok_z(way, h + 1, part).start()

                send_x(source, part)

    def pair_of(j):
        return z + ((j + 1) // 2) * (1 - 2 * (j % 2))

    def both_rows(zz):
        return pl.ds(pl.multiple_of(zz * 2 * rows, 2 * rows), 2 * rows)

    def make_gate(zz):
        here = both_rows(zz)
        gates[here, :] = jnp.dot(tok[here, :], wg[...], preferred_element_type=F32)

    def other_x_arrived(zz):
        if True:
            @pl.when(middle(zz))
            def _():
                whole = tok_rows(zz, 1 - x)
                remote(whole, whole, x_snd.at[zz], x_rcv.at[zz], x_peer).wait_recv()

            @pl.when(jnp.logical_not(middle(zz)))
            def _():
                tok_x_end(zz, 1 - x).wait_recv()

    def gate_step(j, carry):
        zz = pair_of(j)

        @pl.when(inside(zz))
        def _():
            @pl.when(j > 0)
            def _():
                other_x_arrived(zz)

            make_gate(zz)

        return carry

    relays = [(k, s) for k in range(2) for s in range(pieces_w)]

    def relay_to(n):
        while relays and n > 0:
            k, s = relays.pop(0)
            relay_weight(k, s)
            n -= 1

    def halves(h):
        for way in range(2):
            @pl.when(from_origin(way) == h + 1)
            def _():
                if True:
                    tok_half(way, x_peer).wait_recv()

                @pl.when(inside(z + 1 - 2 * way))
                def _():
                    tok_half(way, z_device(z + 1 - 2 * way)).start()

    for h in range(nz - 1):
        for part in range(2):
            hop(h, part, 1 - near_way)
            hop(h, part, near_way)
        if h == 0:
            if True:
                absorb(2, z, 1 - x)
                first_normed(2, (z, 1 - x)).wait_recv()
                for way in range(2):
                    @pl.when(from_origin(way) == 0)
                    def _():
                        tok_half(way, z_device(z + 1 - 2 * way)).start()
            relay_to((pieces_w + 1) // 2)
        elif h == 1:
            if True:
                relay_to(pieces_w - (pieces_w + 1) // 2)
                weight_ready(0)
            if True:
                lax.fori_loop(0, 3, gate_step, 0)
            relay_to(1)
        else:
            relay_to(1)
            if True:
                lax.fori_loop(2 * h - 1, 2 * h + 1, gate_step, 0)
        halves(h)
    if True:
        relay_to(len(relays))

        @pl.when(jnp.logical_not(middle(z)))
        def _():
            zz = last_z - z
            other_x_arrived(zz)
            make_gate(zz)

        weight_ready(1)

    def columns_of(chip):
        return lax.rem(i // 2 + chips - chip, chips)

    def end_way(zz):
        return jnp.where(zz == last_z, 0, 1)

    def sum_x(p, zz, part):
        there = pl.ds(part * keep, rows - keep if part else keep)
        return remote(x_out.at[p, zz, there], x_in.at[p, zz, there], rx_snd.at[part, p],
                      rx_rcv.at[p, zz], x_peer)

    def sum_x_whole(p, zz):
        return remote(x_out.at[p, zz], x_in.at[p, zz], rx_snd.at[0, p], rx_rcv.at[p, zz], x_peer)

    def sum_z(p, way, zz, here=False):
        step = jnp.where(inside(z + 1 - 2 * way), 1 - 2 * way, 0)
        off = 0 if here else step
        return remote(z_out.at[p, zz], z_in.at[p, way, zz], rz_snd.at[p],
                      rz_rcv.at[p, jnp.where(jnp.logical_and(way == 1, zz == z + off), nz, zz)],
                      z_device(z + step))

    def sum_half(p, way, to):
        return remote(h_out.at[p, way], h_in.at[p, way], rh_snd.at[p, way], rh_rcv.at[p, way], to)

    def next_z(way):
        return z_device(jnp.clip(z + 1 - 2 * way, 0, last_z))

    def down(chip, cs, zz):
        def half(xx):
            return hidden[pl.ds(pl.multiple_of((zz * 2 + xx) * rows, rows), rows), :]

        both = jnp.concatenate([half(1 - x), half(x)], axis=0)
        for c in cs:
            p = chip * cuts + c
            for q in range(2):
                part = jnp.dot(both, wd[2 * columns_of(chip) + q, c], preferred_element_type=F32)
                here = slice(q * cw, (q + 1) * cw)
                x_out[p, zz, :, here] = part[:rows].astype(BF16)
                own_part[p, zz, :, here] = part[rows:]
                h_own[p, jnp.where(middle(zz), 2, end_way(zz)), :, here] = part[keep:rows]

    def send_sums(p, zz):
        sum_x(p, zz, 0).start()

        @pl.when(middle(zz))
        def _():
            sum_x(p, zz, 1).start()

    def send_halves(ps, zz):
        for way in range(2):
            @pl.when(jnp.logical_and(from_origin(way) == 0, zz == (0 if way else last_z)))
            def _():
                for p in ps:
                    h_out[p, way] = h_own[p, way].astype(BF16)
                    sum_half(p, way, next_z(way)).start()

    turns = 2 * nz - 1

    def owner(j):
        way = j % 2
        return way, z + (nz - 1 - j // 2) * (1 - 2 * way)

    def finish_half(p, way):
        sum_half(p, way, x_peer).wait_recv()
        h_out[p, way] = (h_own[p, way] + h_in[p, way].astype(F32)).astype(BF16)
        sum_half(p, way, next_z(way)).start()

    def relay_half(p, way):
        @pl.when(middle(z))
        def _():
            if True:
                finish_half(p, way)

    def own_half(p):
        for way in range(2):
            @pl.when(z == (0 if way else last_z))
            def _():
                sum_half(p, way, x_peer).wait_recv()
                x_out[p, z, keep:, :] = (h_own[p, way] + h_in[p, way].astype(F32)).astype(BF16)
                sum_x(p, z, 1).start()

    def finish(p, way, zz):
        more = inside(z - (1 - 2 * way))

        @pl.when(inside(zz))
        def _():
            if True:
                @pl.when(middle(zz))
                def _():
                    sum_x_whole(p, zz).wait_recv()

                @pl.when(jnp.logical_not(middle(zz)))
                def _():
                    sum_x(p, zz, 0).wait_recv()

            @pl.when(more)
            def _():
                if True:
                    sum_z(p, way, zz, True).wait_recv()
                z_out[p, zz] = (
                    own_part[p, zz] + x_in[p, zz].astype(F32) + z_in[p, way, zz].astype(F32)
                ).astype(BF16)

            @pl.when(jnp.logical_not(more))
            def _():
                z_out[p, zz] = (own_part[p, zz] + x_in[p, zz].astype(F32)).astype(BF16)

            sum_z(p, way, zz).start()

    near_ready(2)
    lag = turns - 2

    def hidden_step(j, carry):
        _, zz = owner(j)

        @pl.when(jnp.logical_and(j >= lag, jnp.logical_not(middle(z))))
        def _():
            for p in range(cuts):
                finish(p, *owner(j - lag))

        @pl.when(inside(zz))
        def _():
            here = both_rows(zz)
            gate = gates[here, :]
            upward = jnp.dot(tok[here, :], wu[...], preferred_element_type=F32)
            hidden[here, :] = (gate / (1.0 + jnp.exp(-gate)) * upward).astype(BF16)
            down(0, range(cuts), zz)

            @pl.when(j < turns - 1)
            def _():
                for p in range(cuts):
                    send_sums(p, zz)
                send_halves(range(cuts), zz)

        return carry

    if True:
        lax.fori_loop(0, turns, hidden_step, 0)

    near_end = jnp.where(near_way == 0, last_z, 0)

    def finish_end(p):
        if True:
            relay_half(p, near_way)
            finish(p, near_way, near_end)

    def finish_way(p, way, skip):
        def step(n, carry):
            zz = z + (nz - 1 - n) * (1 - 2 * way)

            @pl.when(zz != skip)
            def _():
                finish(p, way, zz)

            return carry

        lax.fori_loop(0, nz - 1, step, 0)

    def finish_middle(ps):
        for p in ps:
            if True:
                relay_half(p, 1 - near_way)
                finish_way(p, 1 - near_way, -1)
            if True:
                finish_way(p, near_way, near_end)

    def finish_outer(ps, start):
        def step(n, carry):
            if True:
                for p in ps:
                    finish(p, near_way, z + (nz - 1 - n) * (1 - 2 * near_way))
            return carry

        lax.fori_loop(start, nz - 1, step, 0)

    def far_down(s):
        if True:
            far_ready(2, s)

        def step(t, carry):
            chip = 1 + t // turns
            j = t % turns
            _, zz = owner(j)

            @pl.when(inside(zz))
            def _():
                down(chip, (s,), zz)

                @pl.when(j < turns - 1)
                def _():
                    send_sums(chip * cuts + s, zz)
                    send_halves((chip * cuts + s,), zz)

            return carry

        if True:
            lax.fori_loop(0, (chips - 1) * turns, step, 0)

    def own_sums(ps):
        for p in ps:
            sum_x(p, z, 0).start()

            @pl.when(middle(z))
            def _():
                sum_x(p, z, 1).start()

    @pl.when(middle(z))
    def _():
        own_sums(range(cuts))
        for p in range(cuts):
            finish_end(p)
        relay_weight(2, 0)
        finish_middle((0,))

    @pl.when(jnp.logical_not(middle(z)))
    def _():
        relay_weight(2, 0)
        finish(0, near_way, z + (nz - 2) * (1 - 2 * near_way))

    rest = [c * cuts + s for s in range(cuts) for c in range(1, chips)]

    def drain_first():
        for d in steps:
            kv_send(0, d).wait_send()
        for d in range(chips):
            kv_relay(0, d).wait_send()

        @pl.when(o < n_out - 1)
        def _():
            for d in range(chips):
                kv_send(1, d).wait_send()

        @pl.when(o > 0)
        def _():
            for d in range(chips):
                kv_relay(1, d).wait_send()

        for link in range(3):
            def sent(link=link):
                first_attended(link).wait_send()
                whole = tok_rows(z, x)
                remote(whole, whole, r_snd.at[link], r_rcv.at[link], target(link)).wait_send()

            send_link(link, sent)
        for way in range(2):
            step = 1 - 2 * way

            @pl.when(inside(z + step))
            def _():
                tok_half(way, x_peer).wait_send()
                for h in range(1, nz - 1):
                    @pl.when(inside(z - step * h))
                    def _():
                        whole = tok_rows(z, x)
                        remote(whole, whole, z_snd.at[way, h - 1], z_rcv.at[0, way, h - 1], x_peer).wait_send()
        for zz in range(nz):
            @pl.when(z != zz)
            def _():
                if zz == 0 or zz == last_z:
                    tok_x_end(zz, x).wait_send()
                else:
                    whole = tok_rows(zz, x)
                    remote(whole, whole, x_snd.at[zz], x_rcv.at[zz], x_peer).wait_send()

    def drain_sums(p):
        for way in range(2):
            @pl.when(inside(z + 1 - 2 * way))
            def _():
                sum_half(p, way, x_peer).wait_send()
        first = x_out.at[p, :, pl.ds(0, keep)]
        remote(first, first, rx_snd.at[0, p], rx_rcv.at[p, 0], x_peer).wait_send()

        def second(n):
            there = x_out.at[p, pl.ds(0, n), pl.ds(keep, rows - keep)]
            remote(there, there, rx_snd.at[1, p], rx_rcv.at[p, 0], x_peer).wait_send()

        pl.when(middle(z))(lambda: second(nz - 2))
        pl.when(jnp.logical_not(middle(z)))(lambda: second(nz - 1))
        others = z_out.at[p, pl.ds(0, nz - 1)]
        remote(others, others, rz_snd.at[p], rz_rcv.at[p, 0], x_peer).wait_send()

    if True:
        drain_first()
    for s in range(cuts):
        far_down(s)
        if s == 0:
            @pl.when(middle(z))
            def _():
                finish_middle(range(1, cuts))

            @pl.when(jnp.logical_not(middle(z)))
            def _():
                for p in range(1, cuts):
                    finish(p, near_way, z + (nz - 2) * (1 - 2 * near_way))
                finish_outer(range(cuts), 2)

        if s < cuts - 1:
            relay_weight(2, s + 1)
        else:
            @pl.when(middle(z))
            def _():
                own_sums(range(cuts, parts_n))

            @pl.when(jnp.logical_not(middle(z)))
            def _():
                own_sums(range(parts_n))
        for c in range(1, chips):
            finish_end(c * cuts + s)
    if True:
        for k in range(3):
            drain_weights(k)

    @pl.when(middle(z))
    def _():
        finish_middle(rest)

    @pl.when(jnp.logical_not(middle(z)))
    def _():
        finish_outer(rest, 1)

    if True:
        for p in range(parts_n):
            own_half(p)
    for p in range(parts_n):
        if True:
            for way in range(2):
                @pl.when(inside(z - (1 - 2 * way)))
                def _():
                    sum_z(p, way, z, True).wait_recv()
                    own_part[p, z] = own_part[p, z] + z_in[p, way, z].astype(F32)
            sum_x_whole(p, z).wait_recv()
            for q in range(2):
                source = 2 * columns_of(p // cuts) + q
                here = pl.ds(pl.multiple_of(source * width + (p % cuts) * cw, cw), cw)
                cols = slice(q * cw, (q + 1) * cw)
                out_ref[:, here] = (
                    after[:, here].astype(F32)
                    + (own_part[p, z, :, cols] + x_in[p, z, :, cols].astype(F32))).astype(BF16)
        if p < parts_n - 1:
            drain_sums(p)

    drain_sums(parts_n - 1)


def per_device(n_out, n_in, resid, queries, keyvals, piece_order, out_proj, mlp_gain, w_gate, w_up, w_down):
    rows, model = resid.shape
    units, width = w_down.shape
    nz, chips = n_out // 2, n_in // 2
    cuts = max(1, width // 256)
    pieces_w = max(1, 16 // n_in)
    cw = width // cuts
    parts_n = chips * cuts
    early = rows * 3 // 4
    dma = pltpu.SemaphoreType.DMA
    vmem = pl.BlockSpec(memory_space=pltpu.VMEM)
    hbm = pl.BlockSpec(memory_space=pl.ANY)
    spl = max(cuts, pieces_w)
    half = rows - rows // 2
    return pl.pallas_call(
        functools.partial(layer_kernel, n_out, n_in, cuts, pieces_w, early),
        out_shape=pltpu.VMEM(resid.shape, BF16),
        in_specs=[pl.BlockSpec(memory_space=pltpu.SMEM)] + [hbm] * 8,
        out_specs=vmem,
        scratch_shapes=[
            pltpu.VMEM(resid.shape, BF16),
            pltpu.VMEM(queries.shape, BF16),
            pltpu.VMEM(out_proj.shape, BF16),
            pltpu.VMEM((1, model), F32),
            dma((4,)),
            pltpu.VMEM((2 * n_in * rows, keyvals.shape[1]), BF16),
            pltpu.VMEM((model, units), BF16),
            pltpu.VMEM((model, units), BF16),
            pltpu.VMEM((n_in, cuts, units, cw), BF16),
            pltpu.VMEM((n_out * rows, model), BF16),
            pltpu.VMEM((rows, model), BF16),
            pltpu.VMEM(queries.shape, BF16),
            pltpu.VMEM((3, early, model), BF16),
            pltpu.VMEM((3, early, queries.shape[1]), BF16),
            pltpu.VMEM((n_out * rows, units), F32),
            pltpu.VMEM((n_out * rows, units), BF16),
            pltpu.VMEM((parts_n, nz, rows, 2 * cw), BF16),
            pltpu.VMEM((parts_n, nz, rows, 2 * cw), BF16),
            pltpu.VMEM((parts_n, nz, rows, 2 * cw), F32),
            pltpu.VMEM((parts_n, nz, rows, 2 * cw), BF16),
            pltpu.VMEM((parts_n, 2, nz, rows, 2 * cw), BF16),
            pltpu.VMEM((parts_n, 3, half, 2 * cw), F32),
            pltpu.VMEM((parts_n, 2, half, 2 * cw), BF16),
            pltpu.VMEM((parts_n, 2, half, 2 * cw), BF16),
            dma(()), dma((2, chips)), dma((2, chips)), dma((2, n_in)),
            dma((3,)), dma((3,)), dma((3,)), dma((3, chips)), dma((3, chips)),
            dma((3, max(chips - 1, 1), 2, spl)),
            dma((3,)), dma((3,)), dma((3,)), dma((3,)), dma((3,)),
            dma((2, nz - 2)), dma((2, 2, nz - 2)), dma((2,)), dma((2,)), dma((nz,)), dma((nz,)),
            dma((2, parts_n)), dma((parts_n, nz)), dma((parts_n,)), dma((parts_n, nz + 1)),
            dma((parts_n, 2)), dma((parts_n, 2)),
        ],
        compiler_params=pltpu.CompilerParams(
            collective_id=0, has_side_effects=True, vmem_limit_bytes=63000 * 1024
        ),
        name="layer",
    )(piece_order, resid, queries, keyvals, out_proj, mlp_gain.reshape(1, -1), w_gate, w_up, w_down)


def solution(mesh):
    placed = (
        P(("outer", "inner"), None),
        P(("outer", "inner"), None),
        P(("outer", "inner"), None),
        P(),
        P(),
        P(),
        P("inner", "outer"),
        P("inner", "outer"),
        P("outer", "inner"),
    )
    return jax.shard_map(
        functools.partial(per_device, mesh.shape["outer"], mesh.shape["inner"]),
        mesh=mesh,
        in_specs=placed,
        out_specs=P(("outer", "inner"), None),
        check_vma=False,
    )
```

```python
import functools

import jax
import jax.numpy as jnp
from jax import lax
from jax.experimental import pallas as pl
from jax.experimental.pallas import tpu as pltpu
from jax.sharding import PartitionSpec as P

MESH = pl.DeviceIdType.MESH
F32 = jnp.float32
BF16 = jnp.bfloat16
EPS = 1e-05
KEEP = 80


def layer_kernel(
    n_out, n_in, cuts, pieces_w, early, keep,
    order_hbm, resid_hbm, query_hbm, kv_ref, proj_hbm, gain_hbm, wg_ref, wu_ref, wd_ref,
    out_ref,
    order_ref, resid_ref, query_ref, proj_ref, gain_ref, in_sem,
    kv_all, wg, wu, wd, tok, after, att_own, res_in, att_in, gates, upper, hidden,
    x_out, x_in, own_part, z_out, z_in, h_own, h_out, h_in,
    kv_loc, kv_snd, kv_relay_snd, kv_rcv, w_loc, w_pair_snd, w_pair_rcv, w_snd, w_relay_snd, w_rcv,
    r_snd, r_rcv, a_snd, a_rcv, n_rcv, z_snd, z_rcv, g_snd, g_rcv, x_snd, x_rcv,
    rx_snd, rx_rcv, rz_snd, rz_rcv, rh_snd, rh_rcv,
):
    o = lax.axis_index("outer")
    i = lax.axis_index("inner")
    nz = n_out // 2
    z, x = o // 2, o % 2
    core = i % 2
    partner = i + 1 - 2 * core
    x_peer = (z * 2 + 1 - x, i)
    core_peer = (o, partner)
    rows = resid_hbm.shape[0]
    head = kv_ref.shape[1] // 2
    heads = query_ref.shape[1] // head
    pieces = order_ref.shape[0]
    block = n_in * rows
    span = block // pieces
    depth = wg_ref.shape[0]
    units, width = wd_ref.shape
    chips = n_in // 2
    parts_n = chips * cuts
    cw = width // cuts
    keep_t = rows // 2
    last_z = nz - 1

    def remote(src, dst, ssem, rsem, device):
        return pltpu.make_async_remote_copy(
            src_ref=src, dst_ref=dst, send_sem=ssem, recv_sem=rsem,
            device_id=device, device_id_type=MESH,
        )

    def inside(zz):
        return jnp.logical_and(zz >= 0, zz < nz)

    def middle(zz):
        return jnp.logical_and(zz > 0, zz < last_z)

    def z_device(zz):
        return (zz * 2 + x, i)

    barrier = pltpu.get_barrier_semaphore()
    after_o, before_o = lax.rem(o + 1, n_out), lax.rem(o + n_out - 1, n_out)

    def greet(device):
        pl.semaphore_signal(barrier, inc=1, device_id=device, device_id_type=MESH)

    for d in range(1, n_in):
        greet((o, lax.rem(i + d, n_in)))
    greet(x_peer)
    pl.when(z > 0)(lambda: greet(z_device(z - 1)))
    pl.when(z < last_z)(lambda: greet(z_device(z + 1)))

    @pl.when(o > 0)
    def _():
        for d in range(chips):
            greet((before_o, lax.rem(i + 2 * d, n_in)))

    loads = [
        pltpu.make_async_copy(src, dst, in_sem.at[n])
        for n, (src, dst) in enumerate((
            (order_hbm, order_ref), (query_hbm, query_ref), (resid_hbm, resid_ref), (proj_hbm, proj_ref), (gain_hbm, gain_ref)))
    ]
    for load in loads:
        load.start()

    pl.semaphore_wait(
        barrier, n_in + jnp.where(z > 0, 1, 0) + jnp.where(z < last_z, 1, 0)
        + jnp.where(o < n_out - 1, chips, 0))

    own_rows = pl.ds(pl.multiple_of(i * rows, rows), rows)
    kv_copy = pltpu.make_async_copy(kv_ref, kv_all.at[own_rows], kv_loc)
    kv_copy.start()

    steps = range(1, chips)

    def kv_slot(part, q):
        return kv_all.at[pl.ds(pl.multiple_of(part * block + q * rows, rows), rows)]

    def kv_send(part, d):
        return remote(kv_ref, kv_slot(part, i), kv_snd.at[part, d], kv_rcv.at[part, i],
                      (after_o if part else o, lax.rem(i + 2 * d, n_in)))

    def kv_relay(part, d):
        q = lax.rem(i + n_in - 2 * d, n_in)
        src = kv_ref if part == 0 and d == 0 else kv_slot(part, q)
        return remote(src, kv_slot(part, q), kv_relay_snd.at[part, d], kv_rcv.at[part, q], core_peer)

    def kv_arrived(part, q):
        here = kv_slot(part, q)
        remote(here, here, kv_relay_snd.at[part, 0], kv_rcv.at[part, q], core_peer).wait_recv()

    for d in steps:
        kv_send(0, d).start()

    @pl.when(o < n_out - 1)
    def _():
        for d in range(chips):
            kv_send(1, d).start()

    kv_relay(0, 0).start()

    def tok_rows(zz, xx, start=0, size=rows):
        return tok.at[pl.ds(pl.multiple_of((zz * 2 + xx) * rows + start, 16), size)]

    def target(link):
        if isinstance(link, int):
            return x_peer if link == 2 else z_device(z + 1 - 2 * link)
        return z_device(z + 1 - 2 * link)

    def first_resid(link):
        return remote(resid_hbm.at[pl.ds(0, early)], res_in.at[link], r_snd.at[link], r_rcv.at[link],
                      target(link))

    def first_attended(link):
        return remote(att_own.at[pl.ds(0, early)], att_in.at[link], a_snd.at[link], a_rcv.at[link],
                      target(link))

    def first_normed(link, source=None):
        here = tok_rows(*(source or (z, x)), early, rows - early)
        return remote(here, here, r_snd.at[link], n_rcv.at[link], target(link))

    def send_link(link, act):
        if link == 2:
            act()
        else:
            pl.when(inside(z + 1 - 2 * link))(act)

    for link in range(3):
        send_link(link, lambda link=link: first_resid(link).start())

    def slot(k, q, s):
        if k == 2:
            return wd.at[q, s]
        full = wg if k == 0 else wu
        size = depth // pieces_w
        return full.at[pl.ds(pl.multiple_of(q * depth + s * size, size), size)]

    srcs = (wg_ref, wu_ref, wd_ref)

    def w_src(k, s):
        if k == 2:
            return wd_ref.at[:, pl.ds(s * cw, cw)]
        size = depth // pieces_w
        return srcs[k].at[pl.ds(s * size, size)]

    def w_parts(k):
        return cuts if k == 2 else pieces_w

    def shard(k, q):
        if k == 2:
            return wd.at[q]
        full = wg if k == 0 else wu
        return full.at[pl.ds(pl.multiple_of(q * depth, depth), depth)]

    def far(d):
        return lax.rem(i + n_in - 2 * d, n_in)

    def w_far(k, d, s):
        return remote(w_src(k, s), slot(k, i, s), w_snd.at[k, d], w_rcv.at[k, d - 1, 0, s],
                      (o, lax.rem(i + 2 * d, n_in)))

    def w_relay(k, d, s):
        here = slot(k, far(d), s)
        return remote(here, here, w_relay_snd.at[k, d], w_rcv.at[k, d - 1, 1, s], core_peer)

    def w_pair(k, s):
        return remote(w_src(k, s), slot(k, i, s), w_pair_snd.at[k], w_pair_rcv.at[k], core_peer)

    def w_local(k, s):
        return pltpu.make_async_copy(w_src(k, s), slot(k, i, s), w_loc.at[k])

    def near_ready(k):
        mine, other = shard(k, i), shard(k, partner)
        pltpu.make_async_copy(mine, mine, w_loc.at[k]).wait()
        remote(other, other, w_pair_snd.at[k], w_pair_rcv.at[k], core_peer).wait_recv()

    def far_ready(k, s):
        for d in steps:
            here = slot(k, lax.rem(partner + n_in - 2 * d, n_in), s)
            remote(here, here, w_relay_snd.at[k, d], w_rcv.at[k, d - 1, 1, s], core_peer).wait_recv()

    def relay_weight(k, s):
        for d in steps:
            here = slot(k, far(d), s)
            remote(here, here, w_relay_snd.at[k, d], w_rcv.at[k, d - 1, 0, s], core_peer).wait_recv()
            w_relay(k, d, s).start()

    def weight_ready(k):
        near_ready(k)
        for s in range(w_parts(k)):
            far_ready(k, s)

    def drain_weights(k):
        mine = shard(k, i)
        remote(mine, mine, w_pair_snd.at[k], w_pair_rcv.at[k], core_peer).wait_send()
        for d in steps:
            remote(mine, mine, w_snd.at[k, d], w_pair_rcv.at[k], core_peer).wait_send()
            remote(mine, mine, w_relay_snd.at[k, d], w_pair_rcv.at[k], core_peer).wait_send()

    for k in range(3):
        for s in range(w_parts(k)):
            for d in steps:
                w_far(k, d, s).start()
    for k in range(3):
        for s in range(w_parts(k)):
            w_pair(k, s).start()
            w_local(k, s).start()

    loads[0].wait()
    lane = lax.broadcasted_iota(jnp.int32, (rows, block), 1)
    key_pos = jnp.zeros((rows, block), jnp.int32)
    for p in range(pieces):
        key_pos = jnp.where(lane // span == p, order_ref[p] * span + lane % span, key_pos)
    row = lax.broadcasted_iota(jnp.int32, (rows, block), 0)
    query_pos = jnp.zeros((rows, block), jnp.int32)
    for p in range(rows // span):
        query_pos = jnp.where(
            row // span == p, order_ref[i * (rows // span) + p] * span + row % span, query_pos)
    own_visible = key_pos <= query_pos
    before_visible = (jnp.zeros((rows, block), jnp.int32) + o) > 0

    @pl.when(o == 0)
    def _():
        kv_all[block:, :] = jnp.zeros((block, 2 * head), BF16)

    for zz in (0, last_z):
        @pl.when(z != zz)
        def _():
            x_in[:, zz, keep:, :] = jnp.zeros((parts_n, rows - keep, 2 * cw), BF16)

    for d in steps:
        kv_arrived(0, lax.rem(i + n_in - 2 * d, n_in))
        kv_relay(0, d).start()

    @pl.when(o > 0)
    def _():
        for d in range(chips):
            kv_arrived(1, lax.rem(i + n_in - 2 * d, n_in))
            kv_relay(1, d).start()

    kv_copy.wait()
    for d in range(chips):
        kv_arrived(0, lax.rem(partner + 2 * d, n_in))

    @pl.when(o > 0)
    def _():
        for d in range(chips):
            kv_arrived(1, lax.rem(partner + 2 * d, n_in))

    loads[1].wait()
    parts = []
    nt = (((1,), (1,)), ((), ()))
    for h in range(heads):
        query = query_ref[:, h * head:(h + 1) * head]
        own_score = lax.dot_general(
            query, kv_all[:block, :head], nt, preferred_element_type=F32) * head ** (-0.5)
        before_score = lax.dot_general(
            query, kv_all[block:, :head], nt, preferred_element_type=F32) * head ** (-0.5)
        own_score = jnp.where(own_visible, own_score, -1e30)
        before_score = jnp.where(before_visible, before_score, -1e30)
        top = jnp.maximum(
            jnp.max(own_score, axis=1, keepdims=True), jnp.max(before_score, axis=1, keepdims=True))
        own_w = jnp.where(own_visible, jnp.exp(own_score - top), 0.0)
        before_w = jnp.where(before_visible, jnp.exp(before_score - top), 0.0)
        total = jnp.sum(own_w, axis=1, keepdims=True) + jnp.sum(before_w, axis=1, keepdims=True)
        mixed = jnp.dot(own_w.astype(BF16), kv_all[:block, head:], preferred_element_type=F32)
        mixed += jnp.dot(before_w.astype(BF16), kv_all[block:, head:], preferred_element_type=F32)
        parts.append((mixed / total).astype(BF16))
    att_own[...] = jnp.concatenate(parts, axis=1)
    for link in range(3):
        send_link(link, lambda link=link: first_attended(link).start())

    for load in loads[2:]:
        load.wait()

    def normed_of(resid, attended):
        after_attn = (
            resid.astype(F32) + jnp.dot(attended, proj_ref[...], preferred_element_type=F32)
        ).astype(BF16)
        wide = after_attn.astype(F32)
        normed = wide * lax.rsqrt(jnp.mean(wide * wide, axis=1, keepdims=True) + EPS) * gain_ref[...]
        return after_attn, normed.astype(BF16)

    after_attn, normed = normed_of(resid_ref[...], att_own[...])
    after[...] = after_attn
    tok_rows(z, x)[...] = normed
    for link in range(3):
        send_link(link, lambda link=link: first_normed(link).start())

    def part_rows(zz, xx, part):
        return tok_rows(zz, xx, part * early, rows - early if part else early)

    def tok_z(way, h, part):
        step = 1 - 2 * way
        here = part_rows(z - step * h, x, part)
        return remote(here, here, z_snd.at[way, h - 1], z_rcv.at[part, way, h - 1], z_device(z + step))

    def tok_z_arrived(way, h, part):
        here = part_rows(z - (1 - 2 * way) * (h + 1), x, part)
        remote(here, here, z_snd.at[way, h - 1], z_rcv.at[part, way, h - 1], x_peer).wait_recv()

    def tok_x(zz, xx, part):
        here = part_rows(zz, xx, part)
        return remote(here, here, x_snd.at[zz], x_rcv.at[zz], x_peer)

    def tok_x_end(zz, xx):
        here = tok_rows(zz, xx, 0, keep_t)
        return remote(here, here, x_snd.at[zz], x_rcv.at[zz], x_peer)

    def send_x(zz, part):
        @pl.when(middle(zz))
        def _():
            tok_x(zz, x, part).start()

        if part == 0:
            @pl.when(jnp.logical_not(middle(zz)))
            def _():
                tok_x_end(zz, x).start()

    def tok_half(way, to):
        here = tok_rows(last_z if way else 0, 1 - x, keep_t, rows - keep_t)
        return remote(here, here, g_snd.at[way], g_rcv.at[way], to)

    def from_origin(way):
        return last_z - z if way else z

    near_way = jnp.where(2 * z < nz, 0, 1)

    def absorb(link, zz, xx):
        first_resid(link).wait_recv()
        first_attended(link).wait_recv()
        tok_rows(zz, xx, 0, early)[...] = normed_of(res_in[link], att_in[link])[1]

    def hop(h, part, way):
        step = 1 - 2 * way
        source = z - step * (h + 1)

        @pl.when(inside(source))
        def _():
            if h > 0:
                tok_z_arrived(way, h, part)
            elif part == 0:
                absorb(way, source, x)
            else:
                first_normed(way, (source, x)).wait_recv()
            if h < nz - 2:
                @pl.when(inside(z + step))
                def _():
                    tok_z(way, h + 1, part).start()

            send_x(source, part)

    def pair_of(j):
        return z + ((j + 1) // 2) * (1 - 2 * (j % 2))

    def both_rows(zz):
        return pl.ds(pl.multiple_of(zz * 2 * rows, 2 * rows), 2 * rows)

    def make_gate(zz):
        here = both_rows(zz)
        gates[here, :] = jnp.dot(tok[here, :], wg[...], preferred_element_type=F32)

    def other_x_arrived(zz):
        @pl.when(middle(zz))
        def _():
            whole = tok_rows(zz, 1 - x)
            remote(whole, whole, x_snd.at[zz], x_rcv.at[zz], x_peer).wait_recv()

        @pl.when(jnp.logical_not(middle(zz)))
        def _():
            tok_x_end(zz, 1 - x).wait_recv()

    def gate_step(j, carry):
        zz = pair_of(j)

        @pl.when(inside(zz))
        def _():
            @pl.when(j > 0)
            def _():
                other_x_arrived(zz)

            make_gate(zz)

        return carry

    relays = [(k, s) for k in range(2) for s in range(pieces_w)]

    def relay_to(n):
        while relays and n > 0:
            k, s = relays.pop(0)
            relay_weight(k, s)
            n -= 1

    def halves(h):
        for way in range(2):
            @pl.when(from_origin(way) == h + 1)
            def _():
                tok_half(way, x_peer).wait_recv()

                @pl.when(inside(z + 1 - 2 * way))
                def _():
                    tok_half(way, z_device(z + 1 - 2 * way)).start()

    for h in range(nz - 1):
        for part in range(2):
            hop(h, part, 1 - near_way)
            hop(h, part, near_way)
        if h == 0:
            absorb(2, z, 1 - x)
            first_normed(2, (z, 1 - x)).wait_recv()
            for way in range(2):
                @pl.when(from_origin(way) == 0)
                def _():
                    tok_half(way, z_device(z + 1 - 2 * way)).start()
            relay_to((pieces_w + 1) // 2)
        elif h == 1:
            relay_to(pieces_w - (pieces_w + 1) // 2)
            weight_ready(0)
            lax.fori_loop(0, 3, gate_step, 0)
            relay_to(1)
        else:
            relay_to(1)
            lax.fori_loop(2 * h - 1, 2 * h + 1, gate_step, 0)
        halves(h)
    relay_to(len(relays))
    near_ready(1)
    for s in range(pieces_w - 1):
        far_ready(1, s)

    def columns_of(chip):
        return lax.rem(i // 2 + chips - chip, chips)

    def end_way(zz):
        return jnp.where(zz == last_z, 0, 1)

    def sum_x(p, zz, part):
        there = pl.ds(part * keep, rows - keep if part else keep)
        return remote(x_out.at[p, zz, there], x_in.at[p, zz, there], rx_snd.at[part, p],
                      rx_rcv.at[p, zz], x_peer)

    def sum_x_whole(p, zz):
        return remote(x_out.at[p, zz], x_in.at[p, zz], rx_snd.at[0, p], rx_rcv.at[p, zz], x_peer)

    def sum_z(p, way, zz, here=False):
        step = jnp.where(inside(z + 1 - 2 * way), 1 - 2 * way, 0)
        off = 0 if here else step
        return remote(z_out.at[p, zz], z_in.at[p, way, zz], rz_snd.at[p],
                      rz_rcv.at[p, jnp.where(jnp.logical_and(way == 1, zz == z + off), nz, zz)],
                      z_device(z + step))

    def sum_half(p, way, to):
        return remote(h_out.at[p, way], h_in.at[p, way], rh_snd.at[p, way], rh_rcv.at[p, way], to)

    def next_z(way):
        return z_device(jnp.clip(z + 1 - 2 * way, 0, last_z))

    def down(chip, cs, zz):
        def half(xx):
            return hidden[pl.ds(pl.multiple_of((zz * 2 + xx) * rows, rows), rows), :]

        both = jnp.concatenate([half(1 - x), half(x)], axis=0)
        for c in cs:
            p = chip * cuts + c
            for q in range(2):
                part = jnp.dot(both, wd[2 * columns_of(chip) + q, c], preferred_element_type=F32)
                here = slice(q * cw, (q + 1) * cw)
                x_out[p, zz, :, here] = part[:rows].astype(BF16)
                own_part[p, zz, :, here] = part[rows:]
                h_own[p, jnp.where(middle(zz), 2, end_way(zz)), :, here] = part[keep:rows]

    def send_sums(p, zz):
        sum_x(p, zz, 0).start()

        @pl.when(middle(zz))
        def _():
            sum_x(p, zz, 1).start()

    def send_halves(ps, zz):
        for way in range(2):
            @pl.when(jnp.logical_and(from_origin(way) == 0, zz == (0 if way else last_z)))
            def _():
                for p in ps:
                    h_out[p, way] = h_own[p, way].astype(BF16)
                    sum_half(p, way, next_z(way)).start()

    turns = 2 * nz - 1

    def owner(j):
        way = j % 2
        return way, z + (nz - 1 - j // 2) * (1 - 2 * way)

    def finish_half(p, way):
        sum_half(p, way, x_peer).wait_recv()
        h_out[p, way] = (h_own[p, way] + h_in[p, way].astype(F32)).astype(BF16)
        sum_half(p, way, next_z(way)).start()

    def relay_half(p, way):
        @pl.when(middle(z))
        def _():
            finish_half(p, way)

    def own_half(p):
        for way in range(2):
            @pl.when(z == (0 if way else last_z))
            def _():
                sum_half(p, way, x_peer).wait_recv()
                x_out[p, z, keep:, :] = (h_own[p, way] + h_in[p, way].astype(F32)).astype(BF16)
                sum_x(p, z, 1).start()

    def finish(p, way, zz):
        more = inside(z - (1 - 2 * way))

        @pl.when(inside(zz))
        def _():
            @pl.when(middle(zz))
            def _():
                sum_x_whole(p, zz).wait_recv()

            @pl.when(jnp.logical_not(middle(zz)))
            def _():
                sum_x(p, zz, 0).wait_recv()

            @pl.when(more)
            def _():
                sum_z(p, way, zz, True).wait_recv()
                z_out[p, zz] = (
                    own_part[p, zz] + x_in[p, zz].astype(F32) + z_in[p, way, zz].astype(F32)
                ).astype(BF16)

            @pl.when(jnp.logical_not(more))
            def _():
                z_out[p, zz] = (own_part[p, zz] + x_in[p, zz].astype(F32)).astype(BF16)

            sum_z(p, way, zz).start()

    near_ready(2)
    first_zz = z + (nz - 2) * (1 - 2 * near_way)

    def upward_over(zz, shards):
        total = None
        for q in shards:
            here = pl.ds(pl.multiple_of(q * depth, depth), depth)
            part = jnp.dot(tok[both_rows(zz), here], wu[here, :], preferred_element_type=F32)
            total = part if total is None else total + part
        return total

    def make_hidden(zz, upward):
        here = both_rows(zz)
        gate = gates[here, :]
        hidden[here, :] = (gate / (1.0 + jnp.exp(-gate)) * upward).astype(BF16)

    def first_sums(zz):
        for p in range(cuts):
            down(0, (p,), zz)
            send_sums(p, zz)
            send_halves((p,), zz)

    @pl.when(inside(first_zz))
    def _():
        upper[...] = upward_over(first_zz, [partner] + [lax.rem(i + 2 * d, n_in) for d in range(chips)])

    far_ready(1, pieces_w - 1)

    @pl.when(inside(first_zz))
    def _():
        make_hidden(first_zz, upper[...] + upward_over(
            first_zz, [lax.rem(partner + 2 * d, n_in) for d in range(1, chips)]))
        first_sums(first_zz)

    def hidden_step(j, carry):
        _, zz = owner(j)

        @pl.when(jnp.logical_and(j == 3, jnp.logical_not(middle(z))))
        def _():
            finish(0, near_way, first_zz)

        @pl.when(jnp.logical_and(j == turns - 1, jnp.logical_not(middle(z))))
        def _():
            for p in range(1, cuts):
                finish(p, near_way, first_zz)

        @pl.when(jnp.logical_and(inside(zz), zz != first_zz))
        def _():
            @pl.when(j < 2)
            def _():
                other_x_arrived(zz)
                make_gate(zz)

            make_hidden(zz, jnp.dot(tok[both_rows(zz), :], wu[...], preferred_element_type=F32))

            @pl.when(j < turns - 1)
            def _():
                first_sums(zz)

            @pl.when(j == turns - 1)
            def _():
                down(0, range(cuts), zz)

        return carry

    lax.fori_loop(0, turns, hidden_step, 0)

    near_end = jnp.where(near_way == 0, last_z, 0)

    def finish_end(p):
        relay_half(p, near_way)
        finish(p, near_way, near_end)

    def finish_way(p, way, skip):
        def step(n, carry):
            zz = z + (nz - 1 - n) * (1 - 2 * way)

            @pl.when(zz != skip)
            def _():
                finish(p, way, zz)

            return carry

        lax.fori_loop(0, nz - 1, step, 0)

    def finish_outer(ps, start):
        def step(n, carry):
            for p in ps:
                finish(p, near_way, z + (nz - 1 - n) * (1 - 2 * near_way))
            return carry

        lax.fori_loop(start, nz - 1, step, 0)

    def far_down(s, hold=False):
        far_ready(2, s)

        def step(t, carry):
            chip = 1 + t // turns
            j = t % turns
            _, zz = owner(j)

            @pl.when(inside(zz))
            def _():
                down(chip, (s,), zz)

                @pl.when(j < (turns - 3 if hold else turns - 1))
                def _():
                    send_sums(chip * cuts + s, zz)
                    send_halves((chip * cuts + s,), zz)

            return carry

        lax.fori_loop(0, (chips - 1) * turns, step, 0)

    rest = [c * cuts + s for s in range(cuts) for c in range(1, chips)]

    def own_sums(ps):
        for p in ps:
            sum_x(p, z, 0).start()

            @pl.when(middle(z))
            def _():
                sum_x(p, z, 1).start()

    def drain_first():
        for d in steps:
            kv_send(0, d).wait_send()
        for d in range(chips):
            kv_relay(0, d).wait_send()

        @pl.when(o < n_out - 1)
        def _():
            for d in range(chips):
                kv_send(1, d).wait_send()

        @pl.when(o > 0)
        def _():
            for d in range(chips):
                kv_relay(1, d).wait_send()

        for link in range(3):
            def sent(link=link):
                first_attended(link).wait_send()
                whole = tok_rows(z, x)
                remote(whole, whole, r_snd.at[link], r_rcv.at[link], target(link)).wait_send()

            send_link(link, sent)
        for way in range(2):
            step = 1 - 2 * way

            @pl.when(inside(z + step))
            def _():
                tok_half(way, x_peer).wait_send()
                for h in range(1, nz - 1):
                    @pl.when(inside(z - step * h))
                    def _():
                        whole = tok_rows(z, x)
                        remote(whole, whole, z_snd.at[way, h - 1], z_rcv.at[0, way, h - 1], x_peer).wait_send()
        for zz in range(nz):
            @pl.when(z != zz)
            def _():
                if zz == 0 or zz == last_z:
                    tok_x_end(zz, x).wait_send()
                else:
                    whole = tok_rows(zz, x)
                    remote(whole, whole, x_snd.at[zz], x_rcv.at[zz], x_peer).wait_send()

    def drain_sums(p):
        for way in range(2):
            @pl.when(inside(z + 1 - 2 * way))
            def _():
                sum_half(p, way, x_peer).wait_send()
        first = x_out.at[p, :, pl.ds(0, keep)]
        remote(first, first, rx_snd.at[0, p], rx_rcv.at[p, 0], x_peer).wait_send()

        def second(n):
            there = x_out.at[p, pl.ds(0, n), pl.ds(keep, rows - keep)]
            remote(there, there, rx_snd.at[1, p], rx_rcv.at[p, 0], x_peer).wait_send()

        pl.when(middle(z))(lambda: second(nz - 2))
        pl.when(jnp.logical_not(middle(z)))(lambda: second(nz - 1))
        others = z_out.at[p, pl.ds(0, nz - 1)]
        remote(others, others, rz_snd.at[p], rz_rcv.at[p, 0], x_peer).wait_send()

    @pl.when(middle(z))
    def _():
        own_sums(range(cuts))
        for p in range(cuts):
            relay_half(p, near_way)
        relay_weight(2, 0)
        far_down(0)
        for p in range(cuts):
            relay_half(p, 1 - near_way)
        for p in range(cuts):
            finish_way(p, near_way, near_end)
        for p in range(cuts):
            finish(p, near_way, near_end)
        for s in range(1, cuts):
            relay_weight(2, s)
            far_down(s)
        own_sums(rest)
        for p in range(cuts):
            finish_way(p, 1 - near_way, -1)
        for p in rest:
            finish_end(p)
        for p in rest:
            relay_half(p, 1 - near_way)
        for p in rest:
            finish_way(p, 1 - near_way, -1)
            finish_way(p, near_way, near_end)

    @pl.when(jnp.logical_not(middle(z)))
    def _():
        finish(0, near_way, near_end)
        relay_weight(2, 0)
        for p in range(1, cuts):
            finish(p, near_way, near_end)
        far_down(0, True)
        finish_outer((0,), 2)
        for s in range(1, cuts):
            relay_weight(2, s)
            for c in range(1, chips):
                finish_end(c * cuts + s - 1)
            far_down(s, True)
        for p in rest:
            send_sums(p, z + 1 - 2 * near_way)
        own_sums(range(parts_n))
        for c in range(1, chips):
            finish_end(c * cuts + cuts - 1)
        if cuts > 1:
            finish_outer(range(1, cuts), 2)
        finish_outer(rest, 1)

    drain_first()
    for k in range(3):
        drain_weights(k)
    for p in range(parts_n):
        own_half(p)
    for p in range(parts_n):
        for way in range(2):
            @pl.when(inside(z - (1 - 2 * way)))
            def _():
                sum_z(p, way, z, True).wait_recv()
                own_part[p, z] = own_part[p, z] + z_in[p, way, z].astype(F32)
        sum_x_whole(p, z).wait_recv()
        for q in range(2):
            source = 2 * columns_of(p // cuts) + q
            here = pl.ds(pl.multiple_of(source * width + (p % cuts) * cw, cw), cw)
            cols = slice(q * cw, (q + 1) * cw)
            out_ref[:, here] = (
                after[:, here].astype(F32)
                + (own_part[p, z, :, cols] + x_in[p, z, :, cols].astype(F32))).astype(BF16)
        if p < parts_n - 1:
            drain_sums(p)

    drain_sums(parts_n - 1)


def per_device(n_out, n_in, resid, queries, keyvals, piece_order, out_proj, mlp_gain, w_gate, w_up, w_down):
    rows, model = resid.shape
    units, width = w_down.shape
    nz, chips = n_out // 2, n_in // 2
    cuts = max(1, width // 256)
    pieces_w = max(1, 16 // n_in)
    cw = width // cuts
    parts_n = chips * cuts
    early = rows * 3 // 4
    dma = pltpu.SemaphoreType.DMA
    vmem = pl.BlockSpec(memory_space=pltpu.VMEM)
    hbm = pl.BlockSpec(memory_space=pl.ANY)
    spl = max(cuts, pieces_w)
    keep = rows * KEEP // 128
    half = rows - keep
    return pl.pallas_call(
        functools.partial(layer_kernel, n_out, n_in, cuts, pieces_w, early, keep),
        out_shape=pltpu.VMEM(resid.shape, BF16),
        in_specs=[hbm] * 9,
        out_specs=vmem,
        scratch_shapes=[
            pltpu.SMEM(piece_order.shape, jnp.int32),
            pltpu.VMEM(resid.shape, BF16),
            pltpu.VMEM(queries.shape, BF16),
            pltpu.VMEM(out_proj.shape, BF16),
            pltpu.VMEM((1, model), F32),
            dma((5,)),
            pltpu.VMEM((2 * n_in * rows, keyvals.shape[1]), BF16),
            pltpu.VMEM((model, units), BF16),
            pltpu.VMEM((model, units), BF16),
            pltpu.VMEM((n_in, cuts, units, cw), BF16),
            pltpu.VMEM((n_out * rows, model), BF16),
            pltpu.VMEM((rows, model), BF16),
            pltpu.VMEM(queries.shape, BF16),
            pltpu.VMEM((3, early, model), BF16),
            pltpu.VMEM((3, early, queries.shape[1]), BF16),
            pltpu.VMEM((n_out * rows, units), F32),
            pltpu.VMEM((2 * rows, units), F32),
            pltpu.VMEM((n_out * rows, units), BF16),
            pltpu.VMEM((parts_n, nz, rows, 2 * cw), BF16),
            pltpu.VMEM((parts_n, nz, rows, 2 * cw), BF16),
            pltpu.VMEM((parts_n, nz, rows, 2 * cw), F32),
            pltpu.VMEM((parts_n, nz, rows, 2 * cw), BF16),
            pltpu.VMEM((parts_n, 2, nz, rows, 2 * cw), BF16),
            pltpu.VMEM((parts_n, 3, half, 2 * cw), F32),
            pltpu.VMEM((parts_n, 2, half, 2 * cw), BF16),
            pltpu.VMEM((parts_n, 2, half, 2 * cw), BF16),
            dma(()), dma((2, chips)), dma((2, chips)), dma((2, n_in)),
            dma((3,)), dma((3,)), dma((3,)), dma((3, chips)), dma((3, chips)),
            dma((3, max(chips - 1, 1), 2, spl)),
            dma((3,)), dma((3,)), dma((3,)), dma((3,)), dma((3,)),
            dma((2, nz - 2)), dma((2, 2, nz - 2)), dma((2,)), dma((2,)), dma((nz,)), dma((nz,)),
            dma((2, parts_n)), dma((parts_n, nz)), dma((parts_n,)), dma((parts_n, nz + 1)),
            dma((parts_n, 2)), dma((parts_n, 2)),
        ],
        compiler_params=pltpu.CompilerParams(
            collective_id=0, has_side_effects=True, vmem_limit_bytes=63000 * 1024
        ),
        name="layer",
    )(piece_order, resid, queries, keyvals, out_proj, mlp_gain.reshape(1, -1), w_gate, w_up, w_down)


def solution(mesh):
    placed = (
        P(("outer", "inner"), None),
        P(("outer", "inner"), None),
        P(("outer", "inner"), None),
        P(),
        P(),
        P(),
        P("inner", "outer"),
        P("inner", "outer"),
        P("outer", "inner"),
    )
    return jax.shard_map(
        functools.partial(per_device, mesh.shape["outer"], mesh.shape["inner"]),
        mesh=mesh,
        in_specs=placed,
        out_specs=P(("outer", "inner"), None),
        check_vma=False,
    )
```

```python
import functools

import jax
import jax.numpy as jnp
from jax import lax
from jax.experimental import pallas as pl
from jax.experimental.pallas import tpu as pltpu
from jax.sharding import PartitionSpec as P

MESH = pl.DeviceIdType.MESH
F32 = jnp.float32
BF16 = jnp.bfloat16
EPS = 1e-05
KEEP = 80


def layer_kernel(
    n_out, n_in, cuts, pieces_w, early, keep,
    order_hbm, resid_hbm, query_hbm, kv_ref, proj_hbm, gain_hbm, wg_ref, wu_ref, wd_ref,
    out_ref,
    order_ref, resid_ref, query_ref, proj_ref, gain_ref, in_sem,
    kv_all, wg, wu, wd, tok, after, att_own, res_in, att_in, gates, upper, hidden,
    x_out, x_in, own_part, z_out, z_in, h_own, h_out, h_in,
    kv_loc, kv_snd, kv_relay_snd, kv_rcv, w_loc, w_pair_snd, w_pair_rcv, w_snd, w_relay_snd, w_rcv,
    r_snd, r_rcv, a_snd, a_rcv, n_rcv, z_snd, z_rcv, g_snd, g_rcv, x_snd, x_rcv,
    rx_snd, rx_rcv, rz_snd, rz_rcv, rh_snd, rh_rcv,
):
    o = lax.axis_index("outer")
    i = lax.axis_index("inner")
    nz = n_out // 2
    z, x = o // 2, o % 2
    core = i % 2
    partner = i + 1 - 2 * core
    x_peer = (z * 2 + 1 - x, i)
    core_peer = (o, partner)
    rows = resid_hbm.shape[0]
    head = kv_ref.shape[1] // 2
    heads = query_ref.shape[1] // head
    pieces = order_ref.shape[0]
    block = n_in * rows
    span = block // pieces
    depth = wg_ref.shape[0]
    units, width = wd_ref.shape
    chips = n_in // 2
    parts_n = chips * cuts
    cw = width // cuts
    keep_t = rows // 2
    last_z = nz - 1

    def remote(src, dst, ssem, rsem, device):
        return pltpu.make_async_remote_copy(
            src_ref=src, dst_ref=dst, send_sem=ssem, recv_sem=rsem,
            device_id=device, device_id_type=MESH,
        )

    def inside(zz):
        return jnp.logical_and(zz >= 0, zz < nz)

    def middle(zz):
        return jnp.logical_and(zz > 0, zz < last_z)

    def z_device(zz):
        return (zz * 2 + x, i)

    barrier = pltpu.get_barrier_semaphore()
    after_o, before_o = lax.rem(o + 1, n_out), lax.rem(o + n_out - 1, n_out)

    def greet(device):
        pl.semaphore_signal(barrier, inc=1, device_id=device, device_id_type=MESH)

    for d in range(1, n_in):
        greet((o, lax.rem(i + d, n_in)))
    greet(x_peer)
    pl.when(z > 0)(lambda: greet(z_device(z - 1)))
    pl.when(z < last_z)(lambda: greet(z_device(z + 1)))

    @pl.when(o > 0)
    def _():
        for d in range(chips):
            greet((before_o, lax.rem(i + 2 * d, n_in)))

    loads = [
        pltpu.make_async_copy(src, dst, in_sem.at[n])
        for n, (src, dst) in enumerate((
            (order_hbm, order_ref), (query_hbm, query_ref), (resid_hbm, resid_ref), (proj_hbm, proj_ref), (gain_hbm, gain_ref)))
    ]
    for load in loads:
        load.start()

    pl.semaphore_wait(
        barrier, n_in + jnp.where(z > 0, 1, 0) + jnp.where(z < last_z, 1, 0)
        + jnp.where(o < n_out - 1, chips, 0))

    own_rows = pl.ds(pl.multiple_of(i * rows, rows), rows)
    kv_copy = pltpu.make_async_copy(kv_ref, kv_all.at[own_rows], kv_loc)
    kv_copy.start()

    steps = range(1, chips)

    def kv_slot(part, q):
        return kv_all.at[pl.ds(pl.multiple_of(part * block + q * rows, rows), rows)]

    def kv_send(part, d):
        return remote(kv_ref, kv_slot(part, i), kv_snd.at[part, d], kv_rcv.at[part, i],
                      (after_o if part else o, lax.rem(i + 2 * d, n_in)))

    def kv_relay(part, d):
        q = lax.rem(i + n_in - 2 * d, n_in)
        src = kv_ref if part == 0 and d == 0 else kv_slot(part, q)
        return remote(src, kv_slot(part, q), kv_relay_snd.at[part, d], kv_rcv.at[part, q], core_peer)

    def kv_arrived(part, q):
        here = kv_slot(part, q)
        remote(here, here, kv_relay_snd.at[part, 0], kv_rcv.at[part, q], core_peer).wait_recv()

    for d in steps:
        kv_send(0, d).start()

    @pl.when(o < n_out - 1)
    def _():
        for d in range(chips):
            kv_send(1, d).start()

    kv_relay(0, 0).start()

    def tok_rows(zz, xx, start=0, size=rows):
        return tok.at[pl.ds(pl.multiple_of((zz * 2 + xx) * rows + start, 16), size)]

    def target(link):
        if isinstance(link, int):
            return x_peer if link == 2 else z_device(z + 1 - 2 * link)
        return z_device(z + 1 - 2 * link)

    def first_resid(link):
        return remote(resid_hbm.at[pl.ds(0, early)], res_in.at[link], r_snd.at[link], r_rcv.at[link],
                      target(link))

    def first_attended(link):
        return remote(att_own.at[pl.ds(0, early)], att_in.at[link], a_snd.at[link], a_rcv.at[link],
                      target(link))

    def first_normed(link, source=None):
        here = tok_rows(*(source or (z, x)), early, rows - early)
        return remote(here, here, r_snd.at[link], n_rcv.at[link], target(link))

    def send_link(link, act):
        if link == 2:
            act()
        else:
            pl.when(inside(z + 1 - 2 * link))(act)

    for link in range(3):
        send_link(link, lambda link=link: first_resid(link).start())

    def slot(k, q, s):
        if k == 2:
            return wd.at[q, s]
        full = wg if k == 0 else wu
        size = depth // pieces_w[k]
        return full.at[pl.ds(pl.multiple_of(q * depth + s * size, size), size)]

    srcs = (wg_ref, wu_ref, wd_ref)

    def w_src(k, s):
        if k == 2:
            return wd_ref.at[:, pl.ds(s * cw, cw)]
        size = depth // pieces_w[k]
        return srcs[k].at[pl.ds(s * size, size)]

    def w_parts(k):
        return pieces_w[k]

    def w_index(k, s):
        return sum(pieces_w[:k]) + s

    def shard(k, q):
        if k == 2:
            return wd.at[q]
        full = wg if k == 0 else wu
        return full.at[pl.ds(pl.multiple_of(q * depth, depth), depth)]

    def far(d):
        return lax.rem(i + n_in - 2 * d, n_in)

    def w_far(k, d, s):
        return remote(w_src(k, s), slot(k, i, s), w_snd.at[k, d], w_rcv.at[d - 1, 0, w_index(k, s)],
                      (o, lax.rem(i + 2 * d, n_in)))

    def w_relay(k, d, s):
        here = slot(k, far(d), s)
        return remote(here, here, w_relay_snd.at[k, d], w_rcv.at[d - 1, 1, w_index(k, s)], core_peer)

    def w_pair(k, s):
        return remote(w_src(k, s), slot(k, i, s), w_pair_snd.at[k], w_pair_rcv.at[k], core_peer)

    def w_local(k, s):
        return pltpu.make_async_copy(w_src(k, s), slot(k, i, s), w_loc.at[k])

    def near_ready(k):
        mine, other = shard(k, i), shard(k, partner)
        pltpu.make_async_copy(mine, mine, w_loc.at[k]).wait()
        remote(other, other, w_pair_snd.at[k], w_pair_rcv.at[k], core_peer).wait_recv()

    def far_ready(k, s):
        for d in steps:
            here = slot(k, lax.rem(partner + n_in - 2 * d, n_in), s)
            remote(here, here, w_relay_snd.at[k, d], w_rcv.at[d - 1, 1, w_index(k, s)], core_peer).wait_recv()

    def relay_weight(k, s):
        for d in steps:
            here = slot(k, far(d), s)
            remote(here, here, w_relay_snd.at[k, d], w_rcv.at[d - 1, 0, w_index(k, s)], core_peer).wait_recv()
            w_relay(k, d, s).start()

    def weight_ready(k):
        near_ready(k)
        for s in range(w_parts(k)):
            far_ready(k, s)

    def drain_weights(k):
        mine = shard(k, i)
        remote(mine, mine, w_pair_snd.at[k], w_pair_rcv.at[k], core_peer).wait_send()
        for d in steps:
            remote(mine, mine, w_snd.at[k, d], w_pair_rcv.at[k], core_peer).wait_send()
            remote(mine, mine, w_relay_snd.at[k, d], w_pair_rcv.at[k], core_peer).wait_send()

    for k in range(3):
        for s in range(w_parts(k)):
            for d in steps:
                w_far(k, d, s).start()
    for k in range(3):
        for s in range(w_parts(k)):
            w_pair(k, s).start()
            w_local(k, s).start()

    loads[0].wait()
    lane = lax.broadcasted_iota(jnp.int32, (rows, block), 1)
    key_pos = jnp.zeros((rows, block), jnp.int32)
    for p in range(pieces):
        key_pos = jnp.where(lane // span == p, order_ref[p] * span + lane % span, key_pos)
    row = lax.broadcasted_iota(jnp.int32, (rows, block), 0)
    query_pos = jnp.zeros((rows, block), jnp.int32)
    for p in range(rows // span):
        query_pos = jnp.where(
            row // span == p, order_ref[i * (rows // span) + p] * span + row % span, query_pos)
    own_visible = key_pos <= query_pos
    before_visible = (jnp.zeros((rows, block), jnp.int32) + o) > 0

    @pl.when(o == 0)
    def _():
        kv_all[block:, :] = jnp.zeros((block, 2 * head), BF16)

    for zz in (0, last_z):
        @pl.when(z != zz)
        def _():
            x_in[:, zz, keep:, :] = jnp.zeros((parts_n, rows - keep, 2 * cw), BF16)

    for d in steps:
        kv_arrived(0, lax.rem(i + n_in - 2 * d, n_in))
        kv_relay(0, d).start()

    @pl.when(o > 0)
    def _():
        for d in range(chips):
            kv_arrived(1, lax.rem(i + n_in - 2 * d, n_in))
            kv_relay(1, d).start()

    kv_copy.wait()
    for d in range(chips):
        kv_arrived(0, lax.rem(partner + 2 * d, n_in))

    @pl.when(o > 0)
    def _():
        for d in range(chips):
            kv_arrived(1, lax.rem(partner + 2 * d, n_in))

    loads[1].wait()
    parts = []
    nt = (((1,), (1,)), ((), ()))
    for h in range(heads):
        query = query_ref[:, h * head:(h + 1) * head]
        own_score = lax.dot_general(
            query, kv_all[:block, :head], nt, preferred_element_type=F32) * head ** (-0.5)
        before_score = lax.dot_general(
            query, kv_all[block:, :head], nt, preferred_element_type=F32) * head ** (-0.5)
        own_score = jnp.where(own_visible, own_score, -1e30)
        before_score = jnp.where(before_visible, before_score, -1e30)
        top = jnp.maximum(
            jnp.max(own_score, axis=1, keepdims=True), jnp.max(before_score, axis=1, keepdims=True))
        own_w = jnp.where(own_visible, jnp.exp(own_score - top), 0.0)
        before_w = jnp.where(before_visible, jnp.exp(before_score - top), 0.0)
        total = jnp.sum(own_w, axis=1, keepdims=True) + jnp.sum(before_w, axis=1, keepdims=True)
        mixed = jnp.dot(own_w.astype(BF16), kv_all[:block, head:], preferred_element_type=F32)
        mixed += jnp.dot(before_w.astype(BF16), kv_all[block:, head:], preferred_element_type=F32)
        parts.append((mixed / total).astype(BF16))
    att_own[...] = jnp.concatenate(parts, axis=1)
    for link in range(3):
        send_link(link, lambda link=link: first_attended(link).start())

    for load in loads[2:]:
        load.wait()

    def normed_of(resid, attended):
        after_attn = (
            resid.astype(F32) + jnp.dot(attended, proj_ref[...], preferred_element_type=F32)
        ).astype(BF16)
        wide = after_attn.astype(F32)
        normed = wide * lax.rsqrt(jnp.mean(wide * wide, axis=1, keepdims=True) + EPS) * gain_ref[...]
        return after_attn, normed.astype(BF16)

    after_attn, normed = normed_of(resid_ref[...], att_own[...])
    after[...] = after_attn
    tok_rows(z, x)[...] = normed
    for link in range(3):
        send_link(link, lambda link=link: first_normed(link).start())

    def part_rows(zz, xx, part):
        return tok_rows(zz, xx, part * early, rows - early if part else early)

    def tok_z(way, h, part):
        step = 1 - 2 * way
        here = part_rows(z - step * h, x, part)
        return remote(here, here, z_snd.at[way, h - 1], z_rcv.at[part, way, h - 1], z_device(z + step))

    def tok_z_arrived(way, h, part):
        here = part_rows(z - (1 - 2 * way) * (h + 1), x, part)
        remote(here, here, z_snd.at[way, h - 1], z_rcv.at[part, way, h - 1], x_peer).wait_recv()

    def tok_x(zz, xx, part):
        here = part_rows(zz, xx, part)
        return remote(here, here, x_snd.at[zz], x_rcv.at[zz], x_peer)

    def tok_x_end(zz, xx):
        here = tok_rows(zz, xx, 0, keep_t)
        return remote(here, here, x_snd.at[zz], x_rcv.at[zz], x_peer)

    def send_x(zz, part):
        @pl.when(middle(zz))
        def _():
            tok_x(zz, x, part).start()

        if part == 0:
            @pl.when(jnp.logical_not(middle(zz)))
            def _():
                tok_x_end(zz, x).start()

    def tok_half(way, to):
        here = tok_rows(last_z if way else 0, 1 - x, keep_t, rows - keep_t)
        return remote(here, here, g_snd.at[way], g_rcv.at[way], to)

    def from_origin(way):
        return last_z - z if way else z

    near_way = jnp.where(2 * z < nz, 0, 1)

    def absorb(link, zz, xx):
        first_resid(link).wait_recv()
        first_attended(link).wait_recv()
        tok_rows(zz, xx, 0, early)[...] = normed_of(res_in[link], att_in[link])[1]

    def hop(h, part, way):
        step = 1 - 2 * way
        source = z - step * (h + 1)

        @pl.when(inside(source))
        def _():
            if h > 0:
                tok_z_arrived(way, h, part)
            elif part == 0:
                absorb(way, source, x)
            else:
                first_normed(way, (source, x)).wait_recv()
            if h < nz - 2:
                @pl.when(inside(z + step))
                def _():
                    tok_z(way, h + 1, part).start()

            send_x(source, part)

    def pair_of(j):
        return z + ((j + 1) // 2) * (1 - 2 * (j % 2))

    def both_rows(zz):
        return pl.ds(pl.multiple_of(zz * 2 * rows, 2 * rows), 2 * rows)

    def make_gate(zz):
        here = both_rows(zz)
        gates[here, :] = jnp.dot(tok[here, :], wg[...], preferred_element_type=F32)

    def other_x_arrived(zz):
        @pl.when(middle(zz))
        def _():
            whole = tok_rows(zz, 1 - x)
            remote(whole, whole, x_snd.at[zz], x_rcv.at[zz], x_peer).wait_recv()

        @pl.when(jnp.logical_not(middle(zz)))
        def _():
            tok_x_end(zz, 1 - x).wait_recv()

    def gate_step(j, carry):
        zz = pair_of(j)

        @pl.when(inside(zz))
        def _():
            @pl.when(j > 0)
            def _():
                other_x_arrived(zz)

            make_gate(zz)

        return carry

    first_zz = z + (nz - 2) * (1 - 2 * near_way)

    def upward_over(zz, shards):
        total = None
        for q in shards:
            here = pl.ds(pl.multiple_of(q * depth, depth), depth)
            part = jnp.dot(tok[both_rows(zz), here], wu[here, :], preferred_element_type=F32)
            total = part if total is None else total + part
        return total

    relays = [(k, s) for k in range(2) for s in range(pieces_w[k])]

    def relay_to(n):
        while relays and n > 0:
            k, s = relays.pop(0)
            relay_weight(k, s)
            n -= 1

    def halves(h):
        for way in range(2):
            @pl.when(from_origin(way) == h + 1)
            def _():
                tok_half(way, x_peer).wait_recv()

                @pl.when(inside(z + 1 - 2 * way))
                def _():
                    tok_half(way, z_device(z + 1 - 2 * way)).start()

    for h in range(nz - 1):
        for part in range(2):
            hop(h, part, 1 - near_way)
            hop(h, part, near_way)
        if h == 0:
            absorb(2, z, 1 - x)
            first_normed(2, (z, 1 - x)).wait_recv()
            for way in range(2):
                @pl.when(from_origin(way) == 0)
                def _():
                    tok_half(way, z_device(z + 1 - 2 * way)).start()
            relay_to((pieces_w[0] + 1) // 2)
        elif h == 1:
            relay_to(pieces_w[0] // 2)
            weight_ready(0)
            lax.fori_loop(0, 3, gate_step, 0)
            relay_to((pieces_w[1] + 3) // 4)
        else:
            relay_to((pieces_w[1] + 7) // 8)
            lax.fori_loop(2 * h - 1, 2 * h + 1, gate_step, 0)
        if h == nz - 2:
            relay_to(len(relays) - 1)
            near_ready(1)

            @pl.when(inside(first_zz))
            def _():
                upper[...] = upward_over(first_zz, [i, partner])

        halves(h)
    relay_to(len(relays))

    def columns_of(chip):
        return lax.rem(i // 2 + chips - chip, chips)

    def end_way(zz):
        return jnp.where(zz == last_z, 0, 1)

    def sum_x(p, zz, part):
        there = pl.ds(part * keep, rows - keep if part else keep)
        return remote(x_out.at[p, zz, there], x_in.at[p, zz, there], rx_snd.at[part, p],
                      rx_rcv.at[p, zz], x_peer)

    def sum_x_whole(p, zz):
        return remote(x_out.at[p, zz], x_in.at[p, zz], rx_snd.at[0, p], rx_rcv.at[p, zz], x_peer)

    def sum_z(p, way, zz, here=False):
        step = jnp.where(inside(z + 1 - 2 * way), 1 - 2 * way, 0)
        off = 0 if here else step
        return remote(z_out.at[p, zz], z_in.at[p, way, zz], rz_snd.at[p],
                      rz_rcv.at[p, jnp.where(jnp.logical_and(way == 1, zz == z + off), nz, zz)],
                      z_device(z + step))

    def sum_half(p, way, to):
        return remote(h_out.at[p, way], h_in.at[p, way], rh_snd.at[p, way], rh_rcv.at[p, way], to)

    def next_z(way):
        return z_device(jnp.clip(z + 1 - 2 * way, 0, last_z))

    def down(chip, cs, zz):
        def half(xx):
            return hidden[pl.ds(pl.multiple_of((zz * 2 + xx) * rows, rows), rows), :]

        both = jnp.concatenate([half(1 - x), half(x)], axis=0)
        for c in cs:
            p = chip * cuts + c
            for q in range(2):
                part = jnp.dot(both, wd[2 * columns_of(chip) + q, c], preferred_element_type=F32)
                here = slice(q * cw, (q + 1) * cw)
                x_out[p, zz, :, here] = part[:rows].astype(BF16)
                own_part[p, zz, :, here] = part[rows:]
                h_own[p, jnp.where(middle(zz), 2, end_way(zz)), :, here] = part[keep:rows]

    def send_sums(p, zz):
        sum_x(p, zz, 0).start()

        @pl.when(middle(zz))
        def _():
            sum_x(p, zz, 1).start()

    def send_halves(ps, zz):
        for way in range(2):
            @pl.when(jnp.logical_and(from_origin(way) == 0, zz == (0 if way else last_z)))
            def _():
                for p in ps:
                    h_out[p, way] = h_own[p, way].astype(BF16)
                    sum_half(p, way, next_z(way)).start()

    turns = 2 * nz - 1

    def owner(j):
        way = j % 2
        return way, z + (nz - 1 - j // 2) * (1 - 2 * way)

    def finish_half(p, way):
        sum_half(p, way, x_peer).wait_recv()
        h_out[p, way] = (h_own[p, way] + h_in[p, way].astype(F32)).astype(BF16)
        sum_half(p, way, next_z(way)).start()

    def relay_half(p, way):
        @pl.when(middle(z))
        def _():
            finish_half(p, way)

    def own_half(p):
        for way in range(2):
            @pl.when(z == (0 if way else last_z))
            def _():
                sum_half(p, way, x_peer).wait_recv()
                x_out[p, z, keep:, :] = (h_own[p, way] + h_in[p, way].astype(F32)).astype(BF16)
                sum_x(p, z, 1).start()

    def finish(p, way, zz):
        more = inside(z - (1 - 2 * way))

        @pl.when(inside(zz))
        def _():
            @pl.when(middle(zz))
            def _():
                sum_x_whole(p, zz).wait_recv()

            @pl.when(jnp.logical_not(middle(zz)))
            def _():
                sum_x(p, zz, 0).wait_recv()

            @pl.when(more)
            def _():
                sum_z(p, way, zz, True).wait_recv()
                z_out[p, zz] = (
                    own_part[p, zz] + x_in[p, zz].astype(F32) + z_in[p, way, zz].astype(F32)
                ).astype(BF16)

            @pl.when(jnp.logical_not(more))
            def _():
                z_out[p, zz] = (own_part[p, zz] + x_in[p, zz].astype(F32)).astype(BF16)

            sum_z(p, way, zz).start()

    near_ready(2)
    def make_hidden(zz, upward):
        here = both_rows(zz)
        gate = gates[here, :]
        hidden[here, :] = (gate / (1.0 + jnp.exp(-gate)) * upward).astype(BF16)

    def first_sums(zz):
        for p in range(cuts):
            down(0, (p,), zz)
            send_sums(p, zz)
            send_halves((p,), zz)

    @pl.when(inside(first_zz))
    def _():
        upper[...] += upward_over(first_zz, [lax.rem(i + 2 * d, n_in) for d in steps])

    for s in range(pieces_w[1]):
        far_ready(1, s)

    @pl.when(inside(first_zz))
    def _():
        make_hidden(first_zz, upper[...] + upward_over(
            first_zz, [lax.rem(partner + 2 * d, n_in) for d in steps]))
        first_sums(first_zz)

    def hidden_step(j, carry):
        _, zz = owner(j)

        @pl.when(jnp.logical_and(j == 3, jnp.logical_not(middle(z))))
        def _():
            finish(0, near_way, first_zz)

        @pl.when(jnp.logical_and(j == turns - 1, jnp.logical_not(middle(z))))
        def _():
            for p in range(1, cuts):
                finish(p, near_way, first_zz)

        @pl.when(jnp.logical_and(inside(zz), zz != first_zz))
        def _():
            @pl.when(j < 2)
            def _():
                other_x_arrived(zz)
                make_gate(zz)

            make_hidden(zz, jnp.dot(tok[both_rows(zz), :], wu[...], preferred_element_type=F32))

            @pl.when(j < turns - 1)
            def _():
                first_sums(zz)

            @pl.when(j == turns - 1)
            def _():
                down(0, range(cuts), zz)

        return carry

    lax.fori_loop(0, turns, hidden_step, 0)

    near_end = jnp.where(near_way == 0, last_z, 0)

    def finish_end(p):
        relay_half(p, near_way)
        finish(p, near_way, near_end)

    def finish_way(p, way, skip):
        def step(n, carry):
            zz = z + (nz - 1 - n) * (1 - 2 * way)

            @pl.when(zz != skip)
            def _():
                finish(p, way, zz)

            return carry

        lax.fori_loop(0, nz - 1, step, 0)

    def finish_outer(ps, start):
        def step(n, carry):
            for p in ps:
                finish(p, near_way, z + (nz - 1 - n) * (1 - 2 * near_way))
            return carry

        lax.fori_loop(start, nz - 1, step, 0)

    def far_down(s, hold=False):
        far_ready(2, s)

        def step(t, carry):
            chip = 1 + t // turns
            j = t % turns
            _, zz = owner(j)

            @pl.when(inside(zz))
            def _():
                down(chip, (s,), zz)

                @pl.when(j < (turns - 3 if hold else turns - 1))
                def _():
                    send_sums(chip * cuts + s, zz)
                    send_halves((chip * cuts + s,), zz)

            return carry

        lax.fori_loop(0, (chips - 1) * turns, step, 0)

    rest = [c * cuts + s for s in range(cuts) for c in range(1, chips)]

    def own_sums(ps):
        for p in ps:
            sum_x(p, z, 0).start()

            @pl.when(middle(z))
            def _():
                sum_x(p, z, 1).start()

    def drain_first():
        for d in steps:
            kv_send(0, d).wait_send()
        for d in range(chips):
            kv_relay(0, d).wait_send()

        @pl.when(o < n_out - 1)
        def _():
            for d in range(chips):
                kv_send(1, d).wait_send()

        @pl.when(o > 0)
        def _():
            for d in range(chips):
                kv_relay(1, d).wait_send()

        for link in range(3):
            def sent(link=link):
                first_attended(link).wait_send()
                whole = tok_rows(z, x)
                remote(whole, whole, r_snd.at[link], r_rcv.at[link], target(link)).wait_send()

            send_link(link, sent)
        for way in range(2):
            step = 1 - 2 * way

            @pl.when(inside(z + step))
            def _():
                tok_half(way, x_peer).wait_send()
                for h in range(1, nz - 1):
                    @pl.when(inside(z - step * h))
                    def _():
                        whole = tok_rows(z, x)
                        remote(whole, whole, z_snd.at[way, h - 1], z_rcv.at[0, way, h - 1], x_peer).wait_send()
        for zz in range(nz):
            @pl.when(z != zz)
            def _():
                if zz == 0 or zz == last_z:
                    tok_x_end(zz, x).wait_send()
                else:
                    whole = tok_rows(zz, x)
                    remote(whole, whole, x_snd.at[zz], x_rcv.at[zz], x_peer).wait_send()

    def drain_sums(p):
        for way in range(2):
            @pl.when(inside(z + 1 - 2 * way))
            def _():
                sum_half(p, way, x_peer).wait_send()
        first = x_out.at[p, :, pl.ds(0, keep)]
        remote(first, first, rx_snd.at[0, p], rx_rcv.at[p, 0], x_peer).wait_send()

        def second(n):
            there = x_out.at[p, pl.ds(0, n), pl.ds(keep, rows - keep)]
            remote(there, there, rx_snd.at[1, p], rx_rcv.at[p, 0], x_peer).wait_send()

        pl.when(middle(z))(lambda: second(nz - 2))
        pl.when(jnp.logical_not(middle(z)))(lambda: second(nz - 1))
        others = z_out.at[p, pl.ds(0, nz - 1)]
        remote(others, others, rz_snd.at[p], rz_rcv.at[p, 0], x_peer).wait_send()

    @pl.when(middle(z))
    def _():
        own_sums(range(cuts))
        for p in range(cuts):
            relay_half(p, near_way)
        relay_weight(2, 0)
        far_down(0)
        for p in range(cuts):
            relay_half(p, 1 - near_way)
        for p in range(cuts):
            finish_way(p, near_way, near_end)
        for p in range(cuts):
            finish(p, near_way, near_end)
        for s in range(1, cuts):
            relay_weight(2, s)
            far_down(s)
        own_sums(rest)
        for p in range(cuts):
            finish_way(p, 1 - near_way, -1)
        for p in rest:
            finish_end(p)
        for p in rest:
            relay_half(p, 1 - near_way)
        for p in rest:
            finish_way(p, 1 - near_way, -1)
            finish_way(p, near_way, near_end)

    @pl.when(jnp.logical_not(middle(z)))
    def _():
        finish(0, near_way, near_end)
        relay_weight(2, 0)
        for p in range(1, cuts):
            finish(p, near_way, near_end)
        far_down(0, True)
        finish_outer((0,), 2)
        for s in range(1, cuts):
            relay_weight(2, s)
            for c in range(1, chips):
                finish_end(c * cuts + s - 1)
            far_down(s, True)
        for p in rest:
            send_sums(p, z + 1 - 2 * near_way)
        own_sums(range(parts_n))
        for c in range(1, chips):
            finish_end(c * cuts + cuts - 1)
        if cuts > 1:
            finish_outer(range(1, cuts), 2)
        finish_outer(rest, 1)

    drain_first()
    for k in range(3):
        drain_weights(k)
    for p in range(parts_n):
        own_half(p)
    for p in range(parts_n):
        for way in range(2):
            @pl.when(inside(z - (1 - 2 * way)))
            def _():
                sum_z(p, way, z, True).wait_recv()
                own_part[p, z] = own_part[p, z] + z_in[p, way, z].astype(F32)
        sum_x_whole(p, z).wait_recv()
        for q in range(2):
            source = 2 * columns_of(p // cuts) + q
            here = pl.ds(pl.multiple_of(source * width + (p % cuts) * cw, cw), cw)
            cols = slice(q * cw, (q + 1) * cw)
            out_ref[:, here] = (
                after[:, here].astype(F32)
                + (own_part[p, z, :, cols] + x_in[p, z, :, cols].astype(F32))).astype(BF16)
        if p < parts_n - 1:
            drain_sums(p)

    drain_sums(parts_n - 1)


def per_device(n_out, n_in, resid, queries, keyvals, piece_order, out_proj, mlp_gain, w_gate, w_up, w_down):
    rows, model = resid.shape
    units, width = w_down.shape
    nz, chips = n_out // 2, n_in // 2
    cuts = max(1, width // 256)
    pieces_w = (max(1, 8 // n_in), max(1, 32 // n_in), cuts)
    cw = width // cuts
    parts_n = chips * cuts
    early = rows * 3 // 4
    dma = pltpu.SemaphoreType.DMA
    vmem = pl.BlockSpec(memory_space=pltpu.VMEM)
    hbm = pl.BlockSpec(memory_space=pl.ANY)
    keep = rows * KEEP // 128
    half = rows - keep
    return pl.pallas_call(
        functools.partial(layer_kernel, n_out, n_in, cuts, pieces_w, early, keep),
        out_shape=pltpu.VMEM(resid.shape, BF16),
        in_specs=[hbm] * 9,
        out_specs=vmem,
        scratch_shapes=[
            pltpu.SMEM(piece_order.shape, jnp.int32),
            pltpu.VMEM(resid.shape, BF16),
            pltpu.VMEM(queries.shape, BF16),
            pltpu.VMEM(out_proj.shape, BF16),
            pltpu.VMEM((1, model), F32),
            dma((5,)),
            pltpu.VMEM((2 * n_in * rows, keyvals.shape[1]), BF16),
            pltpu.VMEM((model, units), BF16),
            pltpu.VMEM((model, units), BF16),
            pltpu.VMEM((n_in, cuts, units, cw), BF16),
            pltpu.VMEM((n_out * rows, model), BF16),
            pltpu.VMEM((rows, model), BF16),
            pltpu.VMEM(queries.shape, BF16),
            pltpu.VMEM((3, early, model), BF16),
            pltpu.VMEM((3, early, queries.shape[1]), BF16),
            pltpu.VMEM((n_out * rows, units), F32),
            pltpu.VMEM((2 * rows, units), F32),
            pltpu.VMEM((n_out * rows, units), BF16),
            pltpu.VMEM((parts_n, nz, rows, 2 * cw), BF16),
            pltpu.VMEM((parts_n, nz, rows, 2 * cw), BF16),
            pltpu.VMEM((parts_n, nz, rows, 2 * cw), F32),
            pltpu.VMEM((parts_n, nz, rows, 2 * cw), BF16),
            pltpu.VMEM((parts_n, 2, nz, rows, 2 * cw), BF16),
            pltpu.VMEM((parts_n, 3, half, 2 * cw), F32),
            pltpu.VMEM((parts_n, 2, half, 2 * cw), BF16),
            pltpu.VMEM((parts_n, 2, half, 2 * cw), BF16),
            dma(()), dma((2, chips)), dma((2, chips)), dma((2, n_in)),
            dma((3,)), dma((3,)), dma((3,)), dma((3, chips)), dma((3, chips)),
            dma((chips - 1, 2, sum(pieces_w))),
            dma((3,)), dma((3,)), dma((3,)), dma((3,)), dma((3,)),
            dma((2, nz - 2)), dma((2, 2, nz - 2)), dma((2,)), dma((2,)), dma((nz,)), dma((nz,)),
            dma((2, parts_n)), dma((parts_n, nz)), dma((parts_n,)), dma((parts_n, nz + 1)),
            dma((parts_n, 2)), dma((parts_n, 2)),
        ],
        compiler_params=pltpu.CompilerParams(
            collective_id=0, has_side_effects=True, vmem_limit_bytes=63000 * 1024
        ),
        name="layer",
    )(piece_order, resid, queries, keyvals, out_proj, mlp_gain.reshape(1, -1), w_gate, w_up, w_down)


def solution(mesh):
    placed = (
        P(("outer", "inner"), None),
        P(("outer", "inner"), None),
        P(("outer", "inner"), None),
        P(),
        P(),
        P(),
        P("inner", "outer"),
        P("inner", "outer"),
        P("outer", "inner"),
    )
    return jax.shard_map(
        functools.partial(per_device, mesh.shape["outer"], mesh.shape["inner"]),
        mesh=mesh,
        in_specs=placed,
        out_specs=P(("outer", "inner"), None),
        check_vma=False,
    )
```

```python
import functools

import jax
import jax.numpy as jnp
from jax import lax
from jax.experimental import pallas as pl
from jax.experimental.pallas import tpu as pltpu
from jax.sharding import PartitionSpec as P

MESH = pl.DeviceIdType.MESH
F32 = jnp.float32
BF16 = jnp.bfloat16
EPS = 1e-05
KEEP = 80


def layer_kernel(
    n_out, n_in, cuts, pieces_w, early, keep,
    order_hbm, resid_hbm, query_hbm, kv_ref, proj_hbm, gain_hbm, wg_ref, wu_ref, wd_ref,
    out_ref,
    order_ref, resid_ref, query_ref, proj_ref, gain_ref, in_sem,
    kv_all, wg, wu, wd, tok, after, att_own, res_in, att_in, gates, upper, hidden,
    x_out, x_in, own_part, z_out, z_in, h_own, h_out, h_in,
    kv_loc, kv_snd, kv_relay_snd, kv_rcv, w_loc, w_pair_snd, w_pair_rcv, w_snd, w_relay_snd, w_rcv,
    r_snd, r_rcv, a_snd, a_rcv, n_rcv, z_snd, z_rcv, g_snd, g_rcv, x_snd, x_rcv,
    rx_snd, rx_rcv, rz_snd, rz_rcv, rh_snd, rh_rcv,
):
    o = lax.axis_index("outer")
    i = lax.axis_index("inner")
    nz = n_out // 2
    z, x = o // 2, o % 2
    core = i % 2
    partner = i + 1 - 2 * core
    x_peer = (z * 2 + 1 - x, i)
    core_peer = (o, partner)
    rows = resid_hbm.shape[0]
    head = kv_ref.shape[1] // 2
    heads = query_ref.shape[1] // head
    pieces = order_ref.shape[0]
    block = n_in * rows
    span = block // pieces
    depth = wg_ref.shape[0]
    units, width = wd_ref.shape
    chips = n_in // 2
    parts_n = chips * cuts
    cw = width // cuts
    keep_t = rows // 2
    last_z = nz - 1

    def remote(src, dst, ssem, rsem, device):
        return pltpu.make_async_remote_copy(
            src_ref=src, dst_ref=dst, send_sem=ssem, recv_sem=rsem,
            device_id=device, device_id_type=MESH,
        )

    def inside(zz):
        return jnp.logical_and(zz >= 0, zz < nz)

    def middle(zz):
        return jnp.logical_and(zz > 0, zz < last_z)

    def z_device(zz):
        return (zz * 2 + x, i)

    barrier = pltpu.get_barrier_semaphore()
    after_o, before_o = lax.rem(o + 1, n_out), lax.rem(o + n_out - 1, n_out)

    def greet(device):
        pl.semaphore_signal(barrier, inc=1, device_id=device, device_id_type=MESH)

    for d in range(1, n_in):
        greet((o, lax.rem(i + d, n_in)))
    greet(x_peer)
    pl.when(z > 0)(lambda: greet(z_device(z - 1)))
    pl.when(z < last_z)(lambda: greet(z_device(z + 1)))

    @pl.when(o > 0)
    def _():
        for d in range(chips):
            greet((before_o, lax.rem(i + 2 * d, n_in)))

    loads = [
        pltpu.make_async_copy(src, dst, in_sem.at[n])
        for n, (src, dst) in enumerate((
            (order_hbm, order_ref), (query_hbm, query_ref), (resid_hbm, resid_ref), (proj_hbm, proj_ref), (gain_hbm, gain_ref)))
    ]
    for load in loads:
        load.start()

    pl.semaphore_wait(
        barrier, n_in + jnp.where(z > 0, 1, 0) + jnp.where(z < last_z, 1, 0)
        + jnp.where(o < n_out - 1, chips, 0))

    own_rows = pl.ds(pl.multiple_of(i * rows, rows), rows)
    kv_copy = pltpu.make_async_copy(kv_ref, kv_all.at[own_rows], kv_loc)
    kv_copy.start()

    steps = range(1, chips)

    def kv_slot(part, q):
        return kv_all.at[pl.ds(pl.multiple_of(part * block + q * rows, rows), rows)]

    def kv_send(part, d):
        return remote(kv_ref, kv_slot(part, i), kv_snd.at[part, d], kv_rcv.at[part, i],
                      (after_o if part else o, lax.rem(i + 2 * d, n_in)))

    def kv_relay(part, d):
        q = lax.rem(i + n_in - 2 * d, n_in)
        src = kv_ref if part == 0 and d == 0 else kv_slot(part, q)
        return remote(src, kv_slot(part, q), kv_relay_snd.at[part, d], kv_rcv.at[part, q], core_peer)

    def kv_arrived(part, q):
        here = kv_slot(part, q)
        remote(here, here, kv_relay_snd.at[part, 0], kv_rcv.at[part, q], core_peer).wait_recv()

    for d in steps:
        kv_send(0, d).start()

    @pl.when(o < n_out - 1)
    def _():
        for d in range(chips):
            kv_send(1, d).start()

    kv_relay(0, 0).start()

    def tok_rows(zz, xx, start=0, size=rows):
        return tok.at[pl.ds(pl.multiple_of((zz * 2 + xx) * rows + start, 16), size)]

    def target(link):
        if isinstance(link, int):
            return x_peer if link == 2 else z_device(z + 1 - 2 * link)
        return z_device(z + 1 - 2 * link)

    def first_resid(link):
        return remote(resid_hbm.at[pl.ds(0, early)], res_in.at[link], r_snd.at[link], r_rcv.at[link],
                      target(link))

    def first_attended(link):
        return remote(att_own.at[pl.ds(0, early)], att_in.at[link], a_snd.at[link], a_rcv.at[link],
                      target(link))

    def first_normed(link, source=None):
        here = tok_rows(*(source or (z, x)), early, rows - early)
        return remote(here, here, r_snd.at[link], n_rcv.at[link], target(link))

    def send_link(link, act):
        if link == 2:
            act()
        else:
            pl.when(inside(z + 1 - 2 * link))(act)

    for link in range(3):
        send_link(link, lambda link=link: first_resid(link).start())

    def slot(k, q, s):
        if k == 2:
            return wd.at[q, s]
        full = wg if k == 0 else wu
        size = depth // pieces_w[k]
        return full.at[pl.ds(pl.multiple_of(q * depth + s * size, size), size)]

    srcs = (wg_ref, wu_ref, wd_ref)

    def w_src(k, s):
        if k == 2:
            return wd_ref.at[:, pl.ds(s * cw, cw)]
        size = depth // pieces_w[k]
        return srcs[k].at[pl.ds(s * size, size)]

    def w_parts(k):
        return pieces_w[k]

    def w_index(k, s):
        return sum(pieces_w[:k]) + s

    def shard(k, q):
        if k == 2:
            return wd.at[q]
        full = wg if k == 0 else wu
        return full.at[pl.ds(pl.multiple_of(q * depth, depth), depth)]

    def far(d):
        return lax.rem(i + n_in - 2 * d, n_in)

    def w_far(k, d, s):
        return remote(w_src(k, s), slot(k, i, s), w_snd.at[k, d - 1], w_rcv.at[d - 1, 0, w_index(k, s)],
                      (o, lax.rem(i + 2 * d, n_in)))

    def w_relay(k, d, s):
        here = slot(k, far(d), s)
        return remote(here, here, w_relay_snd.at[k, d - 1], w_rcv.at[d - 1, 1, w_index(k, s)], core_peer)

    def w_pair(k, s):
        return remote(w_src(k, s), slot(k, i, s), w_pair_snd.at[k], w_pair_rcv.at[k], core_peer)

    def w_local(k, s):
        return pltpu.make_async_copy(w_src(k, s), slot(k, i, s), w_loc.at[k])

    def near_ready(k):
        mine, other = shard(k, i), shard(k, partner)
        pltpu.make_async_copy(mine, mine, w_loc.at[k]).wait()
        remote(other, other, w_pair_snd.at[k], w_pair_rcv.at[k], core_peer).wait_recv()

    def far_ready(k, s):
        for d in steps:
            here = slot(k, lax.rem(partner + n_in - 2 * d, n_in), s)
            remote(here, here, w_relay_snd.at[k, d - 1], w_rcv.at[d - 1, 1, w_index(k, s)], core_peer).wait_recv()

    def relay_weight(k, s):
        for d in steps:
            here = slot(k, far(d), s)
            remote(here, here, w_relay_snd.at[k, d - 1], w_rcv.at[d - 1, 0, w_index(k, s)], core_peer).wait_recv()
            w_relay(k, d, s).start()

    def weight_ready(k):
        near_ready(k)
        for s in range(w_parts(k)):
            far_ready(k, s)

    def drain_weights(k):
        mine = shard(k, i)
        remote(mine, mine, w_pair_snd.at[k], w_pair_rcv.at[k], core_peer).wait_send()
        for d in steps:
            remote(mine, mine, w_snd.at[k, d - 1], w_pair_rcv.at[k], core_peer).wait_send()
            remote(mine, mine, w_relay_snd.at[k, d - 1], w_pair_rcv.at[k], core_peer).wait_send()

    for k in range(3):
        for s in range(w_parts(k)):
            for d in steps:
                w_far(k, d, s).start()
    for k in range(3):
        for s in range(w_parts(k)):
            w_pair(k, s).start()
            w_local(k, s).start()

    loads[0].wait()
    lane = lax.broadcasted_iota(jnp.int32, (rows, block), 1)
    key_pos = jnp.zeros((rows, block), jnp.int32)
    for p in range(pieces):
        key_pos = jnp.where(lane // span == p, order_ref[p] * span + lane % span, key_pos)
    row = lax.broadcasted_iota(jnp.int32, (rows, block), 0)
    query_pos = jnp.zeros((rows, block), jnp.int32)
    for p in range(rows // span):
        query_pos = jnp.where(
            row // span == p, order_ref[i * (rows // span) + p] * span + row % span, query_pos)
    own_visible = key_pos <= query_pos
    before_visible = (jnp.zeros((rows, block), jnp.int32) + o) > 0

    @pl.when(o == 0)
    def _():
        kv_all[block:, :] = jnp.zeros((block, 2 * head), BF16)

    for zz in (0, last_z):
        @pl.when(z != zz)
        def _():
            x_in[:, zz, keep:, :] = jnp.zeros((parts_n, rows - keep, 2 * cw), BF16)

    for d in steps:
        kv_arrived(0, lax.rem(i + n_in - 2 * d, n_in))
        kv_relay(0, d).start()

    @pl.when(o > 0)
    def _():
        for d in range(chips):
            kv_arrived(1, lax.rem(i + n_in - 2 * d, n_in))
            kv_relay(1, d).start()

    kv_copy.wait()
    for d in range(chips):
        kv_arrived(0, lax.rem(partner + 2 * d, n_in))

    @pl.when(o > 0)
    def _():
        for d in range(chips):
            kv_arrived(1, lax.rem(partner + 2 * d, n_in))

    loads[1].wait()
    parts = []
    nt = (((1,), (1,)), ((), ()))
    for h in range(heads):
        query = query_ref[:, h * head:(h + 1) * head]
        own_score = lax.dot_general(
            query, kv_all[:block, :head], nt, preferred_element_type=F32) * head ** (-0.5)
        before_score = lax.dot_general(
            query, kv_all[block:, :head], nt, preferred_element_type=F32) * head ** (-0.5)
        own_score = jnp.where(own_visible, own_score, -1e30)
        before_score = jnp.where(before_visible, before_score, -1e30)
        top = jnp.maximum(
            jnp.max(own_score, axis=1, keepdims=True), jnp.max(before_score, axis=1, keepdims=True))
        own_w = jnp.where(own_visible, jnp.exp(own_score - top), 0.0)
        before_w = jnp.where(before_visible, jnp.exp(before_score - top), 0.0)
        total = jnp.sum(own_w, axis=1, keepdims=True) + jnp.sum(before_w, axis=1, keepdims=True)
        mixed = jnp.dot(own_w.astype(BF16), kv_all[:block, head:], preferred_element_type=F32)
        mixed += jnp.dot(before_w.astype(BF16), kv_all[block:, head:], preferred_element_type=F32)
        parts.append((mixed / total).astype(BF16))
    att_own[...] = jnp.concatenate(parts, axis=1)
    for link in range(3):
        send_link(link, lambda link=link: first_attended(link).start())

    for load in loads[2:]:
        load.wait()

    def normed_of(resid, attended):
        after_attn = (
            resid.astype(F32) + jnp.dot(attended, proj_ref[...], preferred_element_type=F32)
        ).astype(BF16)
        wide = after_attn.astype(F32)
        normed = wide * lax.rsqrt(jnp.mean(wide * wide, axis=1, keepdims=True) + EPS) * gain_ref[...]
        return after_attn, normed.astype(BF16)

    after_attn, normed = normed_of(resid_ref[...], att_own[...])
    after[...] = after_attn
    tok_rows(z, x)[...] = normed
    for link in range(3):
        send_link(link, lambda link=link: first_normed(link).start())

    def part_rows(zz, xx, part):
        return tok_rows(zz, xx, part * early, rows - early if part else early)

    def tok_z(way, h, part):
        step = 1 - 2 * way
        here = part_rows(z - step * h, x, part)
        return remote(here, here, z_snd.at[way, h - 1], z_rcv.at[part, way, h - 1], z_device(z + step))

    def tok_z_arrived(way, h, part):
        here = part_rows(z - (1 - 2 * way) * (h + 1), x, part)
        remote(here, here, z_snd.at[way, h - 1], z_rcv.at[part, way, h - 1], x_peer).wait_recv()

    def tok_x(zz, xx, part):
        here = part_rows(zz, xx, part)
        return remote(here, here, x_snd.at[zz], x_rcv.at[zz], x_peer)

    def tok_x_end(zz, xx):
        here = tok_rows(zz, xx, 0, keep_t)
        return remote(here, here, x_snd.at[zz], x_rcv.at[zz], x_peer)

    def send_x(zz, part):
        @pl.when(middle(zz))
        def _():
            tok_x(zz, x, part).start()

        if part == 0:
            @pl.when(jnp.logical_not(middle(zz)))
            def _():
                tok_x_end(zz, x).start()

    def tok_half(way, to):
        here = tok_rows(last_z if way else 0, 1 - x, keep_t, rows - keep_t)
        return remote(here, here, g_snd.at[way], g_rcv.at[way], to)

    def from_origin(way):
        return last_z - z if way else z

    near_way = jnp.where(2 * z < nz, 0, 1)

    def absorb(link, zz, xx):
        first_resid(link).wait_recv()
        first_attended(link).wait_recv()
        tok_rows(zz, xx, 0, early)[...] = normed_of(res_in[link], att_in[link])[1]

    def hop(h, part, way):
        step = 1 - 2 * way
        source = z - step * (h + 1)

        @pl.when(inside(source))
        def _():
            if h > 0:
                tok_z_arrived(way, h, part)
            elif part == 0:
                absorb(way, source, x)
            else:
                first_normed(way, (source, x)).wait_recv()
            if h < nz - 2:
                @pl.when(inside(z + step))
                def _():
                    tok_z(way, h + 1, part).start()

            send_x(source, part)

    def pair_of(j):
        return z + ((j + 1) // 2) * (1 - 2 * (j % 2))

    def both_rows(zz):
        return pl.ds(pl.multiple_of(zz * 2 * rows, 2 * rows), 2 * rows)

    def make_gate(zz):
        here = both_rows(zz)
        gates[here, :] = jnp.dot(tok[here, :], wg[...], preferred_element_type=F32)

    def other_x_arrived(zz):
        @pl.when(middle(zz))
        def _():
            whole = tok_rows(zz, 1 - x)
            remote(whole, whole, x_snd.at[zz], x_rcv.at[zz], x_peer).wait_recv()

        @pl.when(jnp.logical_not(middle(zz)))
        def _():
            tok_x_end(zz, 1 - x).wait_recv()

    def gate_step(j, carry):
        zz = pair_of(j)

        @pl.when(inside(zz))
        def _():
            @pl.when(j > 0)
            def _():
                other_x_arrived(zz)

            make_gate(zz)

        return carry

    first_zz = z + (nz - 2) * (1 - 2 * near_way)

    def upward_over(zz, shards):
        total = None
        for q in shards:
            here = pl.ds(pl.multiple_of(q * depth, depth), depth)
            part = jnp.dot(tok[both_rows(zz), here], wu[here, :], preferred_element_type=F32)
            total = part if total is None else total + part
        return total

    relays = [(k, s) for k in range(2) for s in range(pieces_w[k])]

    def relay_to(n):
        while relays and n > 0:
            k, s = relays.pop(0)
            relay_weight(k, s)
            n -= 1

    def halves(h):
        for way in range(2):
            @pl.when(from_origin(way) == h + 1)
            def _():
                tok_half(way, x_peer).wait_recv()

                @pl.when(inside(z + 1 - 2 * way))
                def _():
                    tok_half(way, z_device(z + 1 - 2 * way)).start()

    for h in range(nz - 1):
        for part in range(2):
            hop(h, part, 1 - near_way)
            hop(h, part, near_way)
        if h == 0:
            absorb(2, z, 1 - x)
            first_normed(2, (z, 1 - x)).wait_recv()
            for way in range(2):
                @pl.when(from_origin(way) == 0)
                def _():
                    tok_half(way, z_device(z + 1 - 2 * way)).start()
            relay_to((pieces_w[0] + 1) // 2)
        elif h == 1:
            relay_to(pieces_w[0] // 2)
            weight_ready(0)
            lax.fori_loop(0, 3, gate_step, 0)
            relay_to((pieces_w[1] + 3) // 4)
        else:
            relay_to((pieces_w[1] + 7) // 8)
            lax.fori_loop(2 * h - 1, 2 * h + 1, gate_step, 0)
        if h == nz - 2:
            relay_to(len(relays) - 1)
            near_ready(1)

            @pl.when(inside(first_zz))
            def _():
                upper[...] = upward_over(first_zz, [i, partner])

        halves(h)
    relay_to(len(relays))

    def columns_of(chip):
        return lax.rem(i // 2 + chips - chip, chips)

    def end_way(zz):
        return jnp.where(zz == last_z, 0, 1)

    def sum_x(p, zz, part):
        there = pl.ds(part * keep, rows - keep if part else keep)
        return remote(x_out.at[p, zz, there], x_in.at[p, zz, there], rx_snd.at[part],
                      rx_rcv.at[p, zz], x_peer)

    def sum_x_whole(p, zz):
        return remote(x_out.at[p, zz], x_in.at[p, zz], rx_snd.at[0], rx_rcv.at[p, zz], x_peer)

    def sum_z(p, way, zz, here=False):
        step = jnp.where(inside(z + 1 - 2 * way), 1 - 2 * way, 0)
        off = 0 if here else step
        return remote(z_out.at[p, zz], z_in.at[p, way, zz], rz_snd,
                      rz_rcv.at[p, jnp.where(jnp.logical_and(way == 1, zz == z + off), nz, zz)],
                      z_device(z + step))

    def sum_half(p, way, to):
        return remote(h_out.at[p, way], h_in.at[p, way], rh_snd.at[way], rh_rcv.at[p, way], to)

    def next_z(way):
        return z_device(jnp.clip(z + 1 - 2 * way, 0, last_z))

    def down(chip, cs, zz):
        def half(xx):
            return hidden[pl.ds(pl.multiple_of((zz * 2 + xx) * rows, rows), rows), :]

        both = jnp.concatenate([half(1 - x), half(x)], axis=0)
        for c in cs:
            p = chip * cuts + c
            for q in range(2):
                part = jnp.dot(both, wd[2 * columns_of(chip) + q, c], preferred_element_type=F32)
                here = slice(q * cw, (q + 1) * cw)
                x_out[p, zz, :, here] = part[:rows].astype(BF16)
                own_part[p, zz, :, here] = part[rows:]
                h_own[p, jnp.where(middle(zz), 2, end_way(zz)), :, here] = part[keep:rows]

    def send_sums(p, zz):
        sum_x(p, zz, 0).start()

        @pl.when(middle(zz))
        def _():
            sum_x(p, zz, 1).start()

    def send_halves(ps, zz):
        for way in range(2):
            @pl.when(jnp.logical_and(from_origin(way) == 0, zz == (0 if way else last_z)))
            def _():
                for p in ps:
                    h_out[p, way] = h_own[p, way].astype(BF16)
                    sum_half(p, way, next_z(way)).start()

    turns = 2 * nz - 1

    def owner(j):
        way = j % 2
        return way, z + (nz - 1 - j // 2) * (1 - 2 * way)

    def finish_half(p, way):
        sum_half(p, way, x_peer).wait_recv()
        h_out[p, way] = (h_own[p, way] + h_in[p, way].astype(F32)).astype(BF16)
        sum_half(p, way, next_z(way)).start()

    def relay_half(p, way):
        @pl.when(middle(z))
        def _():
            finish_half(p, way)

    def own_half(p):
        for way in range(2):
            @pl.when(z == (0 if way else last_z))
            def _():
                sum_half(p, way, x_peer).wait_recv()
                x_out[p, z, keep:, :] = (h_own[p, way] + h_in[p, way].astype(F32)).astype(BF16)
                sum_x(p, z, 1).start()

    def finish(p, way, zz):
        more = inside(z - (1 - 2 * way))

        @pl.when(inside(zz))
        def _():
            @pl.when(middle(zz))
            def _():
                sum_x_whole(p, zz).wait_recv()

            @pl.when(jnp.logical_not(middle(zz)))
            def _():
                sum_x(p, zz, 0).wait_recv()

            @pl.when(more)
            def _():
                sum_z(p, way, zz, True).wait_recv()
                z_out[p, zz] = (
                    own_part[p, zz] + x_in[p, zz].astype(F32) + z_in[p, way, zz].astype(F32)
                ).astype(BF16)

            @pl.when(jnp.logical_not(more))
            def _():
                z_out[p, zz] = (own_part[p, zz] + x_in[p, zz].astype(F32)).astype(BF16)

            sum_z(p, way, zz).start()

    near_ready(2)
    def make_hidden(zz, upward):
        here = both_rows(zz)
        gate = gates[here, :]
        hidden[here, :] = (gate / (1.0 + jnp.exp(-gate)) * upward).astype(BF16)

    def first_sums(zz):
        for p in range(cuts):
            down(0, (p,), zz)
            send_sums(p, zz)
            send_halves((p,), zz)

    @pl.when(inside(first_zz))
    def _():
        upper[...] += upward_over(first_zz, [lax.rem(i + 2 * d, n_in) for d in steps])

    @pl.when(jnp.logical_and(jnp.logical_not(middle(z)), core == 1))
    def _():
        other_x_arrived(last_z - z)
        make_gate(last_z - z)

    for s in range(pieces_w[1]):
        far_ready(1, s)

    @pl.when(inside(first_zz))
    def _():
        for xx in (1 - x, x):
            here = pl.ds(pl.multiple_of((first_zz * 2 + xx) * rows, rows), rows)
            upward = upper[pl.ds(pl.multiple_of(xx * rows, rows), rows), :]
            for d in steps:
                q = lax.rem(partner + 2 * d, n_in)
                there = pl.ds(pl.multiple_of(q * depth, depth), depth)
                upward += jnp.dot(tok[here, there], wu[there, :], preferred_element_type=F32)
            gate = gates[here, :]
            hidden[here, :] = (gate / (1.0 + jnp.exp(-gate)) * upward).astype(BF16)
            for q in range(2):
                part = jnp.dot(hidden[here, :], wd[2 * columns_of(0) + q, 0], preferred_element_type=F32)
                cols = slice(q * cw, (q + 1) * cw)
                if xx is x:
                    own_part[0, first_zz, :, cols] = part
                else:
                    x_out[0, first_zz, :, cols] = part.astype(BF16)
                    h_own[0, jnp.where(middle(first_zz), 2, end_way(first_zz)), :, cols] = part[keep:]
            if xx is not x:
                send_sums(0, first_zz)
        for p in range(1, cuts):
            down(0, (p,), first_zz)
            send_sums(p, first_zz)

    def hidden_step(j, carry):
        _, zz = owner(j)

        @pl.when(jnp.logical_and(j == 3, jnp.logical_not(middle(z))))
        def _():
            finish(0, near_way, first_zz)

        @pl.when(jnp.logical_and(j == turns - 1, jnp.logical_not(middle(z))))
        def _():
            for p in range(1, cuts):
                finish(p, near_way, first_zz)

        @pl.when(jnp.logical_and(inside(zz), zz != first_zz))
        def _():
            @pl.when(jnp.logical_and(j < 2, core == 0))
            def _():
                other_x_arrived(zz)
                make_gate(zz)

            make_hidden(zz, jnp.dot(tok[both_rows(zz), :], wu[...], preferred_element_type=F32))

            @pl.when(j < turns - 1)
            def _():
                first_sums(zz)

            @pl.when(j == turns - 1)
            def _():
                down(0, range(cuts), zz)

        return carry

    lax.fori_loop(0, turns, hidden_step, 0)

    near_end = jnp.where(near_way == 0, last_z, 0)

    def finish_end(p):
        relay_half(p, near_way)
        finish(p, near_way, near_end)

    def finish_way(p, way, skip):
        def step(n, carry):
            zz = z + (nz - 1 - n) * (1 - 2 * way)

            @pl.when(zz != skip)
            def _():
                finish(p, way, zz)

            return carry

        lax.fori_loop(0, nz - 1, step, 0)

    def finish_outer(ps, start):
        def step(n, carry):
            for p in ps:
                finish(p, near_way, z + (nz - 1 - n) * (1 - 2 * near_way))
            return carry

        lax.fori_loop(start, nz - 1, step, 0)

    def far_down(s, hold=False):
        far_ready(2, s)

        def step(t, carry):
            chip = 1 + t // turns
            j = t % turns
            _, zz = owner(j)

            @pl.when(inside(zz))
            def _():
                down(chip, (s,), zz)

                @pl.when(j < (turns - 3 if hold else turns - 1))
                def _():
                    send_sums(chip * cuts + s, zz)
                    send_halves((chip * cuts + s,), zz)

            return carry

        lax.fori_loop(0, (chips - 1) * turns, step, 0)

    rest = [c * cuts + s for s in range(cuts) for c in range(1, chips)]

    def own_sums(ps):
        for p in ps:
            sum_x(p, z, 0).start()

            @pl.when(middle(z))
            def _():
                sum_x(p, z, 1).start()

    def drain_first():
        for d in steps:
            kv_send(0, d).wait_send()
        for d in range(chips):
            kv_relay(0, d).wait_send()

        @pl.when(o < n_out - 1)
        def _():
            for d in range(chips):
                kv_send(1, d).wait_send()

        @pl.when(o > 0)
        def _():
            for d in range(chips):
                kv_relay(1, d).wait_send()

        for link in range(3):
            def sent(link=link):
                first_attended(link).wait_send()
                whole = tok_rows(z, x)
                remote(whole, whole, r_snd.at[link], r_rcv.at[link], target(link)).wait_send()

            send_link(link, sent)
        for way in range(2):
            step = 1 - 2 * way

            @pl.when(inside(z + step))
            def _():
                tok_half(way, x_peer).wait_send()
                for h in range(1, nz - 1):
                    @pl.when(inside(z - step * h))
                    def _():
                        whole = tok_rows(z, x)
                        remote(whole, whole, z_snd.at[way, h - 1], z_rcv.at[0, way, h - 1], x_peer).wait_send()
        for zz in range(nz):
            @pl.when(z != zz)
            def _():
                if zz == 0 or zz == last_z:
                    tok_x_end(zz, x).wait_send()
                else:
                    whole = tok_rows(zz, x)
                    remote(whole, whole, x_snd.at[zz], x_rcv.at[zz], x_peer).wait_send()

    def drain_sums():
        for way in range(2):
            @pl.when(inside(z + 1 - 2 * way))
            def _():
                halves_out = h_out.at[:, way]
                remote(halves_out, halves_out, rh_snd.at[way], rh_rcv.at[0, way], x_peer).wait_send()
        first = x_out.at[:, :, pl.ds(0, keep)]
        remote(first, first, rx_snd.at[0], rx_rcv.at[0, 0], x_peer).wait_send()

        def second(n):
            there = x_out.at[:, pl.ds(0, n), pl.ds(keep, rows - keep)]
            remote(there, there, rx_snd.at[1], rx_rcv.at[0, 0], x_peer).wait_send()

        pl.when(middle(z))(lambda: second(nz - 2))
        pl.when(jnp.logical_not(middle(z)))(lambda: second(nz - 1))
        others = z_out.at[:, pl.ds(0, nz - 1)]
        remote(others, others, rz_snd, rz_rcv.at[0, 0], x_peer).wait_send()

    @pl.when(middle(z))
    def _():
        own_sums(range(cuts))
        for p in range(cuts):
            relay_half(p, near_way)
        relay_weight(2, 0)
        far_down(0)
        for p in range(cuts):
            relay_half(p, 1 - near_way)
        for p in range(cuts):
            finish_way(p, near_way, near_end)
        for p in range(cuts):
            finish(p, near_way, near_end)
        for s in range(1, cuts):
            relay_weight(2, s)
            far_down(s)
        own_sums(rest)
        for p in range(cuts):
            finish_way(p, 1 - near_way, -1)
        for p in rest:
            finish_end(p)
        for p in rest:
            relay_half(p, 1 - near_way)
        for p in rest:
            finish_way(p, 1 - near_way, -1)
            finish_way(p, near_way, near_end)

    @pl.when(jnp.logical_not(middle(z)))
    def _():
        finish(0, near_way, near_end)
        relay_weight(2, 0)
        for p in range(1, cuts):
            finish(p, near_way, near_end)
        far_down(0, True)
        finish_outer((0,), 2)
        for s in range(1, cuts):
            relay_weight(2, s)
            for c in range(1, chips):
                finish_end(c * cuts + s - 1)
            far_down(s, True)
        for p in rest:
            send_sums(p, z + 1 - 2 * near_way)
        own_sums(range(parts_n))
        for c in range(1, chips):
            finish_end(c * cuts + cuts - 1)
        if cuts > 1:
            finish_outer(range(1, cuts), 2)
        finish_outer(rest, 1)

    drain_first()
    for k in range(3):
        drain_weights(k)
    for p in range(parts_n):
        own_half(p)
    for p in range(parts_n):
        for way in range(2):
            @pl.when(inside(z - (1 - 2 * way)))
            def _():
                sum_z(p, way, z, True).wait_recv()
                own_part[p, z] = own_part[p, z] + z_in[p, way, z].astype(F32)
        sum_x_whole(p, z).wait_recv()
        for q in range(2):
            source = 2 * columns_of(p // cuts) + q
            here = pl.ds(pl.multiple_of(source * width + (p % cuts) * cw, cw), cw)
            cols = slice(q * cw, (q + 1) * cw)
            out_ref[:, here] = (
                after[:, here].astype(F32)
                + (own_part[p, z, :, cols] + x_in[p, z, :, cols].astype(F32))).astype(BF16)

    drain_sums()


def per_device(n_out, n_in, resid, queries, keyvals, piece_order, out_proj, mlp_gain, w_gate, w_up, w_down):
    rows, model = resid.shape
    units, width = w_down.shape
    nz, chips = n_out // 2, n_in // 2
    cuts = max(1, width // 256)
    pieces_w = (max(1, 8 // n_in), max(1, 32 // n_in), cuts)
    cw = width // cuts
    parts_n = chips * cuts
    early = rows * 3 // 4
    dma = pltpu.SemaphoreType.DMA
    vmem = pl.BlockSpec(memory_space=pltpu.VMEM)
    hbm = pl.BlockSpec(memory_space=pl.ANY)
    keep = rows * KEEP // 128
    half = rows - keep
    return pl.pallas_call(
        functools.partial(layer_kernel, n_out, n_in, cuts, pieces_w, early, keep),
        out_shape=pltpu.VMEM(resid.shape, BF16),
        in_specs=[hbm] * 9,
        out_specs=vmem,
        scratch_shapes=[
            pltpu.SMEM(piece_order.shape, jnp.int32),
            pltpu.VMEM(resid.shape, BF16),
            pltpu.VMEM(queries.shape, BF16),
            pltpu.VMEM(out_proj.shape, BF16),
            pltpu.VMEM((1, model), F32),
            dma((5,)),
            pltpu.VMEM((2 * n_in * rows, keyvals.shape[1]), BF16),
            pltpu.VMEM((model, units), BF16),
            pltpu.VMEM((model, units), BF16),
            pltpu.VMEM((n_in, cuts, units, cw), BF16),
            pltpu.VMEM((n_out * rows, model), BF16),
            pltpu.VMEM((rows, model), BF16),
            pltpu.VMEM(queries.shape, BF16),
            pltpu.VMEM((3, early, model), BF16),
            pltpu.VMEM((3, early, queries.shape[1]), BF16),
            pltpu.VMEM((n_out * rows, units), F32),
            pltpu.VMEM((2 * rows, units), F32),
            pltpu.VMEM((n_out * rows, units), BF16),
            pltpu.VMEM((parts_n, nz, rows, 2 * cw), BF16),
            pltpu.VMEM((parts_n, nz, rows, 2 * cw), BF16),
            pltpu.VMEM((parts_n, nz, rows, 2 * cw), F32),
            pltpu.VMEM((parts_n, nz, rows, 2 * cw), BF16),
            pltpu.VMEM((parts_n, 2, nz, rows, 2 * cw), BF16),
            pltpu.VMEM((parts_n, 3, half, 2 * cw), F32),
            pltpu.VMEM((parts_n, 2, half, 2 * cw), BF16),
            pltpu.VMEM((parts_n, 2, half, 2 * cw), BF16),
            dma(()), dma((2, chips)), dma((2, chips)), dma((2, n_in)),
            dma((3,)), dma((3,)), dma((3,)), dma((3, chips - 1)), dma((3, chips - 1)),
            dma((chips - 1, 2, sum(pieces_w))),
            dma((3,)), dma((3,)), dma((3,)), dma((3,)), dma((3,)),
            dma((2, nz - 2)), dma((2, 2, nz - 2)), dma((2,)), dma((2,)), dma((nz,)), dma((nz,)),
            dma((2,)), dma((parts_n, nz)), dma(()), dma((parts_n, nz + 1)),
            dma((2,)), dma((parts_n, 2)),
        ],
        compiler_params=pltpu.CompilerParams(
            collective_id=0, has_side_effects=True, vmem_limit_bytes=63000 * 1024
        ),
        name="layer",
    )(piece_order, resid, queries, keyvals, out_proj, mlp_gain.reshape(1, -1), w_gate, w_up, w_down)


def solution(mesh):
    placed = (
        P(("outer", "inner"), None),
        P(("outer", "inner"), None),
        P(("outer", "inner"), None),
        P(),
        P(),
        P(),
        P("inner", "outer"),
        P("inner", "outer"),
        P("outer", "inner"),
    )
    return jax.shard_map(
        functools.partial(per_device, mesh.shape["outer"], mesh.shape["inner"]),
        mesh=mesh,
        in_specs=placed,
        out_specs=P(("outer", "inner"), None),
        check_vma=False,
    )
```

```python
import functools

import jax
import jax.numpy as jnp
from jax import lax
from jax.experimental import pallas as pl
from jax.experimental.pallas import tpu as pltpu
from jax.sharding import PartitionSpec as P

MESH = pl.DeviceIdType.MESH
F32 = jnp.float32
BF16 = jnp.bfloat16
EPS = 1e-05
KEEP = 80


def layer_kernel(
    n_out, n_in, cuts, pieces_w, early, keep,
    order_hbm, resid_hbm, query_hbm, kv_ref, proj_hbm, gain_hbm, wg_ref, wu_ref, wd_ref,
    out_ref,
    order_ref, resid_ref, query_ref, proj_ref, gain_ref, in_sem,
    kv_all, wg, wu, wd, tok, after, att_own, res_in, att_in, gates, upper, hidden,
    x_out, x_in, own_part, z_out, z_in, h_own, h_out, h_in,
    kv_loc, kv_snd, kv_relay_snd, kv_rcv, w_loc, w_pair_snd, w_pair_rcv, w_snd, w_relay_snd, w_rcv,
    r_snd, r_rcv, a_snd, a_rcv, n_rcv, z_snd, z_rcv, g_snd, g_rcv, x_snd, x_rcv,
    rx_snd, rx_rcv, rz_snd, rz_rcv, rh_snd, rh_rcv,
):
    o = lax.axis_index("outer")
    i = lax.axis_index("inner")
    nz = n_out // 2
    z, x = o // 2, o % 2
    core = i % 2
    partner = i + 1 - 2 * core
    x_peer = (z * 2 + 1 - x, i)
    core_peer = (o, partner)
    rows = resid_hbm.shape[0]
    head = kv_ref.shape[1] // 2
    heads = query_ref.shape[1] // head
    pieces = order_ref.shape[0]
    block = n_in * rows
    span = block // pieces
    depth = wg_ref.shape[0]
    units, width = wd_ref.shape
    chips = n_in // 2
    parts_n = chips * cuts
    cw = width // cuts
    keep_t = rows // 2
    last_z = nz - 1

    def remote(src, dst, ssem, rsem, device):
        return pltpu.make_async_remote_copy(
            src_ref=src, dst_ref=dst, send_sem=ssem, recv_sem=rsem,
            device_id=device, device_id_type=MESH,
        )

    def inside(zz):
        return jnp.logical_and(zz >= 0, zz < nz)

    def middle(zz):
        return jnp.logical_and(zz > 0, zz < last_z)

    def z_device(zz):
        return (zz * 2 + x, i)

    barrier = pltpu.get_barrier_semaphore()
    after_o, before_o = lax.rem(o + 1, n_out), lax.rem(o + n_out - 1, n_out)

    def greet(device):
        pl.semaphore_signal(barrier, inc=1, device_id=device, device_id_type=MESH)

    for d in range(1, n_in):
        greet((o, lax.rem(i + d, n_in)))
    greet(x_peer)
    pl.when(z > 0)(lambda: greet(z_device(z - 1)))
    pl.when(z < last_z)(lambda: greet(z_device(z + 1)))

    @pl.when(o > 0)
    def _():
        for d in range(chips):
            greet((before_o, lax.rem(i + 2 * d, n_in)))

    loads = [
        pltpu.make_async_copy(src, dst, in_sem.at[n])
        for n, (src, dst) in enumerate((
            (order_hbm, order_ref), (query_hbm, query_ref), (resid_hbm, resid_ref), (proj_hbm, proj_ref), (gain_hbm, gain_ref)))
    ]
    for load in loads:
        load.start()

    pl.semaphore_wait(
        barrier, n_in + jnp.where(z > 0, 1, 0) + jnp.where(z < last_z, 1, 0)
        + jnp.where(o < n_out - 1, chips, 0))

    own_rows = pl.ds(pl.multiple_of(i * rows, rows), rows)
    kv_copy = pltpu.make_async_copy(kv_ref, kv_all.at[own_rows], kv_loc)
    kv_copy.start()

    steps = range(1, chips)

    def kv_slot(part, q):
        return kv_all.at[pl.ds(pl.multiple_of(part * block + q * rows, rows), rows)]

    def kv_send(part, d):
        return remote(kv_ref, kv_slot(part, i), kv_snd.at[part, d], kv_rcv.at[part, i],
                      (after_o if part else o, lax.rem(i + 2 * d, n_in)))

    def kv_relay(part, d):
        q = lax.rem(i + n_in - 2 * d, n_in)
        src = kv_ref if part == 0 and d == 0 else kv_slot(part, q)
        return remote(src, kv_slot(part, q), kv_relay_snd.at[part, d], kv_rcv.at[part, q], core_peer)

    def kv_arrived(part, q):
        here = kv_slot(part, q)
        remote(here, here, kv_relay_snd.at[part, 0], kv_rcv.at[part, q], core_peer).wait_recv()

    for d in steps:
        kv_send(0, d).start()

    @pl.when(o < n_out - 1)
    def _():
        for d in range(chips):
            kv_send(1, d).start()

    kv_relay(0, 0).start()

    def tok_rows(zz, xx, start=0, size=rows):
        return tok.at[pl.ds(pl.multiple_of((zz * 2 + xx) * rows + start, 16), size)]

    def target(link):
        if isinstance(link, int):
            return x_peer if link == 2 else z_device(z + 1 - 2 * link)
        return z_device(z + 1 - 2 * link)

    def first_resid(link, to=None):
        return remote(resid_hbm.at[pl.ds(0, early)], res_in.at[link], r_snd.at[link], r_rcv.at[link],
                      to or target(link))

    def first_attended(link, to=None):
        return remote(att_own.at[pl.ds(0, early)], att_in.at[link], a_snd.at[link], a_rcv.at[link],
                      to or target(link))

    def first_normed(link, source=None, to=None):
        here = tok_rows(*(source or (z, x)), early, rows - early)
        return remote(here, here, r_snd.at[link], n_rcv.at[link], to or target(link))

    def send_link(link, act):
        if link == 2:
            act()
        else:
            pl.when(inside(z + 1 - 2 * link))(act)

    for link in range(3):
        send_link(link, lambda link=link: first_resid(link).start())

    def slot(k, q, s):
        if k == 2:
            return wd.at[q, s]
        full = wg if k == 0 else wu
        size = depth // pieces_w[k]
        return full.at[pl.ds(pl.multiple_of(q * depth + s * size, size), size)]

    srcs = (wg_ref, wu_ref, wd_ref)

    def w_src(k, s):
        if k == 2:
            return wd_ref.at[:, pl.ds(s * cw, cw)]
        size = depth // pieces_w[k]
        return srcs[k].at[pl.ds(s * size, size)]

    def w_parts(k):
        return pieces_w[k]

    def w_index(k, s):
        return sum(pieces_w[:k]) + s

    def shard(k, q):
        if k == 2:
            return wd.at[q]
        full = wg if k == 0 else wu
        return full.at[pl.ds(pl.multiple_of(q * depth, depth), depth)]

    def far(d):
        return lax.rem(i + n_in - 2 * d, n_in)

    def w_far(k, d, s):
        return remote(w_src(k, s), slot(k, i, s), w_snd.at[k, d - 1], w_rcv.at[d - 1, 0, w_index(k, s)],
                      (o, lax.rem(i + 2 * d, n_in)))

    def w_relay(k, d, s):
        here = slot(k, far(d), s)
        return remote(here, here, w_relay_snd.at[k, d - 1], w_rcv.at[d - 1, 1, w_index(k, s)], core_peer)

    def w_pair(k, s):
        return remote(w_src(k, s), slot(k, i, s), w_pair_snd.at[k], w_pair_rcv.at[k], core_peer)

    def w_local(k, s):
        return pltpu.make_async_copy(w_src(k, s), slot(k, i, s), w_loc.at[k])

    def near_ready(k):
        mine, other = shard(k, i), shard(k, partner)
        pltpu.make_async_copy(mine, mine, w_loc.at[k]).wait()
        remote(other, other, w_pair_snd.at[k], w_pair_rcv.at[k], core_peer).wait_recv()

    def far_ready(k, s):
        for d in steps:
            here = slot(k, lax.rem(partner + n_in - 2 * d, n_in), s)
            remote(here, here, w_relay_snd.at[k, d - 1], w_rcv.at[d - 1, 1, w_index(k, s)], core_peer).wait_recv()

    def relay_weight(k, s):
        for d in steps:
            here = slot(k, far(d), s)
            remote(here, here, w_relay_snd.at[k, d - 1], w_rcv.at[d - 1, 0, w_index(k, s)], core_peer).wait_recv()
            w_relay(k, d, s).start()

    def weight_ready(k):
        near_ready(k)
        for s in range(w_parts(k)):
            far_ready(k, s)

    def drain_weights(k):
        mine = shard(k, i)
        remote(mine, mine, w_pair_snd.at[k], w_pair_rcv.at[k], core_peer).wait_send()
        for d in steps:
            remote(mine, mine, w_snd.at[k, d - 1], w_pair_rcv.at[k], core_peer).wait_send()
            remote(mine, mine, w_relay_snd.at[k, d - 1], w_pair_rcv.at[k], core_peer).wait_send()

    for k in range(3):
        for s in range(w_parts(k)):
            for d in steps:
                w_far(k, d, s).start()
    for k in range(3):
        for s in range(w_parts(k)):
            w_pair(k, s).start()
            w_local(k, s).start()

    loads[0].wait()
    lane = lax.broadcasted_iota(jnp.int32, (rows, block), 1)
    key_pos = jnp.zeros((rows, block), jnp.int32)
    for p in range(pieces):
        key_pos = jnp.where(lane // span == p, order_ref[p] * span + lane % span, key_pos)
    row = lax.broadcasted_iota(jnp.int32, (rows, block), 0)
    query_pos = jnp.zeros((rows, block), jnp.int32)
    for p in range(rows // span):
        query_pos = jnp.where(
            row // span == p, order_ref[i * (rows // span) + p] * span + row % span, query_pos)
    own_visible = key_pos <= query_pos
    before_visible = (jnp.zeros((rows, block), jnp.int32) + o) > 0

    @pl.when(o == 0)
    def _():
        kv_all[block:, :] = jnp.zeros((block, 2 * head), BF16)

    for zz in (0, last_z):
        @pl.when(z != zz)
        def _():
            x_in[:, zz, keep:, :] = jnp.zeros((parts_n, rows - keep, 2 * cw), BF16)

    for d in steps:
        kv_arrived(0, lax.rem(i + n_in - 2 * d, n_in))
        kv_relay(0, d).start()

    @pl.when(o > 0)
    def _():
        for d in range(chips):
            kv_arrived(1, lax.rem(i + n_in - 2 * d, n_in))
            kv_relay(1, d).start()

    kv_copy.wait()
    for d in range(chips):
        kv_arrived(0, lax.rem(partner + 2 * d, n_in))

    @pl.when(o > 0)
    def _():
        for d in range(chips):
            kv_arrived(1, lax.rem(partner + 2 * d, n_in))

    loads[1].wait()
    parts = []
    nt = (((1,), (1,)), ((), ()))
    for h in range(heads):
        query = query_ref[:, h * head:(h + 1) * head]
        own_score = lax.dot_general(
            query, kv_all[:block, :head], nt, preferred_element_type=F32) * head ** (-0.5)
        before_score = lax.dot_general(
            query, kv_all[block:, :head], nt, preferred_element_type=F32) * head ** (-0.5)
        own_score = jnp.where(own_visible, own_score, -1e30)
        before_score = jnp.where(before_visible, before_score, -1e30)
        top = jnp.maximum(
            jnp.max(own_score, axis=1, keepdims=True), jnp.max(before_score, axis=1, keepdims=True))
        own_w = jnp.where(own_visible, jnp.exp(own_score - top), 0.0)
        before_w = jnp.where(before_visible, jnp.exp(before_score - top), 0.0)
        total = jnp.sum(own_w, axis=1, keepdims=True) + jnp.sum(before_w, axis=1, keepdims=True)
        mixed = jnp.dot(own_w.astype(BF16), kv_all[:block, head:], preferred_element_type=F32)
        mixed += jnp.dot(before_w.astype(BF16), kv_all[block:, head:], preferred_element_type=F32)
        parts.append((mixed / total).astype(BF16))
    att_own[...] = jnp.concatenate(parts, axis=1)
    for link in range(3):
        send_link(link, lambda link=link: first_attended(link).start())

    for load in loads[2:]:
        load.wait()

    def normed_of(resid, attended):
        after_attn = (
            resid.astype(F32) + jnp.dot(attended, proj_ref[...], preferred_element_type=F32)
        ).astype(BF16)
        wide = after_attn.astype(F32)
        normed = wide * lax.rsqrt(jnp.mean(wide * wide, axis=1, keepdims=True) + EPS) * gain_ref[...]
        return after_attn, normed.astype(BF16)

    after_attn, normed = normed_of(resid_ref[...], att_own[...])
    after[...] = after_attn
    tok_rows(z, x)[...] = normed
    for link in range(3):
        send_link(link, lambda link=link: first_normed(link).start())

    def part_rows(zz, xx, part):
        return tok_rows(zz, xx, part * early, rows - early if part else early)

    def tok_z(way, h, part):
        step = 1 - 2 * way
        here = part_rows(z - step * h, x, part)
        return remote(here, here, z_snd.at[way, h - 1], z_rcv.at[part, way, h - 1], z_device(z + step))

    def tok_z_arrived(way, h, part):
        here = part_rows(z - (1 - 2 * way) * (h + 1), x, part)
        remote(here, here, z_snd.at[way, h - 1], z_rcv.at[part, way, h - 1], x_peer).wait_recv()

    def tok_x(zz, xx, part):
        here = part_rows(zz, xx, part)
        return remote(here, here, x_snd.at[zz], x_rcv.at[zz], x_peer)

    def tok_x_end(zz, xx):
        here = tok_rows(zz, xx, 0, keep_t)
        return remote(here, here, x_snd.at[zz], x_rcv.at[zz], x_peer)

    def send_x(zz, part):
        @pl.when(middle(zz))
        def _():
            tok_x(zz, x, part).start()

        if part == 0:
            @pl.when(jnp.logical_not(middle(zz)))
            def _():
                tok_x_end(zz, x).start()

    def tok_half(way, to):
        here = tok_rows(last_z if way else 0, 1 - x, keep_t, rows - keep_t)
        return remote(here, here, g_snd.at[way], g_rcv.at[way], to)

    def from_origin(way):
        return last_z - z if way else z

    near_way = jnp.where(2 * z < nz, 0, 1)

    def absorb(link, zz, xx):
        first_resid(link, x_peer).wait_recv()
        first_attended(link, x_peer).wait_recv()
        tok_rows(zz, xx, 0, early)[...] = normed_of(res_in[link], att_in[link])[1]

    def hop(h, part, way):
        step = 1 - 2 * way
        source = z - step * (h + 1)

        @pl.when(inside(source))
        def _():
            if h > 0:
                tok_z_arrived(way, h, part)
            elif part == 0:
                absorb(way, source, x)
            else:
                first_normed(way, (source, x), x_peer).wait_recv()
            if h < nz - 2:
                @pl.when(inside(z + step))
                def _():
                    tok_z(way, h + 1, part).start()

            send_x(source, part)

    def pair_of(j):
        return z + ((j + 1) // 2) * (1 - 2 * (j % 2))

    def both_rows(zz):
        return pl.ds(pl.multiple_of(zz * 2 * rows, 2 * rows), 2 * rows)

    def make_gate(zz):
        here = both_rows(zz)
        gates[here, :] = jnp.dot(tok[here, :], wg[...], preferred_element_type=F32)

    def other_x_arrived(zz):
        @pl.when(middle(zz))
        def _():
            whole = tok_rows(zz, 1 - x)
            remote(whole, whole, x_snd.at[zz], x_rcv.at[zz], x_peer).wait_recv()

        @pl.when(jnp.logical_not(middle(zz)))
        def _():
            tok_x_end(zz, 1 - x).wait_recv()

    def gate_step(j, carry):
        zz = pair_of(j)

        @pl.when(inside(zz))
        def _():
            @pl.when(j > 0)
            def _():
                other_x_arrived(zz)

            make_gate(zz)

        return carry

    first_zz = z + (nz - 2) * (1 - 2 * near_way)

    def upward_over(zz, shards):
        total = None
        for q in shards:
            here = pl.ds(pl.multiple_of(q * depth, depth), depth)
            part = jnp.dot(tok[both_rows(zz), here], wu[here, :], preferred_element_type=F32)
            total = part if total is None else total + part
        return total

    relays = [(k, s) for k in range(2) for s in range(pieces_w[k])]

    def relay_to(n):
        while relays and n > 0:
            k, s = relays.pop(0)
            relay_weight(k, s)
            n -= 1

    def halves(h):
        for way in range(2):
            @pl.when(from_origin(way) == h + 1)
            def _():
                tok_half(way, x_peer).wait_recv()

                @pl.when(inside(z + 1 - 2 * way))
                def _():
                    tok_half(way, z_device(z + 1 - 2 * way)).start()

    for h in range(nz - 1):
        for part in range(2):
            hop(h, part, 1 - near_way)
            hop(h, part, near_way)
        if h == 0:
            absorb(2, z, 1 - x)
            first_normed(2, (z, 1 - x), x_peer).wait_recv()
            for way in range(2):
                @pl.when(from_origin(way) == 0)
                def _():
                    tok_half(way, z_device(z + 1 - 2 * way)).start()
            relay_to((pieces_w[0] + 1) // 2)
        elif h == 1:
            relay_to(pieces_w[0] // 2)
            weight_ready(0)
            lax.fori_loop(0, 3, gate_step, 0)
            relay_to((pieces_w[1] + 3) // 4)
        else:
            relay_to((pieces_w[1] + 7) // 8)
            lax.fori_loop(2 * h - 1, 2 * h + 1, gate_step, 0)
        if h == nz - 2:
            relay_to(len(relays) - 1)
            near_ready(1)

            @pl.when(inside(first_zz))
            def _():
                upper[...] = upward_over(first_zz, [i, partner])

        halves(h)
    relay_to(len(relays))

    def columns_of(chip):
        return lax.rem(i // 2 + chips - chip, chips)

    def end_way(zz):
        return jnp.where(zz == last_z, 0, 1)

    def sum_x(p, zz, part):
        there = pl.ds(part * keep, rows - keep if part else keep)
        return remote(x_out.at[p, zz, there], x_in.at[p, zz, there], rx_snd.at[part],
                      rx_rcv.at[p, zz], x_peer)

    def sum_x_whole(p, zz):
        return remote(x_out.at[p, zz], x_in.at[p, zz], rx_snd.at[0], rx_rcv.at[p, zz], x_peer)

    def sum_z(p, way, zz, here=False):
        step = jnp.where(inside(z + 1 - 2 * way), 1 - 2 * way, 0)
        off = 0 if here else step
        return remote(z_out.at[p, zz], z_in.at[p, way, zz], rz_snd,
                      rz_rcv.at[p, jnp.where(jnp.logical_and(way == 1, zz == z + off), nz, zz)],
                      z_device(z + step))

    def sum_half(p, way, to):
        return remote(h_out.at[p, way], h_in.at[p, way], rh_snd.at[way], rh_rcv.at[p, way], to)

    def next_z(way):
        return z_device(jnp.clip(z + 1 - 2 * way, 0, last_z))

    def down(chip, cs, zz):
        def half(xx):
            return hidden[pl.ds(pl.multiple_of((zz * 2 + xx) * rows, rows), rows), :]

        both = jnp.concatenate([half(1 - x), half(x)], axis=0)
        for c in cs:
            p = chip * cuts + c
            for q in range(2):
                part = jnp.dot(both, wd[2 * columns_of(chip) + q, c], preferred_element_type=F32)
                here = slice(q * cw, (q + 1) * cw)
                x_out[p, zz, :, here] = part[:rows].astype(BF16)
                own_part[p, zz, :, here] = part[rows:]
                h_own[p, jnp.where(middle(zz), 2, end_way(zz)), :, here] = part[keep:rows]

    def send_sums(p, zz):
        sum_x(p, zz, 0).start()

        @pl.when(middle(zz))
        def _():
            sum_x(p, zz, 1).start()

    def send_halves(ps, zz):
        for way in range(2):
            @pl.when(jnp.logical_and(from_origin(way) == 0, zz == (0 if way else last_z)))
            def _():
                for p in ps:
                    h_out[p, way] = h_own[p, way].astype(BF16)
                    sum_half(p, way, next_z(way)).start()

    turns = 2 * nz - 1

    def owner(j):
        way = j % 2
        return way, z + (nz - 1 - j // 2) * (1 - 2 * way)

    def finish_half(p, way):
        sum_half(p, way, x_peer).wait_recv()
        h_out[p, way] = (h_own[p, way] + h_in[p, way].astype(F32)).astype(BF16)
        sum_half(p, way, next_z(way)).start()

    def relay_half(p, way):
        @pl.when(middle(z))
        def _():
            finish_half(p, way)

    def own_half(p):
        for way in range(2):
            @pl.when(z == (0 if way else last_z))
            def _():
                sum_half(p, way, x_peer).wait_recv()
                x_out[p, z, keep:, :] = (h_own[p, way] + h_in[p, way].astype(F32)).astype(BF16)
                sum_x(p, z, 1).start()

    def finish(p, way, zz):
        more = inside(z - (1 - 2 * way))

        @pl.when(inside(zz))
        def _():
            @pl.when(middle(zz))
            def _():
                sum_x_whole(p, zz).wait_recv()

            @pl.when(jnp.logical_not(middle(zz)))
            def _():
                sum_x(p, zz, 0).wait_recv()

            @pl.when(more)
            def _():
                sum_z(p, way, zz, True).wait_recv()
                z_out[p, zz] = (
                    own_part[p, zz] + x_in[p, zz].astype(F32) + z_in[p, way, zz].astype(F32)
                ).astype(BF16)

            @pl.when(jnp.logical_not(more))
            def _():
                z_out[p, zz] = (own_part[p, zz] + x_in[p, zz].astype(F32)).astype(BF16)

            sum_z(p, way, zz).start()

    near_ready(2)
    def make_hidden(zz, upward):
        here = both_rows(zz)
        gate = gates[here, :]
        hidden[here, :] = (gate / (1.0 + jnp.exp(-gate)) * upward).astype(BF16)

    def first_sums(zz):
        for p in range(cuts):
            down(0, (p,), zz)
            send_sums(p, zz)
            send_halves((p,), zz)

    @pl.when(inside(first_zz))
    def _():
        upper[...] += upward_over(first_zz, [lax.rem(i + 2 * d, n_in) for d in steps])

    @pl.when(jnp.logical_and(jnp.logical_not(middle(z)), core == 1))
    def _():
        other_x_arrived(last_z - z)
        make_gate(last_z - z)

    for s in range(pieces_w[1]):
        far_ready(1, s)

    @pl.when(inside(first_zz))
    def _():
        for xx in (1 - x, x):
            here = pl.ds(pl.multiple_of((first_zz * 2 + xx) * rows, rows), rows)
            upward = upper[pl.ds(pl.multiple_of(xx * rows, rows), rows), :]
            for d in steps:
                q = lax.rem(partner + 2 * d, n_in)
                there = pl.ds(pl.multiple_of(q * depth, depth), depth)
                upward += jnp.dot(tok[here, there], wu[there, :], preferred_element_type=F32)
            gate = gates[here, :]
            hidden[here, :] = (gate / (1.0 + jnp.exp(-gate)) * upward).astype(BF16)
            for q in range(2):
                part = jnp.dot(hidden[here, :], wd[2 * columns_of(0) + q, 0], preferred_element_type=F32)
                cols = slice(q * cw, (q + 1) * cw)
                if xx is x:
                    own_part[0, first_zz, :, cols] = part
                else:
                    x_out[0, first_zz, :, cols] = part.astype(BF16)
                    h_own[0, jnp.where(middle(first_zz), 2, end_way(first_zz)), :, cols] = part[keep:]
            if xx is not x:
                send_sums(0, first_zz)
        for p in range(1, cuts):
            down(0, (p,), first_zz)
            send_sums(p, first_zz)

    def hidden_step(j, carry):
        _, zz = owner(j)

        @pl.when(jnp.logical_and(j == 3, jnp.logical_not(middle(z))))
        def _():
            finish(0, near_way, first_zz)

        @pl.when(jnp.logical_and(j == turns - 1, jnp.logical_not(middle(z))))
        def _():
            for p in range(1, cuts):
                finish(p, near_way, first_zz)

        @pl.when(jnp.logical_and(inside(zz), zz != first_zz))
        def _():
            @pl.when(jnp.logical_and(j < 2, core == 0))
            def _():
                other_x_arrived(zz)
                make_gate(zz)

            make_hidden(zz, jnp.dot(tok[both_rows(zz), :], wu[...], preferred_element_type=F32))

            @pl.when(j < turns - 1)
            def _():
                first_sums(zz)

            @pl.when(j == turns - 1)
            def _():
                down(0, range(cuts), zz)

        return carry

    lax.fori_loop(0, turns, hidden_step, 0)

    near_end = jnp.where(near_way == 0, last_z, 0)

    def finish_end(p):
        relay_half(p, near_way)
        finish(p, near_way, near_end)

    def finish_way(p, way, skip):
        def step(n, carry):
            zz = z + (nz - 1 - n) * (1 - 2 * way)

            @pl.when(zz != skip)
            def _():
                finish(p, way, zz)

            return carry

        lax.fori_loop(0, nz - 1, step, 0)

    def finish_outer(ps, start):
        def step(n, carry):
            for p in ps:
                finish(p, near_way, z + (nz - 1 - n) * (1 - 2 * near_way))
            return carry

        lax.fori_loop(start, nz - 1, step, 0)

    def far_down(s, hold=False):
        far_ready(2, s)

        def step(t, carry):
            chip = 1 + t // turns
            j = t % turns
            _, zz = owner(j)

            @pl.when(inside(zz))
            def _():
                down(chip, (s,), zz)

                @pl.when(j < (turns - 3 if hold else turns - 1))
                def _():
                    send_sums(chip * cuts + s, zz)
                    send_halves((chip * cuts + s,), zz)

            return carry

        lax.fori_loop(0, (chips - 1) * turns, step, 0)

    rest = [c * cuts + s for s in range(cuts) for c in range(1, chips)]

    def own_sums(ps):
        for p in ps:
            sum_x(p, z, 0).start()

            @pl.when(middle(z))
            def _():
                sum_x(p, z, 1).start()

    def drain_first():
        for d in steps:
            kv_send(0, d).wait_send()
        for d in range(chips):
            kv_relay(0, d).wait_send()

        @pl.when(o < n_out - 1)
        def _():
            for d in range(chips):
                kv_send(1, d).wait_send()

        @pl.when(o > 0)
        def _():
            for d in range(chips):
                kv_relay(1, d).wait_send()

        for link in range(3):
            def sent(link=link):
                first_attended(link).wait_send()
                whole = tok_rows(z, x)
                remote(whole, whole, r_snd.at[link], r_rcv.at[link], target(link)).wait_send()

            send_link(link, sent)
        for way in range(2):
            step = 1 - 2 * way

            @pl.when(inside(z + step))
            def _():
                tok_half(way, x_peer).wait_send()
                for h in range(1, nz - 1):
                    @pl.when(inside(z - step * h))
                    def _():
                        whole = tok_rows(z, x)
                        remote(whole, whole, z_snd.at[way, h - 1], z_rcv.at[0, way, h - 1], x_peer).wait_send()
        for zz in range(nz):
            @pl.when(z != zz)
            def _():
                if zz == 0 or zz == last_z:
                    tok_x_end(zz, x).wait_send()
                else:
                    whole = tok_rows(zz, x)
                    remote(whole, whole, x_snd.at[zz], x_rcv.at[zz], x_peer).wait_send()

    def drain_sums():
        for way in range(2):
            @pl.when(inside(z + 1 - 2 * way))
            def _():
                halves_out = h_out.at[:, way]
                remote(halves_out, halves_out, rh_snd.at[way], rh_rcv.at[0, way], x_peer).wait_send()
        first = x_out.at[:, :, pl.ds(0, keep)]
        remote(first, first, rx_snd.at[0], rx_rcv.at[0, 0], x_peer).wait_send()

        def second(n):
            there = x_out.at[:, pl.ds(0, n), pl.ds(keep, rows - keep)]
            remote(there, there, rx_snd.at[1], rx_rcv.at[0, 0], x_peer).wait_send()

        pl.when(middle(z))(lambda: second(nz - 2))
        pl.when(jnp.logical_not(middle(z)))(lambda: second(nz - 1))
        others = z_out.at[:, pl.ds(0, nz - 1)]
        remote(others, others, rz_snd, rz_rcv.at[0, 0], x_peer).wait_send()

    @pl.when(middle(z))
    def _():
        own_sums(range(cuts))
        for p in range(cuts):
            relay_half(p, near_way)
        relay_weight(2, 0)
        far_down(0)
        for p in range(cuts):
            relay_half(p, 1 - near_way)
        for p in range(cuts):
            finish_way(p, near_way, near_end)
        for p in range(cuts):
            finish(p, near_way, near_end)
        for s in range(1, cuts):
            relay_weight(2, s)
            far_down(s)
        own_sums(rest)
        for p in range(cuts):
            finish_way(p, 1 - near_way, -1)
        for p in rest:
            finish_end(p)
        for p in rest:
            relay_half(p, 1 - near_way)
        for p in rest:
            finish_way(p, 1 - near_way, -1)
            finish_way(p, near_way, near_end)

    @pl.when(jnp.logical_not(middle(z)))
    def _():
        finish(0, near_way, near_end)
        relay_weight(2, 0)
        for p in range(1, cuts):
            finish(p, near_way, near_end)
        far_down(0, True)
        finish_outer((0,), 2)
        for s in range(1, cuts):
            relay_weight(2, s)
            for c in range(1, chips):
                finish_end(c * cuts + s - 1)
            far_down(s, True)
        for p in rest:
            send_sums(p, z + 1 - 2 * near_way)
        own_sums(range(parts_n))
        for c in range(1, chips):
            finish_end(c * cuts + cuts - 1)
        if cuts > 1:
            finish_outer(range(1, cuts), 2)
        finish_outer(rest, 1)

    drain_first()
    for k in range(3):
        drain_weights(k)
    for p in range(parts_n):
        own_half(p)
    for p in range(parts_n):
        for way in range(2):
            @pl.when(inside(z - (1 - 2 * way)))
            def _():
                sum_z(p, way, z, True).wait_recv()
                own_part[p, z] = own_part[p, z] + z_in[p, way, z].astype(F32)
        sum_x_whole(p, z).wait_recv()
        for q in range(2):
            source = 2 * columns_of(p // cuts) + q
            here = pl.ds(pl.multiple_of(source * width + (p % cuts) * cw, cw), cw)
            cols = slice(q * cw, (q + 1) * cw)
            out_ref[:, here] = (
                after[:, here].astype(F32)
                + (own_part[p, z, :, cols] + x_in[p, z, :, cols].astype(F32))).astype(BF16)

    drain_sums()


def per_device(n_out, n_in, resid, queries, keyvals, piece_order, out_proj, mlp_gain, w_gate, w_up, w_down):
    rows, model = resid.shape
    units, width = w_down.shape
    nz, chips = n_out // 2, n_in // 2
    cuts = max(1, width // 256)
    pieces_w = (max(1, 8 // n_in), max(1, 32 // n_in), cuts)
    cw = width // cuts
    parts_n = chips * cuts
    early = rows * 3 // 4
    dma = pltpu.SemaphoreType.DMA
    vmem = pl.BlockSpec(memory_space=pltpu.VMEM)
    hbm = pl.BlockSpec(memory_space=pl.ANY)
    keep = rows * KEEP // 128
    half = rows - keep
    return pl.pallas_call(
        functools.partial(layer_kernel, n_out, n_in, cuts, pieces_w, early, keep),
        out_shape=pltpu.VMEM(resid.shape, BF16),
        in_specs=[hbm] * 9,
        out_specs=vmem,
        scratch_shapes=[
            pltpu.SMEM(piece_order.shape, jnp.int32),
            pltpu.VMEM(resid.shape, BF16),
            pltpu.VMEM(queries.shape, BF16),
            pltpu.VMEM(out_proj.shape, BF16),
            pltpu.VMEM((1, model), F32),
            dma((5,)),
            pltpu.VMEM((2 * n_in * rows, keyvals.shape[1]), BF16),
            pltpu.VMEM((model, units), BF16),
            pltpu.VMEM((model, units), BF16),
            pltpu.VMEM((n_in, cuts, units, cw), BF16),
            pltpu.VMEM((n_out * rows, model), BF16),
            pltpu.VMEM((rows, model), BF16),
            pltpu.VMEM(queries.shape, BF16),
            pltpu.VMEM((3, early, model), BF16),
            pltpu.VMEM((3, early, queries.shape[1]), BF16),
            pltpu.VMEM((n_out * rows, units), F32),
            pltpu.VMEM((2 * rows, units), F32),
            pltpu.VMEM((n_out * rows, units), BF16),
            pltpu.VMEM((parts_n, nz, rows, 2 * cw), BF16),
            pltpu.VMEM((parts_n, nz, rows, 2 * cw), BF16),
            pltpu.VMEM((parts_n, nz, rows, 2 * cw), F32),
            pltpu.VMEM((parts_n, nz, rows, 2 * cw), BF16),
            pltpu.VMEM((parts_n, 2, nz, rows, 2 * cw), BF16),
            pltpu.VMEM((parts_n, 3, half, 2 * cw), F32),
            pltpu.VMEM((parts_n, 2, half, 2 * cw), BF16),
            pltpu.VMEM((parts_n, 2, half, 2 * cw), BF16),
            dma(()), dma((2, chips)), dma((2, chips)), dma((2, n_in)),
            dma((3,)), dma((3,)), dma((3,)), dma((3, chips - 1)), dma((3, chips - 1)),
            dma((chips - 1, 2, sum(pieces_w))),
            dma((3,)), dma((3,)), dma((3,)), dma((3,)), dma((3,)),
            dma((2, nz - 2)), dma((2, 2, nz - 2)), dma((2,)), dma((2,)), dma((nz,)), dma((nz,)),
            dma((2,)), dma((parts_n, nz)), dma(()), dma((parts_n, nz + 1)),
            dma((2,)), dma((parts_n, 2)),
        ],
        compiler_params=pltpu.CompilerParams(
            collective_id=0, has_side_effects=True, vmem_limit_bytes=63000 * 1024
        ),
        name="layer",
    )(piece_order, resid, queries, keyvals, out_proj, mlp_gain.reshape(1, -1), w_gate, w_up, w_down)


def solution(mesh):
    placed = (
        P(("outer", "inner"), None),
        P(("outer", "inner"), None),
        P(("outer", "inner"), None),
        P(),
        P(),
        P(),
        P("inner", "outer"),
        P("inner", "outer"),
        P("outer", "inner"),
    )
    return jax.shard_map(
        functools.partial(per_device, mesh.shape["outer"], mesh.shape["inner"]),
        mesh=mesh,
        in_specs=placed,
        out_specs=P(("outer", "inner"), None),
        check_vma=False,
    )
```

```python
import functools

import jax
import jax.numpy as jnp
from jax import lax
from jax.experimental import pallas as pl
from jax.experimental.pallas import tpu as pltpu
from jax.sharding import PartitionSpec as P

MESH = pl.DeviceIdType.MESH
F32 = jnp.float32
BF16 = jnp.bfloat16
EPS = 1e-05
KEEP = 80


def layer_kernel(
    n_out, n_in, cuts, pieces_w, early, keep,
    order_hbm, resid_hbm, query_hbm, kv_ref, proj_hbm, gain_hbm, wg_ref, wu_ref, wd_ref,
    out_ref,
    order_ref, resid_ref, query_ref, proj_ref, gain_ref, in_sem,
    kv_all, wg, wu, wd, tok, after, att_own, res_in, att_in, gates, upper, hidden,
    x_out, x_in, own_part, z_out, z_in, h_own, h_out, h_in,
    kv_loc, kv_snd, kv_relay_snd, kv_rcv, w_loc, w_pair_snd, w_pair_rcv, w_snd, w_relay_snd, w_rcv,
    r_snd, r_rcv, a_snd, a_rcv, n_rcv, z_snd, z_rcv, g_snd, g_rcv, x_snd, x_rcv,
    rx_snd, rx_rcv, rz_snd, rz_rcv, rh_snd, rh_rcv,
):
    o = lax.axis_index("outer")
    i = lax.axis_index("inner")
    nz = n_out // 2
    z, x = o // 2, o % 2
    core = i % 2
    partner = i + 1 - 2 * core
    x_peer = (z * 2 + 1 - x, i)
    core_peer = (o, partner)
    rows = resid_hbm.shape[0]
    head = kv_ref.shape[1] // 2
    heads = query_ref.shape[1] // head
    pieces = order_ref.shape[0]
    block = n_in * rows
    span = block // pieces
    depth = wg_ref.shape[0]
    units, width = wd_ref.shape
    chips = n_in // 2
    parts_n = chips * cuts
    cw = width // cuts
    keep_t = rows // 2
    last_z = nz - 1

    def remote(src, dst, ssem, rsem, device):
        return pltpu.make_async_remote_copy(
            src_ref=src, dst_ref=dst, send_sem=ssem, recv_sem=rsem,
            device_id=device, device_id_type=MESH,
        )

    def inside(zz):
        return jnp.logical_and(zz >= 0, zz < nz)

    def middle(zz):
        return jnp.logical_and(zz > 0, zz < last_z)

    def z_device(zz):
        return (zz * 2 + x, i)

    barrier = pltpu.get_barrier_semaphore()
    after_o, before_o = lax.rem(o + 1, n_out), lax.rem(o + n_out - 1, n_out)

    def greet(device):
        pl.semaphore_signal(barrier, inc=1, device_id=device, device_id_type=MESH)

    for d in range(1, n_in):
        greet((o, lax.rem(i + d, n_in)))
    greet(x_peer)
    pl.when(z > 0)(lambda: greet(z_device(z - 1)))
    pl.when(z < last_z)(lambda: greet(z_device(z + 1)))

    @pl.when(o > 0)
    def _():
        for d in range(chips):
            greet((before_o, lax.rem(i + 2 * d, n_in)))

    loads = [
        pltpu.make_async_copy(src, dst, in_sem.at[n])
        for n, (src, dst) in enumerate((
            (order_hbm, order_ref), (query_hbm, query_ref), (resid_hbm, resid_ref), (proj_hbm, proj_ref), (gain_hbm, gain_ref)))
    ]
    for load in loads:
        load.start()

    pl.semaphore_wait(
        barrier, n_in + jnp.where(z > 0, 1, 0) + jnp.where(z < last_z, 1, 0)
        + jnp.where(o < n_out - 1, chips, 0))

    own_rows = pl.ds(pl.multiple_of(i * rows, rows), rows)
    kv_copy = pltpu.make_async_copy(kv_ref, kv_all.at[own_rows], kv_loc)
    kv_copy.start()

    steps = range(1, chips)

    def kv_slot(part, q):
        return kv_all.at[pl.ds(pl.multiple_of(part * block + q * rows, rows), rows)]

    def kv_send(part, d):
        return remote(kv_ref, kv_slot(part, i), kv_snd.at[part, d], kv_rcv.at[part, i],
                      (after_o if part else o, lax.rem(i + 2 * d, n_in)))

    def kv_relay(part, d):
        q = lax.rem(i + n_in - 2 * d, n_in)
        src = kv_ref if part == 0 and d == 0 else kv_slot(part, q)
        return remote(src, kv_slot(part, q), kv_relay_snd.at[part, d], kv_rcv.at[part, q], core_peer)

    def kv_arrived(part, q):
        here = kv_slot(part, q)
        remote(here, here, kv_relay_snd.at[part, 0], kv_rcv.at[part, q], core_peer).wait_recv()

    for d in steps:
        kv_send(0, d).start()

    @pl.when(o < n_out - 1)
    def _():
        for d in range(chips):
            kv_send(1, d).start()

    kv_relay(0, 0).start()

    def tok_rows(zz, xx, start=0, size=rows):
        return tok.at[pl.ds(pl.multiple_of((zz * 2 + xx) * rows + start, 16), size)]

    def target(link):
        if isinstance(link, int):
            return x_peer if link == 2 else z_device(z + 1 - 2 * link)
        return z_device(z + 1 - 2 * link)

    def first_resid(link, to=None):
        return remote(resid_hbm.at[pl.ds(0, early)], res_in.at[link], r_snd.at[link], r_rcv.at[link],
                      to or target(link))

    def first_attended(link, to=None):
        return remote(att_own.at[pl.ds(0, early)], att_in.at[link], a_snd.at[link], a_rcv.at[link],
                      to or target(link))

    def first_normed(link, source=None, to=None):
        here = tok_rows(*(source or (z, x)), early, rows - early)
        return remote(here, here, r_snd.at[link], n_rcv.at[link], to or target(link))

    def send_link(link, act):
        if link == 2:
            act()
        else:
            pl.when(inside(z + 1 - 2 * link))(act)

    for link in range(3):
        send_link(link, lambda link=link: first_resid(link).start())

    def slot(k, q, s):
        if k == 2:
            return wd.at[q, s]
        full = wg if k == 0 else wu
        size = depth // pieces_w[k]
        return full.at[pl.ds(pl.multiple_of(q * depth + s * size, size), size)]

    srcs = (wg_ref, wu_ref, wd_ref)

    def w_src(k, s):
        if k == 2:
            return wd_ref.at[:, pl.ds(s * cw, cw)]
        size = depth // pieces_w[k]
        return srcs[k].at[pl.ds(s * size, size)]

    def w_parts(k):
        return pieces_w[k]

    def w_index(k, s):
        return sum(pieces_w[:k]) + s

    def shard(k, q):
        if k == 2:
            return wd.at[q]
        full = wg if k == 0 else wu
        return full.at[pl.ds(pl.multiple_of(q * depth, depth), depth)]

    def far(d):
        return lax.rem(i + n_in - 2 * d, n_in)

    def w_far(k, d, s):
        return remote(w_src(k, s), slot(k, i, s), w_snd.at[k, d - 1], w_rcv.at[d - 1, 0, w_index(k, s)],
                      (o, lax.rem(i + 2 * d, n_in)))

    def w_relay(k, d, s):
        here = slot(k, far(d), s)
        return remote(here, here, w_relay_snd.at[k, d - 1], w_rcv.at[d - 1, 1, w_index(k, s)], core_peer)

    def w_pair(k, s):
        return remote(w_src(k, s), slot(k, i, s), w_pair_snd.at[k], w_pair_rcv.at[k], core_peer)

    def w_local(k, s):
        return pltpu.make_async_copy(w_src(k, s), slot(k, i, s), w_loc.at[k])

    def near_ready(k):
        mine, other = shard(k, i), shard(k, partner)
        pltpu.make_async_copy(mine, mine, w_loc.at[k]).wait()
        remote(other, other, w_pair_snd.at[k], w_pair_rcv.at[k], core_peer).wait_recv()

    def far_ready(k, s):
        for d in steps:
            here = slot(k, lax.rem(partner + n_in - 2 * d, n_in), s)
            remote(here, here, w_relay_snd.at[k, d - 1], w_rcv.at[d - 1, 1, w_index(k, s)], core_peer).wait_recv()

    def relay_weight(k, s):
        for d in steps:
            here = slot(k, far(d), s)
            remote(here, here, w_relay_snd.at[k, d - 1], w_rcv.at[d - 1, 0, w_index(k, s)], core_peer).wait_recv()
            w_relay(k, d, s).start()

    def weight_ready(k):
        near_ready(k)
        for s in range(w_parts(k)):
            far_ready(k, s)

    def drain_weights(k):
        mine = shard(k, i)
        remote(mine, mine, w_pair_snd.at[k], w_pair_rcv.at[k], core_peer).wait_send()
        for d in steps:
            remote(mine, mine, w_snd.at[k, d - 1], w_pair_rcv.at[k], core_peer).wait_send()
            remote(mine, mine, w_relay_snd.at[k, d - 1], w_pair_rcv.at[k], core_peer).wait_send()

    def send_far(k):
        for s in range(w_parts(k)):
            for d in steps:
                w_far(k, d, s).start()

    send_far(0)
    send_far(1)
    for k in range(3):
        for s in range(w_parts(k)):
            w_pair(k, s).start()
            w_local(k, s).start()

    loads[0].wait()
    lane = lax.broadcasted_iota(jnp.int32, (rows, block), 1)
    key_pos = jnp.zeros((rows, block), jnp.int32)
    for p in range(pieces):
        key_pos = jnp.where(lane // span == p, order_ref[p] * span + lane % span, key_pos)
    row = lax.broadcasted_iota(jnp.int32, (rows, block), 0)
    query_pos = jnp.zeros((rows, block), jnp.int32)
    for p in range(rows // span):
        query_pos = jnp.where(
            row // span == p, order_ref[i * (rows // span) + p] * span + row % span, query_pos)
    own_visible = key_pos <= query_pos
    before_visible = (jnp.zeros((rows, block), jnp.int32) + o) > 0

    @pl.when(o == 0)
    def _():
        kv_all[block:, :] = jnp.zeros((block, 2 * head), BF16)

    for zz in (0, last_z):
        @pl.when(z != zz)
        def _():
            x_in[:, zz, keep:, :] = jnp.zeros((parts_n, rows - keep, 2 * cw), BF16)

    for d in steps:
        kv_arrived(0, lax.rem(i + n_in - 2 * d, n_in))
        kv_relay(0, d).start()

    @pl.when(o > 0)
    def _():
        for d in range(chips):
            kv_arrived(1, lax.rem(i + n_in - 2 * d, n_in))
            kv_relay(1, d).start()

    kv_copy.wait()
    for d in range(chips):
        kv_arrived(0, lax.rem(partner + 2 * d, n_in))

    @pl.when(o > 0)
    def _():
        for d in range(chips):
            kv_arrived(1, lax.rem(partner + 2 * d, n_in))

    loads[1].wait()
    parts = []
    nt = (((1,), (1,)), ((), ()))
    for h in range(heads):
        query = query_ref[:, h * head:(h + 1) * head]
        own_score = lax.dot_general(
            query, kv_all[:block, :head], nt, preferred_element_type=F32) * head ** (-0.5)
        before_score = lax.dot_general(
            query, kv_all[block:, :head], nt, preferred_element_type=F32) * head ** (-0.5)
        own_score = jnp.where(own_visible, own_score, -1e30)
        before_score = jnp.where(before_visible, before_score, -1e30)
        top = jnp.maximum(
            jnp.max(own_score, axis=1, keepdims=True), jnp.max(before_score, axis=1, keepdims=True))
        own_w = jnp.where(own_visible, jnp.exp(own_score - top), 0.0)
        before_w = jnp.where(before_visible, jnp.exp(before_score - top), 0.0)
        total = jnp.sum(own_w, axis=1, keepdims=True) + jnp.sum(before_w, axis=1, keepdims=True)
        mixed = jnp.dot(own_w.astype(BF16), kv_all[:block, head:], preferred_element_type=F32)
        mixed += jnp.dot(before_w.astype(BF16), kv_all[block:, head:], preferred_element_type=F32)
        parts.append((mixed / total).astype(BF16))
    att_own[...] = jnp.concatenate(parts, axis=1)
    for link in range(3):
        send_link(link, lambda link=link: first_attended(link).start())

    for load in loads[2:]:
        load.wait()

    def normed_of(resid, attended):
        after_attn = (
            resid.astype(F32) + jnp.dot(attended, proj_ref[...], preferred_element_type=F32)
        ).astype(BF16)
        wide = after_attn.astype(F32)
        normed = wide * lax.rsqrt(jnp.mean(wide * wide, axis=1, keepdims=True) + EPS) * gain_ref[...]
        return after_attn, normed.astype(BF16)

    after_attn, normed = normed_of(resid_ref[...], att_own[...])
    after[...] = after_attn
    tok_rows(z, x)[...] = normed
    for link in range(3):
        send_link(link, lambda link=link: first_normed(link).start())

    def part_rows(zz, xx, part):
        return tok_rows(zz, xx, part * early, rows - early if part else early)

    def tok_z(way, h, part):
        step = 1 - 2 * way
        here = part_rows(z - step * h, x, part)
        return remote(here, here, z_snd.at[way, h - 1], z_rcv.at[part, way, h - 1], z_device(z + step))

    def tok_z_arrived(way, h, part):
        here = part_rows(z - (1 - 2 * way) * (h + 1), x, part)
        remote(here, here, z_snd.at[way, h - 1], z_rcv.at[part, way, h - 1], x_peer).wait_recv()

    def tok_x(zz, xx, part):
        here = part_rows(zz, xx, part)
        return remote(here, here, x_snd.at[zz], x_rcv.at[zz], x_peer)

    def tok_x_end(zz, xx):
        here = tok_rows(zz, xx, 0, keep_t)
        return remote(here, here, x_snd.at[zz], x_rcv.at[zz], x_peer)

    def send_x(zz, part):
        @pl.when(middle(zz))
        def _():
            tok_x(zz, x, part).start()

        if part == 0:
            @pl.when(jnp.logical_not(middle(zz)))
            def _():
                tok_x_end(zz, x).start()

    def tok_half(way, to):
        here = tok_rows(last_z if way else 0, 1 - x, keep_t, rows - keep_t)
        return remote(here, here, g_snd.at[way], g_rcv.at[way], to)

    def from_origin(way):
        return last_z - z if way else z

    near_way = jnp.where(2 * z < nz, 0, 1)

    def absorb(link, zz, xx):
        first_resid(link, x_peer).wait_recv()
        first_attended(link, x_peer).wait_recv()
        tok_rows(zz, xx, 0, early)[...] = normed_of(res_in[link], att_in[link])[1]

    def hop(h, part, way):
        step = 1 - 2 * way
        source = z - step * (h + 1)

        @pl.when(inside(source))
        def _():
            if h > 0:
                tok_z_arrived(way, h, part)
            elif part == 0:
                absorb(way, source, x)
            else:
                first_normed(way, (source, x), x_peer).wait_recv()
            if h < nz - 2:
                @pl.when(inside(z + step))
                def _():
                    tok_z(way, h + 1, part).start()

            send_x(source, part)

    def pair_of(j):
        return z + ((j + 1) // 2) * (1 - 2 * (j % 2))

    def both_rows(zz):
        return pl.ds(pl.multiple_of(zz * 2 * rows, 2 * rows), 2 * rows)

    def make_gate(zz):
        here = both_rows(zz)
        gates[here, :] = jnp.dot(tok[here, :], wg[...], preferred_element_type=F32)

    def other_x_arrived(zz):
        @pl.when(middle(zz))
        def _():
            whole = tok_rows(zz, 1 - x)
            remote(whole, whole, x_snd.at[zz], x_rcv.at[zz], x_peer).wait_recv()

        @pl.when(jnp.logical_not(middle(zz)))
        def _():
            tok_x_end(zz, 1 - x).wait_recv()

    def gate_step(j, carry):
        zz = pair_of(j)

        @pl.when(inside(zz))
        def _():
            @pl.when(j > 0)
            def _():
                other_x_arrived(zz)

            make_gate(zz)

        return carry

    first_zz = z + (nz - 2) * (1 - 2 * near_way)

    def upward_over(zz, shards):
        total = None
        for q in shards:
            here = pl.ds(pl.multiple_of(q * depth, depth), depth)
            part = jnp.dot(tok[both_rows(zz), here], wu[here, :], preferred_element_type=F32)
            total = part if total is None else total + part
        return total

    relays = [(k, s) for k in range(2) for s in range(pieces_w[k])]

    def relay_to(n):
        while relays and n > 0:
            k, s = relays.pop(0)
            relay_weight(k, s)
            n -= 1

    def halves(h):
        for way in range(2):
            @pl.when(from_origin(way) == h + 1)
            def _():
                tok_half(way, x_peer).wait_recv()

                @pl.when(inside(z + 1 - 2 * way))
                def _():
                    tok_half(way, z_device(z + 1 - 2 * way)).start()

    for h in range(nz - 1):
        for part in range(2):
            hop(h, part, 1 - near_way)
            hop(h, part, near_way)
        if h == 0:
            absorb(2, z, 1 - x)
            first_normed(2, (z, 1 - x), x_peer).wait_recv()
            for way in range(2):
                @pl.when(from_origin(way) == 0)
                def _():
                    tok_half(way, z_device(z + 1 - 2 * way)).start()
            relay_to((pieces_w[0] + 1) // 2)
        elif h == 1:
            relay_to(pieces_w[0] // 2)
            weight_ready(0)
            lax.fori_loop(0, 3, gate_step, 0)
            relay_to((pieces_w[1] + 3) // 4)
        else:
            relay_to((pieces_w[1] + 7) // 8)
            lax.fori_loop(2 * h - 1, 2 * h + 1, gate_step, 0)
        if h == nz - 2:
            relay_to(len(relays) - 1)
            send_far(2)
            near_ready(1)

            @pl.when(inside(first_zz))
            def _():
                upper[...] = upward_over(first_zz, [i, partner])

        halves(h)
    relay_to(len(relays))

    def columns_of(chip):
        return lax.rem(i // 2 + chips - chip, chips)

    def end_way(zz):
        return jnp.where(zz == last_z, 0, 1)

    def sum_x(p, zz, part):
        there = pl.ds(part * keep, rows - keep if part else keep)
        return remote(x_out.at[p, zz, there], x_in.at[p, zz, there], rx_snd.at[part],
                      rx_rcv.at[p, zz], x_peer)

    def sum_x_whole(p, zz):
        return remote(x_out.at[p, zz], x_in.at[p, zz], rx_snd.at[0], rx_rcv.at[p, zz], x_peer)

    def sum_z(p, way, zz, here=False):
        step = jnp.where(inside(z + 1 - 2 * way), 1 - 2 * way, 0)
        off = 0 if here else step
        return remote(z_out.at[p, zz], z_in.at[p, way, zz], rz_snd,
                      rz_rcv.at[p, jnp.where(jnp.logical_and(way == 1, zz == z + off), nz, zz)],
                      z_device(z + step))

    def sum_half(p, way, to):
        return remote(h_out.at[p, way], h_in.at[p, way], rh_snd.at[way], rh_rcv.at[p, way], to)

    def next_z(way):
        return z_device(jnp.clip(z + 1 - 2 * way, 0, last_z))

    def down(chip, cs, zz):
        def half(xx):
            return hidden[pl.ds(pl.multiple_of((zz * 2 + xx) * rows, rows), rows), :]

        both = jnp.concatenate([half(1 - x), half(x)], axis=0)
        for c in cs:
            p = chip * cuts + c
            for q in range(2):
                part = jnp.dot(both, wd[2 * columns_of(chip) + q, c], preferred_element_type=F32)
                here = slice(q * cw, (q + 1) * cw)
                x_out[p, zz, :, here] = part[:rows].astype(BF16)
                own_part[p, zz, :, here] = part[rows:]
                h_own[p, jnp.where(middle(zz), 2, end_way(zz)), :, here] = part[keep:rows]

    def send_sums(p, zz):
        sum_x(p, zz, 0).start()

        @pl.when(middle(zz))
        def _():
            sum_x(p, zz, 1).start()

    def send_halves(ps, zz):
        for way in range(2):
            @pl.when(jnp.logical_and(from_origin(way) == 0, zz == (0 if way else last_z)))
            def _():
                for p in ps:
                    h_out[p, way] = h_own[p, way].astype(BF16)
                    sum_half(p, way, next_z(way)).start()

    turns = 2 * nz - 1

    def owner(j):
        way = j % 2
        return way, z + (nz - 1 - j // 2) * (1 - 2 * way)

    def finish_half(p, way):
        sum_half(p, way, x_peer).wait_recv()
        h_out[p, way] = (h_own[p, way] + h_in[p, way].astype(F32)).astype(BF16)
        sum_half(p, way, next_z(way)).start()

    def relay_half(p, way):
        @pl.when(middle(z))
        def _():
            finish_half(p, way)

    def own_half(p):
        for way in range(2):
            @pl.when(z == (0 if way else last_z))
            def _():
                sum_half(p, way, x_peer).wait_recv()
                x_out[p, z, keep:, :] = (h_own[p, way] + h_in[p, way].astype(F32)).astype(BF16)
                sum_x(p, z, 1).start()

    def finish(p, way, zz):
        more = inside(z - (1 - 2 * way))

        @pl.when(inside(zz))
        def _():
            @pl.when(middle(zz))
            def _():
                sum_x_whole(p, zz).wait_recv()

            @pl.when(jnp.logical_not(middle(zz)))
            def _():
                sum_x(p, zz, 0).wait_recv()

            @pl.when(more)
            def _():
                sum_z(p, way, zz, True).wait_recv()
                z_out[p, zz] = (
                    own_part[p, zz] + x_in[p, zz].astype(F32) + z_in[p, way, zz].astype(F32)
                ).astype(BF16)

            @pl.when(jnp.logical_not(more))
            def _():
                z_out[p, zz] = (own_part[p, zz] + x_in[p, zz].astype(F32)).astype(BF16)

            sum_z(p, way, zz).start()

    near_ready(2)
    def make_hidden(zz, upward):
        here = both_rows(zz)
        gate = gates[here, :]
        hidden[here, :] = (gate / (1.0 + jnp.exp(-gate)) * upward).astype(BF16)

    def first_sums(zz):
        for p in range(cuts):
            down(0, (p,), zz)
            send_sums(p, zz)
            send_halves((p,), zz)

    @pl.when(inside(first_zz))
    def _():
        upper[...] += upward_over(first_zz, [lax.rem(i + 2 * d, n_in) for d in steps])

    @pl.when(jnp.logical_and(jnp.logical_not(middle(z)), core == 1))
    def _():
        other_x_arrived(last_z - z)
        make_gate(last_z - z)

    for s in range(pieces_w[1]):
        far_ready(1, s)

    @pl.when(inside(first_zz))
    def _():
        for xx in (1 - x, x):
            here = pl.ds(pl.multiple_of((first_zz * 2 + xx) * rows, rows), rows)
            upward = upper[pl.ds(pl.multiple_of(xx * rows, rows), rows), :]
            for d in steps:
                q = lax.rem(partner + 2 * d, n_in)
                there = pl.ds(pl.multiple_of(q * depth, depth), depth)
                upward += jnp.dot(tok[here, there], wu[there, :], preferred_element_type=F32)
            gate = gates[here, :]
            hidden[here, :] = (gate / (1.0 + jnp.exp(-gate)) * upward).astype(BF16)
            for q in range(2):
                part = jnp.dot(hidden[here, :], wd[2 * columns_of(0) + q, 0], preferred_element_type=F32)
                cols = slice(q * cw, (q + 1) * cw)
                if xx is x:
                    own_part[0, first_zz, :, cols] = part
                else:
                    x_out[0, first_zz, :, cols] = part.astype(BF16)
                    h_own[0, jnp.where(middle(first_zz), 2, end_way(first_zz)), :, cols] = part[keep:]
            if xx is not x:
                send_sums(0, first_zz)
        for p in range(1, cuts):
            down(0, (p,), first_zz)
            send_sums(p, first_zz)

    def hidden_step(j, carry):
        _, zz = owner(j)

        @pl.when(jnp.logical_and(j == 3, jnp.logical_not(middle(z))))
        def _():
            finish(0, near_way, first_zz)

        @pl.when(jnp.logical_and(j == turns - 1, jnp.logical_not(middle(z))))
        def _():
            for p in range(1, cuts):
                finish(p, near_way, first_zz)

        @pl.when(jnp.logical_and(inside(zz), zz != first_zz))
        def _():
            @pl.when(jnp.logical_and(j < 2, core == 0))
            def _():
                other_x_arrived(zz)
                make_gate(zz)

            make_hidden(zz, jnp.dot(tok[both_rows(zz), :], wu[...], preferred_element_type=F32))

            @pl.when(j < turns - 1)
            def _():
                first_sums(zz)

            @pl.when(j == turns - 1)
            def _():
                down(0, range(cuts), zz)

        return carry

    lax.fori_loop(0, turns, hidden_step, 0)

    near_end = jnp.where(near_way == 0, last_z, 0)

    def finish_end(p):
        relay_half(p, near_way)
        finish(p, near_way, near_end)

    def finish_way(p, way, skip):
        def step(n, carry):
            zz = z + (nz - 1 - n) * (1 - 2 * way)

            @pl.when(zz != skip)
            def _():
                finish(p, way, zz)

            return carry

        lax.fori_loop(0, nz - 1, step, 0)

    def finish_outer(ps, start):
        def step(n, carry):
            for p in ps:
                finish(p, near_way, z + (nz - 1 - n) * (1 - 2 * near_way))
            return carry

        lax.fori_loop(start, nz - 1, step, 0)

    def far_down(s, hold=False):
        far_ready(2, s)

        def step(t, carry):
            chip = 1 + t // turns
            j = t % turns
            _, zz = owner(j)

            @pl.when(inside(zz))
            def _():
                down(chip, (s,), zz)

                @pl.when(j < (turns - 3 if hold else turns - 1))
                def _():
                    send_sums(chip * cuts + s, zz)
                    send_halves((chip * cuts + s,), zz)

            return carry

        lax.fori_loop(0, (chips - 1) * turns, step, 0)

    rest = [c * cuts + s for s in range(cuts) for c in range(1, chips)]

    def own_sums(ps):
        for p in ps:
            sum_x(p, z, 0).start()

            @pl.when(middle(z))
            def _():
                sum_x(p, z, 1).start()

    def drain_first():
        for d in steps:
            kv_send(0, d).wait_send()
        for d in range(chips):
            kv_relay(0, d).wait_send()

        @pl.when(o < n_out - 1)
        def _():
            for d in range(chips):
                kv_send(1, d).wait_send()

        @pl.when(o > 0)
        def _():
            for d in range(chips):
                kv_relay(1, d).wait_send()

        for link in range(3):
            def sent(link=link):
                first_attended(link).wait_send()
                whole = tok_rows(z, x)
                remote(whole, whole, r_snd.at[link], r_rcv.at[link], target(link)).wait_send()

            send_link(link, sent)
        for way in range(2):
            step = 1 - 2 * way

            @pl.when(inside(z + step))
            def _():
                tok_half(way, x_peer).wait_send()
                for h in range(1, nz - 1):
                    @pl.when(inside(z - step * h))
                    def _():
                        whole = tok_rows(z, x)
                        remote(whole, whole, z_snd.at[way, h - 1], z_rcv.at[0, way, h - 1], x_peer).wait_send()
        for zz in range(nz):
            @pl.when(z != zz)
            def _():
                if zz == 0 or zz == last_z:
                    tok_x_end(zz, x).wait_send()
                else:
                    whole = tok_rows(zz, x)
                    remote(whole, whole, x_snd.at[zz], x_rcv.at[zz], x_peer).wait_send()

    def drain_sums():
        for way in range(2):
            @pl.when(inside(z + 1 - 2 * way))
            def _():
                halves_out = h_out.at[:, way]
                remote(halves_out, halves_out, rh_snd.at[way], rh_rcv.at[0, way], x_peer).wait_send()
        first = x_out.at[:, :, pl.ds(0, keep)]
        remote(first, first, rx_snd.at[0], rx_rcv.at[0, 0], x_peer).wait_send()

        def second(n):
            there = x_out.at[:, pl.ds(0, n), pl.ds(keep, rows - keep)]
            remote(there, there, rx_snd.at[1], rx_rcv.at[0, 0], x_peer).wait_send()

        pl.when(middle(z))(lambda: second(nz - 2))
        pl.when(jnp.logical_not(middle(z)))(lambda: second(nz - 1))
        others = z_out.at[:, pl.ds(0, nz - 1)]
        remote(others, others, rz_snd, rz_rcv.at[0, 0], x_peer).wait_send()

    @pl.when(middle(z))
    def _():
        own_sums(range(cuts))
        for p in range(cuts):
            relay_half(p, near_way)
        relay_weight(2, 0)
        far_down(0)
        for p in range(cuts):
            relay_half(p, 1 - near_way)
        for p in range(cuts):
            finish_way(p, near_way, near_end)
        for p in range(cuts):
            finish(p, near_way, near_end)
        for s in range(1, cuts):
            relay_weight(2, s)
            far_down(s)
        own_sums(rest)
        for p in range(cuts):
            finish_way(p, 1 - near_way, -1)
        for p in rest:
            finish_end(p)
        for p in rest:
            relay_half(p, 1 - near_way)
        for p in rest:
            finish_way(p, 1 - near_way, -1)
            finish_way(p, near_way, near_end)

    @pl.when(jnp.logical_not(middle(z)))
    def _():
        finish(0, near_way, near_end)
        relay_weight(2, 0)
        for p in range(1, cuts):
            finish(p, near_way, near_end)
        far_down(0, True)
        finish_outer((0,), 2)
        for s in range(1, cuts):
            relay_weight(2, s)
            for c in range(1, chips):
                finish_end(c * cuts + s - 1)
            far_down(s, True)
        for p in rest:
            send_sums(p, z + 1 - 2 * near_way)
        own_sums(range(parts_n))
        for c in range(1, chips):
            finish_end(c * cuts + cuts - 1)
        if cuts > 1:
            finish_outer(range(1, cuts), 2)
        finish_outer(rest, 1)

    drain_first()
    for k in range(3):
        drain_weights(k)
    for p in range(parts_n):
        own_half(p)
    for p in range(parts_n):
        for way in range(2):
            @pl.when(inside(z - (1 - 2 * way)))
            def _():
                sum_z(p, way, z, True).wait_recv()
                own_part[p, z] = own_part[p, z] + z_in[p, way, z].astype(F32)
        sum_x_whole(p, z).wait_recv()
        for q in range(2):
            source = 2 * columns_of(p // cuts) + q
            here = pl.ds(pl.multiple_of(source * width + (p % cuts) * cw, cw), cw)
            cols = slice(q * cw, (q + 1) * cw)
            out_ref[:, here] = (
                after[:, here].astype(F32)
                + (own_part[p, z, :, cols] + x_in[p, z, :, cols].astype(F32))).astype(BF16)

    drain_sums()


def per_device(n_out, n_in, resid, queries, keyvals, piece_order, out_proj, mlp_gain, w_gate, w_up, w_down):
    rows, model = resid.shape
    units, width = w_down.shape
    nz, chips = n_out // 2, n_in // 2
    cuts = max(1, width // 256)
    pieces_w = (max(1, 8 // n_in), max(1, 32 // n_in), cuts)
    cw = width // cuts
    parts_n = chips * cuts
    early = rows * 80 // 128
    dma = pltpu.SemaphoreType.DMA
    vmem = pl.BlockSpec(memory_space=pltpu.VMEM)
    hbm = pl.BlockSpec(memory_space=pl.ANY)
    keep = rows * KEEP // 128
    half = rows - keep
    return pl.pallas_call(
        functools.partial(layer_kernel, n_out, n_in, cuts, pieces_w, early, keep),
        out_shape=pltpu.VMEM(resid.shape, BF16),
        in_specs=[hbm] * 9,
        out_specs=vmem,
        scratch_shapes=[
            pltpu.SMEM(piece_order.shape, jnp.int32),
            pltpu.VMEM(resid.shape, BF16),
            pltpu.VMEM(queries.shape, BF16),
            pltpu.VMEM(out_proj.shape, BF16),
            pltpu.VMEM((1, model), F32),
            dma((5,)),
            pltpu.VMEM((2 * n_in * rows, keyvals.shape[1]), BF16),
            pltpu.VMEM((model, units), BF16),
            pltpu.VMEM((model, units), BF16),
            pltpu.VMEM((n_in, cuts, units, cw), BF16),
            pltpu.VMEM((n_out * rows, model), BF16),
            pltpu.VMEM((rows, model), BF16),
            pltpu.VMEM(queries.shape, BF16),
            pltpu.VMEM((3, early, model), BF16),
            pltpu.VMEM((3, early, queries.shape[1]), BF16),
            pltpu.VMEM((n_out * rows, units), F32),
            pltpu.VMEM((2 * rows, units), F32),
            pltpu.VMEM((n_out * rows, units), BF16),
            pltpu.VMEM((parts_n, nz, rows, 2 * cw), BF16),
            pltpu.VMEM((parts_n, nz, rows, 2 * cw), BF16),
            pltpu.VMEM((parts_n, nz, rows, 2 * cw), F32),
            pltpu.VMEM((parts_n, nz, rows, 2 * cw), BF16),
            pltpu.VMEM((parts_n, 2, nz, rows, 2 * cw), BF16),
            pltpu.VMEM((parts_n, 3, half, 2 * cw), F32),
            pltpu.VMEM((parts_n, 2, half, 2 * cw), BF16),
            pltpu.VMEM((parts_n, 2, half, 2 * cw), BF16),
            dma(()), dma((2, chips)), dma((2, chips)), dma((2, n_in)),
            dma((3,)), dma((3,)), dma((3,)), dma((3, chips - 1)), dma((3, chips - 1)),
            dma((chips - 1, 2, sum(pieces_w))),
            dma((3,)), dma((3,)), dma((3,)), dma((3,)), dma((3,)),
            dma((2, nz - 2)), dma((2, 2, nz - 2)), dma((2,)), dma((2,)), dma((nz,)), dma((nz,)),
            dma((2,)), dma((parts_n, nz)), dma(()), dma((parts_n, nz + 1)),
            dma((2,)), dma((parts_n, 2)),
        ],
        compiler_params=pltpu.CompilerParams(
            collective_id=0, has_side_effects=True, vmem_limit_bytes=63000 * 1024
        ),
        name="layer",
    )(piece_order, resid, queries, keyvals, out_proj, mlp_gain.reshape(1, -1), w_gate, w_up, w_down)


def solution(mesh):
    placed = (
        P(("outer", "inner"), None),
        P(("outer", "inner"), None),
        P(("outer", "inner"), None),
        P(),
        P(),
        P(),
        P("inner", "outer"),
        P("inner", "outer"),
        P("outer", "inner"),
    )
    return jax.shard_map(
        functools.partial(per_device, mesh.shape["outer"], mesh.shape["inner"]),
        mesh=mesh,
        in_specs=placed,
        out_specs=P(("outer", "inner"), None),
        check_vma=False,
    )
```
